128 devices in a mesh: sx: 16 (over y, z), sy: 8 (over x, core).
Axes of the slice: x: 4, y: 4, z: 4, core: 2. Of those that a mesh axis runs over, the one named last changes fastest.
Arguments:
- rhs: float32 [12288, 16384], P('sx', 'sy')
- sigma: float32 [12288, 16384], P('sx', 'sy'), may hold values from 0.05 to 2
- tile_list: int32 [262144], P(('sx', 'sy')), may hold values from 0 to 12287, as said below
- tile_owner: int32 [262144, 1], P(('sx', 'sy')), may hold values from 0 to 127, as said below
- schur_blocks: bfloat16 [128, 128, 128], P(('sx', 'sy')), as said below
Outputs:
- corrected: float32 [12288, 16384], P('sx', 'sy')
- iface_residual: float32 [262144, 128], P(('sx', 'sy'))
- iface_direction: float32 [262144, 128], P(('sx', 'sy'))
The draws below stay inside these ranges and needn't reach their ends.
Inputs may be any that keep to these rules, and one draw needn't show every extreme that they name: `tile_owner`: within the 2048 tiles of one subdomain no owner appears more than 32 times. `tile_list`: every listed run touches its block's rim: it lies in the block's first or last row, or is the first or last run of its row. Runs may repeat. `schur_blocks`: each block is symmetric.
All inputs are finite; a program needn't handle non-finite values.
Results may differ from the reference program's by a relative error of at most 0.012.
Values may be sent and summed in bfloat16 or wider, within the bound.
No kernel may reach another device: no remote copies, remote signals or barrier semaphores. Data moves between devices by JAX's collectives and lax.ppermute only.
A program may use at most 128 MiB of HBM per device.

```python
import math
import jax
import jax.numpy as jnp
from jax import lax

CR = 768
CC = 2048
TW = 128
TPD = 2048
NROW = 12288
NCOL = 16384
TILES = 262144
N_SX = 16
N_SY = 8


def draw_rhs(key, part):
    key_two = jax.random.fold_in(jax.random.fold_in(key, 11), 1)
    rowpos = jnp.arange(NROW, dtype=jnp.float32) / NROW
    colpos = jnp.arange(NCOL, dtype=jnp.float32) / NCOL
    scale = (1.0 + rowpos[:, None]) * (1.0 + colpos[None, :])
    return jax.random.normal(key_two, (NROW, NCOL), jnp.float32) * scale


def draw_tile_list(key, part):
    runs = CC // TW
    count = N_SX * N_SY
    rim_total = 2 * runs + 2 * (CR - 2)
    pick = jax.random.randint(jax.random.fold_in(key, 37), (count, TPD), 0, rim_total, jnp.int32)
    bottom = (CR - 1) * runs + (pick - runs)
    side_pos = pick - 2 * runs
    row_side = 1 + side_pos // 2
    edge = row_side * runs + side_pos % 2 * (runs - 1)
    chosen = jnp.where(pick < runs, pick, jnp.where(pick < 2 * runs, bottom, edge))
    chosen = chosen.at[:, 0].set(0).at[:, 1].set(CR * runs - 1)
    return chosen.astype(jnp.int32).reshape(count * TPD)


def owner_order(key):
    count = N_SX * N_SY
    return jax.random.permutation(jax.random.fold_in(key, 71), count).astype(jnp.int32)


def draw_tile_owner(key, part):
    count = N_SX * N_SY
    half_count = count // 2
    capacity = 2 * TPD // count
    order = owner_order(key)
    base_key = jax.random.fold_in(key, 73)
    denom = 2 * (N_SX - 1) * (N_SY - 1)

    def one_device(device):
        row_index = device // N_SY
        col_index = device % N_SY
        start = 1 + (row_index * (N_SY - 1) + col_index * (N_SX - 1)) * (half_count - 1) // denom
        sub_key = jax.random.fold_in(base_key, device)
        key_one, key_two = jax.random.split(sub_key)
        ranks = start + jnp.arange(half_count * capacity, dtype=jnp.int32) // capacity
        picked = jax.random.permutation(key_one, ranks)[:TPD - capacity]
        pool = jnp.concatenate([jnp.zeros((capacity,), jnp.int32), picked.astype(jnp.int32)])
        pool = jax.random.permutation(key_two, pool)
        return order[pool]
    owners = jax.vmap(one_device)(jnp.arange(count, dtype=jnp.int32))
    return owners.astype(jnp.int32).reshape(count * TPD, 1)


def draw_schur_blocks(key, part):
    key_one, key_two = jax.random.split(jax.random.fold_in(key, 23))
    count = N_SX * N_SY
    order = owner_order(key)
    rank = jnp.zeros((count,), jnp.int32).at[order].set(jnp.arange(count, dtype=jnp.int32))
    level = 2.0 * jnp.power(4.0, rank.astype(jnp.float32) / (count - 1))
    raw = jax.random.uniform(key_one, (count, TW, TW), jnp.float32, -0.25, 0.25)
    diag = jax.random.uniform(key_two, (count, TW), jnp.float32, 3.5, 5.0)
    sym = 0.5 * (raw + jnp.swapaxes(raw, 1, 2))
    eye = jnp.eye(TW, dtype=jnp.float32)
    full = sym * (1.0 - eye)[None] + eye[None] * diag[:, :, None]
    full = full * (0.25 * level)[:, None, None]
    return full.astype(jnp.bfloat16)


def level_of(key, shape, pieces, low, high):
    factor_of = 1.0
    for position, blocks in pieces:
        heights = jax.random.uniform(jax.random.fold_in(jax.random.fold_in(key, 6), position), (blocks,), jnp.float32, low / len(pieces), high / len(pieces))
        factor_of = factor_of * jnp.repeat(jnp.exp(heights), shape[position] // blocks).reshape((-1,) + (1,) * (len(shape) - 1 - position))
    return factor_of


def setup_inputs(seed: int = 0) -> dict:
    arg_keys = jax.random.split(jax.random.key(seed), 6)
    return {
        "rhs": draw_rhs(jax.random.fold_in(arg_keys[5], 71), 0),
        "sigma": jnp.clip(jnp.exp(math.log(2.0) - 3.6888794 * jax.random.uniform(arg_keys[1], (NROW, NCOL), jnp.float32) ** level_of(arg_keys[1], (NROW, NCOL), ((0, 16), (1, 8)), -0.2, 0.2)), 0.05, 2.0),
        "tile_list": draw_tile_list(jax.random.fold_in(arg_keys[5], 71), 0),
        "tile_owner": draw_tile_owner(jax.random.fold_in(arg_keys[5], 71), 0),
        "schur_blocks": draw_schur_blocks(jax.random.fold_in(arg_keys[5], 71), 0),
    }


def apply_op(field, sigma):
    padded = jnp.pad(field, 1)
    beside = padded[2:, 1:-1] + padded[:-2, 1:-1] + padded[1:-1, 2:] + padded[1:-1, :-2]
    return (4.0 + sigma) * field - beside


def to_blocks(field):
    return field.reshape(N_SX, CR, N_SY, CC).transpose(0, 2, 1, 3).reshape(N_SX * N_SY, CR * CC // TW, TW)


def reference(rhs, sigma, tile_list, tile_owner, schur_blocks):
    dinv = 1.0 / (4.0 + sigma)
    first = 0.6111111 * dinv * rhs
    second = first + 2.75 * dinv * (rhs - apply_op(first, sigma))
    field_res = rhs - apply_op(second, sigma)
    lists = tile_list.reshape(N_SX * N_SY, TPD)
    owners = tile_owner.reshape(N_SX * N_SY, TPD)
    r_tiles = jax.vmap(lambda blk, idx: blk[idx])(to_blocks(field_res), lists)

    def one_source(pair):
        tiles, own = pair
        mats = schur_blocks[own].astype(jnp.float32)
        half = lax.optimization_barrier(tiles.astype(jnp.bfloat16)).astype(jnp.float32)
        prod = jnp.einsum('tc,tcn->tn', half, mats)
        return lax.optimization_barrier(prod.astype(jnp.bfloat16)).astype(jnp.float32)

    q_tiles = lax.map(one_source, (r_tiles, owners))
    rr_old = jnp.sum(r_tiles * r_tiles)
    pq_sum = jnp.sum(r_tiles * q_tiles)
    alpha = rr_old / pq_sum
    iface_residual = r_tiles - alpha * q_tiles
    rr_new = jnp.sum(iface_residual * iface_residual)
    iface_direction = iface_residual + (rr_new / rr_old) * r_tiles
    added = jax.vmap(lambda blk, idx, val: blk.at[idx].add(val))(to_blocks(second), lists, alpha * r_tiles)
    corrected = added.reshape(N_SX, N_SY, CR, CC).transpose(0, 2, 1, 3).reshape(NROW, NCOL)
    return corrected, iface_residual.reshape(TILES, TW), iface_direction.reshape(TILES, TW)
```

```python
import jax
import jax.numpy as jnp
from jax import lax
from jax.experimental import pallas as pl
from jax.experimental.pallas import tpu as pltpu
from jax.sharding import Mesh, PartitionSpec as P

F32 = jnp.float32
BF16 = jnp.bfloat16
R, C, W = 768, 2048, 128
T = 2048
CAP = 32
NG = 64
RIM = 2 * R + 32
PR = 72
OFF = 16
FR = R + 2 * OFF
ROWS = ("y", "z")
COLS = ("x", "c")
ALL = ("y", "z", "x", "c")
CHIPS = ("y", "z", "x")
VM = pl.BlockSpec(memory_space=pltpu.VMEM)
SM = pl.BlockSpec(memory_space=pltpu.SMEM)
ANY = pl.BlockSpec(memory_space=pl.ANY)
PARAMS = pltpu.CompilerParams(vmem_limit_bytes=56 << 20)


def sds(shape, dtype=F32):
    return jax.ShapeDtypeStruct(shape, dtype)


def pack_kernel(s_ref, out_ref):
    s = s_ref[0].astype(F32)
    top, bot = s[:64], s[64:]
    i = lax.broadcasted_iota(jnp.int32, (64, W), 0)
    j = lax.broadcasted_iota(jnp.int32, (64, W), 1)
    d = j - i
    body = jnp.where((d >= 0) & (d < 64), top, bot)
    cross = jnp.where(d == 64, top, 0.0)
    half = jnp.sum(cross, axis=0, keepdims=True)
    row = half + pltpu.roll(half, 64, axis=1)
    full = jnp.concatenate([body, jnp.broadcast_to(row, (8, W))], axis=0).astype(BF16)
    for k in range(NG):
        out_ref[k] = full


def pack(blocks):
    return pl.pallas_call(pack_kernel, out_shape=sds((NG, PR, W), BF16), in_specs=[VM], out_specs=VM, compiler_params=PARAMS, name="pack")(blocks)


def dense_kernel(x_ref, s_ref, xp_ref, sp_ref, xn_ref, sn_ref, out_ref, f_ref):
    t = 4.0 + s_ref[...]
    dinv = 1.0 / t
    x = x_ref[...]
    f = 0.6111111 * dinv * x
    f_ref[8:72] = f
    f_ref[0:8] = 0.6111111 * (1.0 / (4.0 + sp_ref[...])) * xp_ref[...]
    f_ref[72:80] = 0.6111111 * (1.0 / (4.0 + sn_ref[...])) * xn_ref[...]
    beside = f_ref[9:73] + f_ref[7:71] + pltpu.roll(f, C - 1, axis=1) + pltpu.roll(f, 1, axis=1)
    out_ref[...] = f + 2.75 * dinv * (x - (t * f - beside))


def dense(rhs, sigma):
    main = pl.BlockSpec((64, C), lambda i: (i, 0))
    prev = pl.BlockSpec((8, C), lambda i: (jnp.maximum(8 * i - 1, 0), 0))
    succ = pl.BlockSpec((8, C), lambda i: (jnp.minimum(8 * i + 8, R // 8 - 1), 0))
    return pl.pallas_call(
        dense_kernel, grid=(R // 64,), out_shape=sds((R, C)), in_specs=[main, main, prev, prev, succ, succ], out_specs=main,
        scratch_shapes=[pltpu.VMEM((80, C), F32)], compiler_params=PARAMS, name="dense")(rhs, sigma, rhs, sigma, rhs, sigma)


def rim_kernel(has_ref, xl, sl, xr, sr, xt, st, xb, sb, hup, hdn, hcl, hcr, r_out, secl, secr, sect, secb, X, D, F, S, X2, D2, F2, S2):
    up, down, left, right = (has_ref[k] for k in range(4))

    def strip(x, s, c0, hc, lanes, alive, sec, base, lo):
        lane = lax.broadcasted_iota(jnp.int32, (1, 2 * W), 1)

        def put(v, rows, k):
            a = jnp.where(lane == lanes[0], hc[rows, k:k + 1], v)
            return jnp.where(lane == lanes[1], hc[rows, k + 1:k + 2], a)

        own, above, under = slice(OFF, OFF + R), slice(OFF - 2, OFF), slice(OFF + R, OFF + R + 2)
        cols = slice(c0, c0 + 2 * W)
        for ref, k, src in ((X, 0, x), (D, 2, s)):
            ref[0:OFF] = jnp.zeros((OFF, 2 * W), F32)
            ref[OFF + R:FR] = jnp.zeros((OFF, 2 * W), F32)
            ref[above] = put(hup[k:k + 2, cols], above, k)
            ref[own] = put(src[...], own, k)
            ref[under] = put(hdn[k:k + 2, cols], under, k)
        F[...] = 0.6111111 * (1.0 / (4.0 + D[...])) * X[...]
        mid = slice(8, FR - 8)
        t = 4.0 + D[mid]
        f = F[mid]
        beside = F[9:FR - 7] + F[7:FR - 9] + pltpu.roll(f, 2 * W - 1, axis=1) + pltpu.roll(f, 1, axis=1)
        sec_v = f + 2.75 * (1.0 / t) * (X[mid] - (t * f - beside))
        row = lax.broadcasted_iota(jnp.int32, (FR - 16, 1), 0) + (8 - OFF)
        keep = ((row >= 0) | (up > 0)) & ((row < R) | (down > 0))
        keep = keep & (((lane != lanes[0]) & (lane != lanes[1])) | (alive > 0))
        S[mid] = jnp.where(keep, sec_v, 0.0)
        g = S[own]
        beside = S[OFF + 1:OFF + R + 1] + S[OFF - 1:OFF + R - 1] + pltpu.roll(g, 2 * W - 1, axis=1) + pltpu.roll(g, 1, axis=1)
        res = X[own] - ((4.0 + D[own]) * g - beside)
        r_out[base:base + R] = res[:, lo:lo + W]
        sec[...] = g[:, lo:lo + W]

    strip(xl, sl, 0, hcl, (2 * W - 2, 2 * W - 1), left, secl, 0, 0)
    strip(xr, sr, C - 2 * W, hcr, (0, 1), right, secr, R, W)

    def edge(x, s, own, halo, h, at, alive, gone, sec, sec_rows, base):
        for ref, k, src in ((X2, 0, x), (D2, 2, s)):
            ref[...] = jnp.zeros((32, C), F32)
            ref[own] = src[...]
            ref[halo] = h[k:k + 2]
        F2[...] = 0.6111111 * (1.0 / (4.0 + D2[...])) * X2[...]
        mid = slice(8, 24)
        t = 4.0 + D2[mid]
        f = F2[mid]
        beside = F2[9:25] + F2[7:23] + pltpu.roll(f, C - 1, axis=1) + pltpu.roll(f, 1, axis=1)
        sec_v = f + 2.75 * (1.0 / t) * (X2[mid] - (t * f - beside))
        row = lax.broadcasted_iota(jnp.int32, (16, 1), 0) + 8
        S2[mid] = jnp.where(gone(row) & (alive == 0), 0.0, sec_v)
        sec[...] = S2[sec_rows]
        g = S2[mid]
        sides = pltpu.roll(g, C - 1, axis=1) + pltpu.roll(g, 1, axis=1)
        S2[0:1] = sides[at - 8:at - 7]
        a = slice(at, at + 1)
        res = X2[a] - ((4.0 + D2[a]) * S2[a] - (S2[at + 1:at + 2] + S2[at - 1:at] + S2[0:1]))
        for k in range(C // W):
            r_out[base + k:base + k + 1] = res[:, k * W:(k + 1) * W]

    edge(xt, st, slice(16, 32), slice(14, 16), hup, 16, up, lambda row: row < 16, sect, slice(16, 24), 2 * R)
    edge(xb, sb, slice(0, 16), slice(16, 18), hdn, 15, down, lambda row: row >= 16, secb, slice(8, 16), 2 * R + 16)


def rim(has, rhs, sigma, hup, hdn, hcl, hcr):
    left = pl.BlockSpec((R, 2 * W), lambda i: (0, 0))
    right = pl.BlockSpec((R, 2 * W), lambda i: (0, C // (2 * W) - 1))
    top = pl.BlockSpec((16, C), lambda i: (0, 0))
    bottom = pl.BlockSpec((16, C), lambda i: (R // 16 - 1, 0))

    def whole(shape):
        return pl.BlockSpec(shape, lambda i: (0,) * len(shape))

    outs = [(RIM, W), (R, W), (R, W), (8, C), (8, C)]
    return pl.pallas_call(
        rim_kernel, grid=(1,), out_shape=[sds(s) for s in outs],
        in_specs=[SM, left, left, right, right, top, top, bottom, bottom, whole((4, C)), whole((4, C)), whole((FR, 4)), whole((FR, 4))],
        out_specs=[whole(s) for s in outs],
        scratch_shapes=[pltpu.VMEM((FR, 2 * W), F32)] * 4 + [pltpu.VMEM((32, C), F32)] * 4,
        compiler_params=PARAMS, name="rim")(has, rhs, sigma, rhs, sigma, rhs, sigma, rhs, sigma, hup, hdn, hcl, hcr)


def place_kernel(run_ref, slot_ref, r_ref, tiles_ref, slots_ref):
    slots_ref[...] = jnp.zeros_like(slots_ref)

    def body(b, carry):
        for u in range(16):
            t = b * 16 + u
            row = r_ref[pl.ds(run_ref[t], 1), :]
            tiles_ref[pl.ds(t, 1), :] = row
            slots_ref[pl.ds(slot_ref[t], 1), :] = row
        return carry

    lax.fori_loop(0, T // 16, body, 0)


def place(run, slot, r_rim):
    return pl.pallas_call(place_kernel, out_shape=[sds((T, W)), sds((2 * NG * CAP, W))], in_specs=[SM, SM, VM], out_specs=[VM, VM],
                          compiler_params=PARAMS, name="place")(run, slot, r_rim)


def product_kernel(first, slots_ref, blk_ref, *refs):
    if first:
        q_ref, sums_ref, v_ref = refs
    else:
        prev_ref, q_ref, sums_ref = refs
    i = lax.broadcasted_iota(jnp.int32, (64, W), 0)
    j = lax.broadcasted_iota(jnp.int32, (64, W), 1)
    d = j - i
    band = jnp.where((d >= 0) & (d < 64), 1.0, 0.0)
    mask_top = jnp.where(d == 0, 0.5, band).astype(BF16)
    mask_bot = jnp.where(d == 64, 0.5, 1.0 - band).astype(BF16)

    def fold(v):
        return jnp.sum(v.reshape(CAP // 8, 8, W), axis=0)

    scale = 1.0 if first else prev_ref[3, 0:1, :]

    def body(g, carry):
        rr, pq, vv, ra, qa = carry
        rows = pl.ds(pl.multiple_of(g * CAP, CAP), CAP)
        r = slots_ref[rows, :]
        half = r.astype(BF16)
        b = blk_ref[g, 0:64, :]
        u = jnp.concatenate([b * mask_top, b * mask_bot], axis=0)
        cross = blk_ref[g, 64:72, :].astype(F32)
        swapped = pltpu.roll(half.astype(F32), 64, axis=1)
        q = jnp.dot(half, u, preferred_element_type=F32)
        q = q + lax.dot_general(half, u, (((1,), (1,)), ((), ())), preferred_element_type=F32)
        q = q + (swapped.reshape(CAP // 8, 8, W) * cross[None]).reshape(CAP, W)
        q = q.astype(BF16).astype(F32)
        q_ref[rows, :] = q
        rr = rr + fold(r * r)
        pq = pq + fold(r * q)
        if first:
            ra = ra + fold(jnp.abs(r))
            qa = qa + fold(jnp.abs(q))
        else:
            v = q * scale
            vv = vv + fold(v * v)
        return rr, pq, vv, ra, qa

    zero = jnp.zeros((8, W), F32)
    rr, pq, vv, ra, qa = lax.fori_loop(0, NG, body, (zero,) * 5, unroll=8)
    if first:
        ra, qa = jnp.sum(ra), jnp.sum(qa)
        ok = (qa > 0.0) & (ra > 0.0)
        a0 = jnp.full((1, W), jnp.where(ok, ra, 1.0)) / jnp.full((1, W), jnp.where(ok, qa, 1.0))

        def second_pass(k, acc):
            v = q_ref[pl.ds(pl.multiple_of(k * 64, 64), 64), :] * a0
            return acc + jnp.sum((v * v).reshape(8, 8, W), axis=0)

        vv = lax.fori_loop(0, NG * CAP // 64, second_pass, zero, unroll=8)
        sums_ref[0], sums_ref[1], sums_ref[2] = rr, pq, vv
        sums_ref[3] = jnp.broadcast_to(a0, (8, W))
    else:
        rows = [jnp.sum(v + prev_ref[k], axis=0, keepdims=True) for k, v in enumerate((rr, pq, vv))]
        full = jnp.concatenate(rows + [scale], axis=0)
        for k in range(2 * NG):
            sums_ref[k] = full


def product_first(slots, blocks):
    spec = pl.BlockSpec((NG * CAP, W), lambda i: (0, 0))

    def kernel(s, b, q, sums):
        product_kernel(True, s, b, q, sums, None)

    return pl.pallas_call(kernel, grid=(1,), out_shape=[sds((NG * CAP, W)), sds((4, 8, W))],
                          in_specs=[spec, pl.BlockSpec((NG, PR, W), lambda i: (0, 0, 0))],
                          out_specs=[spec, pl.BlockSpec((4, 8, W), lambda i: (0, 0, 0))], compiler_params=PARAMS, name="product_a")(slots, blocks)


def product_second(slots, blocks, prev):
    def kernel(s, b, p, q, sums):
        product_kernel(False, s, b, p, q, sums)

    return pl.pallas_call(kernel, grid=(1,), out_shape=[sds((NG * CAP, W)), sds((2 * NG, 4, W))],
                          in_specs=[pl.BlockSpec((NG * CAP, W), lambda i: (1, 0)), pl.BlockSpec((NG, PR, W), lambda i: (0, 0, 0)),
                                    pl.BlockSpec((4, 8, W), lambda i: (0, 0, 0))],
                          out_specs=[pl.BlockSpec((NG * CAP, W), lambda i: (0, 0)), pl.BlockSpec((2 * NG, 4, W), lambda i: (0, 0, 0))],
                          compiler_params=PARAMS, name="product_b")(slots, blocks, prev)


def order_kernel(slot_ref, qa_ref, qb_ref, out_ref, q_ref):
    q_ref[0:NG * CAP] = qa_ref[...]
    q_ref[NG * CAP:] = qb_ref[...]

    def body(b, carry):
        for u in range(16):
            t = b * 16 + u
            out_ref[pl.ds(t, 1), :] = q_ref[pl.ds(slot_ref[t], 1), :]
        return carry

    lax.fori_loop(0, T // 16, body, 0)


def order(slot, qa, qb):
    return pl.pallas_call(order_kernel, out_shape=sds((T, W)), in_specs=[SM, VM, VM], out_specs=VM,
                          scratch_shapes=[pltpu.VMEM((2 * NG * CAP, W), F32)], compiler_params=PARAMS, name="order")(slot, qa, qb)


CH = 8
TC = T // CH


def final_kernel(red_ref, r_ref, q_ref, rim_ref, cnt_ref, secl, secr, sect, secb, field_ref, out_ref, res_ref, dir_ref, coef, bl, br, bt, bb, sems):
    step = pl.program_id(0)
    inner = slice(W, C - W)
    copies = [
        pltpu.make_async_copy(bl, out_ref.at[:, 0:W], sems.at[0]),
        pltpu.make_async_copy(br, out_ref.at[:, C - W:C], sems.at[1]),
        pltpu.make_async_copy(bt.at[:, inner], out_ref.at[0:8, inner], sems.at[2]),
        pltpu.make_async_copy(bb.at[:, inner], out_ref.at[R - 8:R, inner], sems.at[3]),
    ]

    @pl.when(step == 0)
    def _():
        rr = jnp.sum(red_ref[:, 0, :])
        pq = jnp.sum(red_ref[:, 1, :])
        alpha = jnp.full((1, W), rr) / jnp.full((1, W), pq)
        t = alpha / red_ref[:, 3, :]
        qq = jnp.sum(t * t * red_ref[:, 2, :])
        rr_new = rr - 2.0 * alpha * pq + qq
        coef[0:1] = alpha
        coef[1:2] = rr_new / rr
        bl[...] = secl[...] + alpha * (cnt_ref[0:R] * rim_ref[0:R])
        br[...] = secr[...] + alpha * (cnt_ref[R:2 * R] * rim_ref[R:2 * R])
        bt[...] = sect[...]
        bb[...] = secb[...]
        for k in range(1, C // W - 1):
            lanes = slice(k * W, (k + 1) * W)
            a = slice(2 * R + k, 2 * R + k + 1)
            bt[0:1, lanes] = sect[0:1, lanes] + alpha * (cnt_ref[a] * rim_ref[a])
            b = slice(2 * R + 16 + k, 2 * R + 17 + k)
            bb[7:8, lanes] = secb[7:8, lanes] + alpha * (cnt_ref[b] * rim_ref[b])
        for c in copies:
            c.start()

    r = r_ref[...]
    res = r - coef[0:1] * q_ref[...]
    res_ref[...] = res
    dir_ref[...] = res + coef[1:2] * r

    @pl.when(step == CH - 1)
    def _():
        for c in copies:
            c.wait()


def final(red, r_tiles, q_tiles, r_rim, cnt, secl, secr, sect, secb, field):
    def whole(shape):
        return pl.BlockSpec(shape, lambda i: (0,) * len(shape))

    chunk = pl.BlockSpec((TC, W), lambda i: (i, 0))
    return pl.pallas_call(
        final_kernel, grid=(CH,), out_shape=[sds((R, C)), sds((T, W)), sds((T, W))],
        in_specs=[whole((2 * NG, 4, W)), chunk, chunk, whole((RIM, W)), whole((RIM, W)), whole((R, W)), whole((R, W)), whole((8, C)), whole((8, C)), ANY],
        out_specs=[ANY, chunk, chunk],
        scratch_shapes=[pltpu.VMEM((8, W), F32), pltpu.VMEM((R, W), F32), pltpu.VMEM((R, W), F32), pltpu.VMEM((8, C), F32), pltpu.VMEM((8, C), F32),
                        pltpu.SemaphoreType.DMA((4,))],
        input_output_aliases={9: 0}, compiler_params=PARAMS, name="final")(red, r_tiles, q_tiles, r_rim, cnt, secl, secr, sect, secb, field)


def per_device(rhs, sigma, tile_list, tile_owner, schur_blocks):
    core = lax.axis_index("c")
    packed = pack(schur_blocks)
    mine = lax.all_to_all(packed, CHIPS, 0, 0, tiled=True)
    theirs = lax.ppermute(mine, "c", [(0, 1), (1, 0)])
    nrow, ncol = 16, 8
    up = [(i, i + 1) for i in range(nrow - 1)]
    down = [(i + 1, i) for i in range(nrow - 1)]
    hup = lax.ppermute(jnp.concatenate([rhs[-2:], sigma[-2:]]), ROWS, up)
    hdn = lax.ppermute(jnp.concatenate([rhs[:2], sigma[:2]]), ROWS, down)

    def cols(sl):
        a = jnp.concatenate([hup[0:2, sl], rhs[:, sl], hdn[0:2, sl]], axis=0)
        b = jnp.concatenate([hup[2:4, sl], sigma[:, sl], hdn[2:4, sl]], axis=0)
        return jnp.concatenate([a.T, b.T], axis=0)

    rightward = [(i, i + 1) for i in range(ncol - 1)]
    leftward = [(i + 1, i) for i in range(ncol - 1)]
    hcl = lax.ppermute(cols(slice(C - 2, C)), COLS, rightward)
    hcr = lax.ppermute(cols(slice(0, 2)), COLS, leftward)
    hcl = jnp.pad(hcl.T, ((OFF - 2, OFF - 2), (0, 0)))
    hcr = jnp.pad(hcr.T, ((OFF - 2, OFF - 2), (0, 0)))
    row_at = lax.axis_index(ROWS)
    col_at = lax.axis_index(COLS)
    has = jnp.stack([row_at > 0, row_at < nrow - 1, col_at > 0, col_at < ncol - 1]).astype(jnp.int32)
    r_rim, secl, secr, sect, secb = rim(has, rhs, sigma, hup, hdn, hcl, hcr)
    runs = C // W
    trow, tcol = tile_list // runs, tile_list % runs
    run = jnp.where(tcol == 0, trow, jnp.where(tcol == runs - 1, R + trow, jnp.where(trow == 0, 2 * R + tcol, 2 * R + 16 + tcol)))
    owner = tile_owner[:, 0]
    onehot = (owner[:, None] == jnp.arange(2 * NG, dtype=jnp.int32)[None, :]).astype(jnp.int32)
    ranks = jnp.cumsum(onehot, axis=0) - onehot
    rank = jnp.sum(ranks * onehot, axis=1)
    slot = (((owner & 1) ^ core) * NG + (owner >> 1)) * CAP + rank
    hits = (jnp.arange(RIM, dtype=jnp.int32)[:, None] == run[None, :]).astype(BF16)
    cnt = jnp.dot(hits, jnp.ones((T, W), BF16), preferred_element_type=F32)
    r_tiles, slots = place(run, slot, r_rim)
    qa, part = product_first(slots, mine)
    qb, sums = product_second(slots, theirs, part)
    red = lax.all_to_all(sums, ALL, 0, 0, tiled=True)
    q_tiles = order(slot, qa, qb)
    field = dense(rhs, sigma)
    return tuple(final(red, r_tiles, q_tiles, r_rim, cnt, secl, secr, sect, secb, field))


def solution(mesh):
    grid = Mesh(mesh.devices.reshape(4, 4, 4, 2), ("y", "z", "x", "c"))
    in_specs = (P(ROWS, COLS), P(ROWS, COLS), P(ALL), P(ALL, None), P(ALL, None, None))
    out_specs = (P(ROWS, COLS), P(ALL, None), P(ALL, None))
    return jax.shard_map(per_device, mesh=grid, in_specs=in_specs, out_specs=out_specs, check_vma=False)
```

```python
import jax
import jax.numpy as jnp
from jax import lax
from jax.experimental import pallas as pl
from jax.experimental.pallas import tpu as pltpu
from jax.sharding import Mesh, PartitionSpec as P

F32 = jnp.float32
BF16 = jnp.bfloat16
R, C, W = 768, 2048, 128
T = 2048
CAP = 32
NG = 64
RIM = 2 * R + 32
PR = 72
OFF = 16
FR = R + 2 * OFF
FC = 896
ROWS = ("y", "z")
COLS = ("x", "c")
ALL = ("y", "z", "x", "c")
CHIPS = ("y", "z", "x")
VM = pl.BlockSpec(memory_space=pltpu.VMEM)
SM = pl.BlockSpec(memory_space=pltpu.SMEM)
ANY = pl.BlockSpec(memory_space=pl.ANY)
ND = 8
C1 = 0.6111111
K1 = C1 + 2.75 * (1.0 - C1)
K2 = 2.75 * C1
PARAMS = pltpu.CompilerParams(vmem_limit_bytes=20 << 20)


def sds(shape, dtype=F32):
    return jax.ShapeDtypeStruct(shape, dtype)


def pack_kernel(s_ref, out_ref):
    s = s_ref[0].astype(F32)
    top, bot = s[:64], s[64:]
    i = lax.broadcasted_iota(jnp.int32, (64, W), 0)
    j = lax.broadcasted_iota(jnp.int32, (64, W), 1)
    d = j - i
    body = jnp.where((d >= 0) & (d < 64), top, bot)
    cross = jnp.where(d == 64, top, 0.0)
    half = jnp.sum(cross, axis=0, keepdims=True)
    row = half + pltpu.roll(half, 64, axis=1)
    full = jnp.concatenate([body, jnp.broadcast_to(row, (8, W))], axis=0).astype(BF16)
    for k in range(NG):
        out_ref[k] = full


def pack(blocks):
    return pl.pallas_call(pack_kernel, out_shape=sds((NG, PR, W), BF16), in_specs=[VM], out_specs=VM, compiler_params=PARAMS, name="pack")(blocks)


def sides(tiles):
    lane = lax.broadcasted_iota(jnp.int32, (1, W), 1)
    n = len(tiles)
    prev = [pltpu.roll(t, 1, axis=1) for t in tiles]
    succ = [pltpu.roll(t, W - 1, axis=1) for t in tiles]
    return [jnp.where(lane == 0, prev[c - 1], prev[c]) + jnp.where(lane == W - 1, succ[(c + 1) % n], succ[c]) for c in range(n)]


def dense_kernel(x_ref, s_ref, xp_ref, sp_ref, xn_ref, sn_ref, out_ref, g_ref, d_ref):
    tiles = [slice(c * W, (c + 1) * W) for c in range(C // W)]
    n = 8 * ND
    for c, lanes in enumerate(tiles):
        dinv = 1.0 / (4.0 + s_ref[:, lanes])
        d_ref[c] = dinv
        g_ref[c, 8:8 + n] = dinv * x_ref[:, lanes]
        g_ref[c, 7:8] = xp_ref[7:8, lanes] / (4.0 + sp_ref[7:8, lanes])
        g_ref[c, 8 + n:9 + n] = xn_ref[0:1, lanes] / (4.0 + sn_ref[0:1, lanes])
    for k in range(ND):
        rows = slice(8 * k, 8 * k + 8)
        side = sides([g_ref[c, 8 * k + 8:8 * k + 16] for c in range(C // W)])
        for c, lanes in enumerate(tiles):
            beside = (g_ref[c, 8 * k + 7:8 * k + 15] + g_ref[c, 8 * k + 9:8 * k + 17]) + side[c]
            out_ref[rows, lanes] = d_ref[c, rows] * (K1 * x_ref[rows, lanes] + K2 * beside)


def dense(rhs, sigma):
    n = 8 * ND
    main = pl.BlockSpec((n, C), lambda i: (i, 0))
    prev = pl.BlockSpec((8, C), lambda i: (jnp.maximum(ND * i - 1, 0), 0))
    succ = pl.BlockSpec((8, C), lambda i: (jnp.minimum(ND * i + ND, R // 8 - 1), 0))
    return pl.pallas_call(
        dense_kernel, grid=(R // n,), out_shape=sds((R, C)), in_specs=[main, main, prev, prev, succ, succ], out_specs=main,
        scratch_shapes=[pltpu.VMEM((C // W, n + 16, W), F32), pltpu.VMEM((C // W, n, W), F32)],
        compiler_params=PARAMS, name="dense")(rhs, sigma, rhs, sigma, rhs, sigma)


def cols_kernel(xl, sl, xr, sr, hup, hdn, right_out, left_out, buf):
    buf[0:OFF] = jnp.zeros((OFF, W), F32)
    buf[OFF + R:FC] = jnp.zeros((FC - OFF - R, W), F32)
    for out, x, s, c0, lane in ((right_out, xr, sr, C - W, W - 8), (left_out, xl, sl, 0, 0)):
        cols = slice(c0, c0 + W)
        for k, src in ((0, x), (2, s)):
            buf[OFF - 2:OFF] = hup[k:k + 2, cols]
            buf[OFF:OFF + R] = src[...]
            buf[OFF + R:OFF + R + 2] = hdn[k:k + 2, cols]
            for c in range(FC // W):
                out[4 * k:4 * k + 8, c * W:(c + 1) * W] = buf[c * W:(c + 1) * W].T[lane:lane + 8]


def edge_cols(rhs, sigma, hup, hdn):
    left = pl.BlockSpec((R, W), lambda i: (0, 0))
    right = pl.BlockSpec((R, W), lambda i: (0, C // W - 1))
    rows = pl.BlockSpec((4, C), lambda i: (0, 0))
    out = pl.BlockSpec((16, FC), lambda i: (0, 0))
    return pl.pallas_call(cols_kernel, grid=(1,), out_shape=[sds((16, FC))] * 2, in_specs=[left, left, right, right, rows, rows], out_specs=[out, out],
                          scratch_shapes=[pltpu.VMEM((FC, W), F32)], compiler_params=PARAMS, name="cols")(rhs, sigma, rhs, sigma, hup, hdn)


def rim_kernel(has_ref, xl, sl, xr, sr, xt, st, xb, sb, hup, hdn, hcl, hcr, r_out, secl, secr, sect, secb, X, D, G, S, H, D2, G2, S2):
    up, down, left, right = (has_ref[k] for k in range(4))
    lane = lax.broadcasted_iota(jnp.int32, (1, W), 1)

    def stencil(x, d, above, under, side):
        return d * (K1 * x + K2 * ((above + under) + side))

    def strip(x, s, c0, hc, m, a, alive, sec, base):
        q = 1 - m
        sel = (lane == a) | (lane == a + 1)
        pad = jnp.zeros((W - 8, W), F32)
        for n in (0, 1):
            for c in range(FC // W):
                got = hc[8 * n:8 * n + 8, c * W:(c + 1) * W]
                H[n, c * W:(c + 1) * W] = jnp.concatenate([got, pad] if a == 0 else [pad, got], axis=0).T
        for c in (0, 1):
            cols = slice(c0 + c * W, c0 + (c + 1) * W)
            for rows, xv, sv in ((slice(OFF - 2, OFF), hup[0:2, cols], hup[2:4, cols]),
                                 (slice(OFF + R, OFF + R + 2), hdn[0:2, cols], hdn[2:4, cols]),
                                 (slice(OFF, OFF + R), x[:, c * W:(c + 1) * W], s[:, c * W:(c + 1) * W])):
                if c == m:
                    xv = jnp.where(sel, H[0, rows], xv)
                    sv = jnp.where(sel, H[1, rows], sv)
                dinv = 1.0 / (4.0 + sv)
                D[c, rows] = dinv
                X[c, rows] = xv
                G[c, rows] = dinv * xv
        live = ~sel | (alive > 0)

        def second(r0, n, ok):
            rows = slice(r0, r0 + n)
            side = sides([G[0, rows], G[1, rows]])
            for c in (0, 1):
                v = stencil(X[c, rows], D[c, rows], G[c, r0 - 1:r0 + n - 1], G[c, r0 + 1:r0 + n + 1], side[c])
                keep = live if c == m else None
                if ok is not None:
                    keep = ok if keep is None else keep & ok
                S[c, rows] = v if keep is None else jnp.where(keep, v, 0.0)

        second(OFF - 1, 1, up > 0)
        second(OFF + R, 1, down > 0)
        for k in range(R // 8):
            second(OFF + 8 * k, 8, None)
        for k in range(R // 8):
            r0 = OFF + 8 * k
            rows = slice(r0, r0 + 8)
            side = sides([S[0, rows], S[1, rows]])[q]
            v = S[q, rows]
            own = slice(8 * k, 8 * k + 8)
            t = 4.0 + s[own, q * W:(q + 1) * W]
            r_out[base + 8 * k:base + 8 * k + 8] = X[q, rows] - (t * v - ((S[q, r0 - 1:r0 + 7] + S[q, r0 + 1:r0 + 9]) + side))
            sec[own] = v

    strip(xl, sl, 0, hcl, 1, W - 2, left, secl, 0)
    strip(xr, sr, C - 2 * W, hcr, 0, 0, right, secr, R)

    def edge(x, s, halo, h, g, o, alive, sec, line, base):
        nt = C // W
        tiles = [slice(c * W, (c + 1) * W) for c in range(nt)]
        ok = alive > 0
        for c, cols in enumerate(tiles):
            dinv = 1.0 / (4.0 + s[:, cols])
            D2[c, 8:24] = dinv
            G2[c, 8:24] = dinv * x[:, cols]
            dinv = 1.0 / (4.0 + halo[2:4, cols])
            D2[c, h:h + 2] = dinv
            G2[c, h:h + 2] = dinv * halo[0:2, cols]
        side = sides([G2[c, g:g + 8] for c in range(nt)])
        outer = sides([G2[c, o:o + 1] for c in range(nt)])
        near = halo[1:2, :] if o < g else halo[0:1, :]
        for c, cols in enumerate(tiles):
            S2[c, g:g + 8] = stencil(x[g - 8:g, cols], D2[c, g:g + 8], G2[c, g - 1:g + 7], G2[c, g + 1:g + 9], side[c])
            v = stencil(near[:, cols], D2[c, o:o + 1], G2[c, o - 1:o], G2[c, o + 1:o + 2], outer[c])
            S2[c, o:o + 1] = jnp.where(ok, v, 0.0)
        side = sides([S2[c, g:g + 8] for c in range(nt)])
        for c, cols in enumerate(tiles):
            v = S2[c, g:g + 8]
            sec[:, cols] = v
            at = g + line
            one = slice(at, at + 1)
            t = 4.0 + s[at - 8:at - 7, cols]
            res = x[at - 8:at - 7, cols] - (t * S2[c, one] - ((S2[c, at - 1:at] + S2[c, at + 1:at + 2]) + side[c][line:line + 1]))
            r_out[base + c:base + c + 1] = res

    edge(xt, st, hup, 6, 8, 7, up, sect, 0, 2 * R)
    edge(xb, sb, hdn, 24, 16, 24, down, secb, 7, 2 * R + 16)


def rim(has, rhs, sigma, hup, hdn, hcl, hcr):
    left = pl.BlockSpec((R, 2 * W), lambda i: (0, 0))
    right = pl.BlockSpec((R, 2 * W), lambda i: (0, C // (2 * W) - 1))
    top = pl.BlockSpec((16, C), lambda i: (0, 0))
    bottom = pl.BlockSpec((16, C), lambda i: (R // 16 - 1, 0))

    def whole(shape):
        return pl.BlockSpec(shape, lambda i: (0,) * len(shape))

    outs = [(RIM, W), (R, W), (R, W), (8, C), (8, C)]
    return pl.pallas_call(
        rim_kernel, grid=(1,), out_shape=[sds(s) for s in outs],
        in_specs=[SM, left, left, right, right, top, top, bottom, bottom, whole((4, C)), whole((4, C)), whole((16, FC)), whole((16, FC))],
        out_specs=[whole(s) for s in outs],
        scratch_shapes=[pltpu.VMEM((2, FR, W), F32)] * 4 + [pltpu.VMEM((2, FC, W), F32)] + [pltpu.VMEM((C // W, 32, W), F32)] * 3,
        compiler_params=PARAMS, name="rim")(has, rhs, sigma, rhs, sigma, rhs, sigma, rhs, sigma, hup, hdn, hcl, hcr)


def place_kernel(run_ref, slot_ref, r_ref, tiles_ref, slots_ref):
    slots_ref[...] = jnp.zeros_like(slots_ref)

    def body(b, carry):
        for u in range(16):
            t = b * 16 + u
            row = r_ref[pl.ds(run_ref[t], 1), :]
            tiles_ref[pl.ds(t, 1), :] = row
            slots_ref[pl.ds(slot_ref[t], 1), :] = row
        return carry

    lax.fori_loop(0, T // 16, body, 0)


def place(run, slot, r_rim):
    return pl.pallas_call(place_kernel, out_shape=[sds((T, W)), sds((2 * NG * CAP, W))], in_specs=[SM, SM, VM], out_specs=[VM, VM],
                          compiler_params=PARAMS, name="place")(run, slot, r_rim)


def product_kernel(first, slots_ref, blk_ref, *refs):
    if first:
        q_ref, sums_ref, v_ref = refs
    else:
        prev_ref, q_ref, sums_ref = refs
    i = lax.broadcasted_iota(jnp.int32, (64, W), 0)
    j = lax.broadcasted_iota(jnp.int32, (64, W), 1)
    d = j - i
    band = jnp.where((d >= 0) & (d < 64), 1.0, 0.0)
    mask_top = jnp.where(d == 0, 0.5, band).astype(BF16)
    mask_bot = jnp.where(d == 64, 0.5, 1.0 - band).astype(BF16)

    def fold(v):
        return jnp.sum(v.reshape(CAP // 8, 8, W), axis=0)

    scale = 1.0 if first else prev_ref[3, 0:1, :]

    def body(g, carry):
        rr, pq, vv, ra, qa = carry
        rows = pl.ds(pl.multiple_of(g * CAP, CAP), CAP)
        r = slots_ref[rows, :]
        half = r.astype(BF16)
        b = blk_ref[g, 0:64, :]
        u = jnp.concatenate([b * mask_top, b * mask_bot], axis=0)
        cross = blk_ref[g, 64:72, :].astype(F32)
        swapped = pltpu.roll(half.astype(F32), 64, axis=1)
        q = jnp.dot(half, u, preferred_element_type=F32)
        q = q + lax.dot_general(half, u, (((1,), (1,)), ((), ())), preferred_element_type=F32)
        q = q + (swapped.reshape(CAP // 8, 8, W) * cross[None]).reshape(CAP, W)
        q = q.astype(BF16).astype(F32)
        q_ref[rows, :] = q
        rr = rr + fold(r * r)
        pq = pq + fold(r * q)
        if first:
            ra = ra + fold(jnp.abs(r))
            qa = qa + fold(jnp.abs(q))
        else:
            v = q * scale
            vv = vv + fold(v * v)
        return rr, pq, vv, ra, qa

    zero = jnp.zeros((8, W), F32)
    rr, pq, vv, ra, qa = lax.fori_loop(0, NG, body, (zero,) * 5, unroll=8)
    if first:
        ra, qa = jnp.sum(ra), jnp.sum(qa)
        ok = (qa > 0.0) & (ra > 0.0)
        a0 = jnp.full((1, W), jnp.where(ok, ra, 1.0)) / jnp.full((1, W), jnp.where(ok, qa, 1.0))

        def second_pass(k, acc):
            v = q_ref[pl.ds(pl.multiple_of(k * 64, 64), 64), :] * a0
            return acc + jnp.sum((v * v).reshape(8, 8, W), axis=0)

        vv = lax.fori_loop(0, NG * CAP // 64, second_pass, zero, unroll=8)
        sums_ref[0], sums_ref[1], sums_ref[2] = rr, pq, vv
        sums_ref[3] = jnp.broadcast_to(a0, (8, W))
    else:
        rows = [jnp.sum(v + prev_ref[k], axis=0, keepdims=True) for k, v in enumerate((rr, pq, vv))]
        full = jnp.concatenate(rows + [scale], axis=0)
        for k in range(2 * NG):
            sums_ref[k] = full


def product_first(slots, blocks):
    spec = pl.BlockSpec((NG * CAP, W), lambda i: (0, 0))

    def kernel(s, b, q, sums):
        product_kernel(True, s, b, q, sums, None)

    return pl.pallas_call(kernel, grid=(1,), out_shape=[sds((2 * NG * CAP, W)), sds((4, 8, W))],
                          in_specs=[spec, pl.BlockSpec((NG, PR, W), lambda i: (0, 0, 0))],
                          out_specs=[spec, pl.BlockSpec((4, 8, W), lambda i: (0, 0, 0))], compiler_params=PARAMS, name="product_a")(slots, blocks)


def product_second(slots, blocks, prev, half):
    def kernel(s, b, p, h, q, sums):
        product_kernel(False, s, b, p, q, sums)

    return pl.pallas_call(kernel, grid=(1,), out_shape=[sds((2 * NG * CAP, W)), sds((2 * NG, 4, W))], input_output_aliases={3: 0},
                          in_specs=[pl.BlockSpec((NG * CAP, W), lambda i: (1, 0)), pl.BlockSpec((NG, PR, W), lambda i: (0, 0, 0)),
                                    pl.BlockSpec((4, 8, W), lambda i: (0, 0, 0)), ANY],
                          out_specs=[pl.BlockSpec((NG * CAP, W), lambda i: (1, 0)), pl.BlockSpec((2 * NG, 4, W), lambda i: (0, 0, 0))],
                          compiler_params=PARAMS, name="product_b")(slots, blocks, prev, half)


def order_kernel(slot_ref, q_ref, out_ref):
    def body(b, carry):
        for u in range(16):
            t = b * 16 + u
            out_ref[pl.ds(t, 1), :] = q_ref[pl.ds(slot_ref[t], 1), :]
        return carry

    lax.fori_loop(0, T // 16, body, 0)


def order(slot, q):
    return pl.pallas_call(order_kernel, out_shape=sds((T, W)), in_specs=[SM, VM], out_specs=VM, compiler_params=PARAMS, name="order")(slot, q)


CH = 8
TC = T // CH


def final_kernel(red_ref, r_ref, q_ref, rim_ref, cnt_ref, secl, secr, sect, secb, field_ref, out_ref, res_ref, dir_ref, coef, bl, br, bt, bb, sems):
    step = pl.program_id(0)
    inner = slice(W, C - W)
    copies = [
        pltpu.make_async_copy(bl, out_ref.at[:, 0:W], sems.at[0]),
        pltpu.make_async_copy(br, out_ref.at[:, C - W:C], sems.at[1]),
        pltpu.make_async_copy(bt.at[:, inner], out_ref.at[0:8, inner], sems.at[2]),
        pltpu.make_async_copy(bb.at[:, inner], out_ref.at[R - 8:R, inner], sems.at[3]),
    ]

    @pl.when(step == 0)
    def _():
        rr = jnp.sum(red_ref[:, 0, :])
        pq = jnp.sum(red_ref[:, 1, :])
        alpha = jnp.full((1, W), rr) / jnp.full((1, W), pq)
        t = alpha / red_ref[:, 3, :]
        qq = jnp.sum(t * t * red_ref[:, 2, :])
        rr_new = rr - 2.0 * alpha * pq + qq
        coef[0:1] = alpha
        coef[1:2] = rr_new / rr
        bl[...] = secl[...] + alpha * (cnt_ref[0:R] * rim_ref[0:R])
        br[...] = secr[...] + alpha * (cnt_ref[R:2 * R] * rim_ref[R:2 * R])
        bt[...] = sect[...]
        bb[...] = secb[...]
        for k in range(1, C // W - 1):
            lanes = slice(k * W, (k + 1) * W)
            a = slice(2 * R + k, 2 * R + k + 1)
            bt[0:1, lanes] = sect[0:1, lanes] + alpha * (cnt_ref[a] * rim_ref[a])
            b = slice(2 * R + 16 + k, 2 * R + 17 + k)
            bb[7:8, lanes] = secb[7:8, lanes] + alpha * (cnt_ref[b] * rim_ref[b])
        for c in copies:
            c.start()

    r = r_ref[...]
    res = r - coef[0:1] * q_ref[...]
    res_ref[...] = res
    dir_ref[...] = res + coef[1:2] * r

    @pl.when(step == CH - 1)
    def _():
        for c in copies:
            c.wait()


def final(red, r_tiles, q_tiles, r_rim, cnt, secl, secr, sect, secb, field):
    def whole(shape):
        return pl.BlockSpec(shape, lambda i: (0,) * len(shape))

    chunk = pl.BlockSpec((TC, W), lambda i: (i, 0))
    return pl.pallas_call(
        final_kernel, grid=(CH,), out_shape=[sds((R, C)), sds((T, W)), sds((T, W))],
        in_specs=[whole((2 * NG, 4, W)), chunk, chunk, whole((RIM, W)), whole((RIM, W)), whole((R, W)), whole((R, W)), whole((8, C)), whole((8, C)), ANY],
        out_specs=[ANY, chunk, chunk],
        scratch_shapes=[pltpu.VMEM((8, W), F32), pltpu.VMEM((R, W), F32), pltpu.VMEM((R, W), F32), pltpu.VMEM((8, C), F32), pltpu.VMEM((8, C), F32),
                        pltpu.SemaphoreType.DMA((4,))],
        input_output_aliases={9: 0}, compiler_params=PARAMS, name="final")(red, r_tiles, q_tiles, r_rim, cnt, secl, secr, sect, secb, field)


def per_device(rhs, sigma, tile_list, tile_owner, schur_blocks):
    core = lax.axis_index("c")
    packed = pack(schur_blocks)
    mine = lax.all_to_all(packed, CHIPS, 0, 0, tiled=True)
    nrow, ncol = 16, 8
    up = [(i, i + 1) for i in range(nrow - 1)]
    down = [(i + 1, i) for i in range(nrow - 1)]
    hup = lax.ppermute(jnp.concatenate([rhs[-2:], sigma[-2:]]), ROWS, up)
    hdn = lax.ppermute(jnp.concatenate([rhs[:2], sigma[:2]]), ROWS, down)

    rightward = [(i, i + 1) for i in range(ncol - 1)]
    leftward = [(i + 1, i) for i in range(ncol - 1)]
    to_right, to_left = edge_cols(rhs, sigma, hup, hdn)
    hcl = lax.ppermute(to_right, COLS, rightward)
    hcr = lax.ppermute(to_left, COLS, leftward)
    row_at = lax.axis_index(ROWS)
    col_at = lax.axis_index(COLS)
    has = jnp.stack([row_at > 0, row_at < nrow - 1, col_at > 0, col_at < ncol - 1]).astype(jnp.int32)
    r_rim, secl, secr, sect, secb = rim(has, rhs, sigma, hup, hdn, hcl, hcr)
    runs = C // W
    trow, tcol = tile_list // runs, tile_list % runs
    run = jnp.where(tcol == 0, trow, jnp.where(tcol == runs - 1, R + trow, jnp.where(trow == 0, 2 * R + tcol, 2 * R + 16 + tcol)))
    owner = tile_owner[:, 0]
    onehot = (owner[:, None] == jnp.arange(2 * NG, dtype=jnp.int32)[None, :]).astype(jnp.int32)
    ranks = jnp.cumsum(onehot, axis=0) - onehot
    rank = jnp.sum(ranks * onehot, axis=1)
    slot = (((owner & 1) ^ core) * NG + (owner >> 1)) * CAP + rank
    hits = (jnp.arange(RIM, dtype=jnp.int32)[:, None] == run[None, :]).astype(BF16)
    cnt = jnp.dot(hits, jnp.ones((T, W), BF16), preferred_element_type=F32)
    r_tiles, slots = place(run, slot, r_rim)
    mine, slots = lax.optimization_barrier((mine, slots))
    theirs = lax.ppermute(mine, "c", [(0, 1), (1, 0)])
    q, part = product_first(slots, mine)
    q, sums = product_second(slots, theirs, part, q)
    red = lax.all_to_all(sums, ALL, 0, 0, tiled=True)
    q_tiles = order(slot, q)
    field = dense(rhs, sigma)
    return tuple(final(red, r_tiles, q_tiles, r_rim, cnt, secl, secr, sect, secb, field))


def solution(mesh):
    grid = Mesh(mesh.devices.reshape(4, 4, 4, 2), ("y", "z", "x", "c"))
    in_specs = (P(ROWS, COLS), P(ROWS, COLS), P(ALL), P(ALL, None), P(ALL, None, None))
    out_specs = (P(ROWS, COLS), P(ALL, None), P(ALL, None))
    return jax.shard_map(per_device, mesh=grid, in_specs=in_specs, out_specs=out_specs, check_vma=False)
```

```python
import jax
import jax.numpy as jnp
from jax import lax
from jax.experimental import pallas as pl
from jax.experimental.pallas import tpu as pltpu
from jax.sharding import Mesh, PartitionSpec as P

F32 = jnp.float32
BF16 = jnp.bfloat16
R, C, W = 768, 2048, 128
T = 2048
CAP = 32
NG = 64
RIM = 2 * R + 32
PR = 72
OFF = 16
FR = R + 2 * OFF
FC = 896
ROWS = ("y", "z")
COLS = ("x", "c")
ALL = ("y", "z", "x", "c")
CHIPS = ("y", "z", "x")
VM = pl.BlockSpec(memory_space=pltpu.VMEM)
SM = pl.BlockSpec(memory_space=pltpu.SMEM)
ANY = pl.BlockSpec(memory_space=pl.ANY)
ND = 8
C1 = 0.6111111
K1 = C1 + 2.75 * (1.0 - C1)
K2 = 2.75 * C1
PARAMS = pltpu.CompilerParams(vmem_limit_bytes=20 << 20)


def sds(shape, dtype=F32):
    return jax.ShapeDtypeStruct(shape, dtype)


def keep(shape, dtype=F32):
    return pltpu.VMEM(shape, dtype)


def in_hbm(x):
    return pltpu.with_memory_space_constraint(x, pltpu.HBM)


def in_vmem(x):
    return pltpu.with_memory_space_constraint(x, pltpu.VMEM)


def pack_kernel(s_ref, out_ref):
    s = s_ref[0].astype(F32)
    top, bot = s[:64], s[64:]
    i = lax.broadcasted_iota(jnp.int32, (64, W), 0)
    j = lax.broadcasted_iota(jnp.int32, (64, W), 1)
    d = j - i
    body = jnp.where((d >= 0) & (d < 64), top, bot)
    cross = jnp.where(d == 64, top, 0.0)
    half = jnp.sum(cross, axis=0, keepdims=True)
    row = half + pltpu.roll(half, 64, axis=1)
    full = jnp.concatenate([body, jnp.broadcast_to(row, (8, W))], axis=0).astype(BF16)
    for k in range(NG):
        out_ref[k] = full


def pack(blocks):
    return pl.pallas_call(pack_kernel, out_shape=sds((NG, PR, W), BF16), in_specs=[VM], out_specs=VM, compiler_params=PARAMS, name="pack")(blocks)


def sides(tiles):
    lane = lax.broadcasted_iota(jnp.int32, (1, W), 1)
    n = len(tiles)
    prev = [pltpu.roll(t, 1, axis=1) for t in tiles]
    succ = [pltpu.roll(t, W - 1, axis=1) for t in tiles]
    return [jnp.where(lane == 0, prev[c - 1], prev[c]) + jnp.where(lane == W - 1, succ[(c + 1) % n], succ[c]) for c in range(n)]


def dense_kernel(x_ref, s_ref, xp_ref, sp_ref, xn_ref, sn_ref, out_ref, g_ref, d_ref):
    tiles = [slice(c * W, (c + 1) * W) for c in range(C // W)]
    n = 8 * ND
    for c, lanes in enumerate(tiles):
        dinv = 1.0 / (4.0 + s_ref[:, lanes])
        d_ref[c] = dinv
        g_ref[c, 8:8 + n] = dinv * x_ref[:, lanes]
        g_ref[c, 7:8] = xp_ref[7:8, lanes] / (4.0 + sp_ref[7:8, lanes])
        g_ref[c, 8 + n:9 + n] = xn_ref[0:1, lanes] / (4.0 + sn_ref[0:1, lanes])
    for k in range(ND):
        rows = slice(8 * k, 8 * k + 8)
        side = sides([g_ref[c, 8 * k + 8:8 * k + 16] for c in range(C // W)])
        for c, lanes in enumerate(tiles):
            beside = (g_ref[c, 8 * k + 7:8 * k + 15] + g_ref[c, 8 * k + 9:8 * k + 17]) + side[c]
            out_ref[rows, lanes] = d_ref[c, rows] * (K1 * x_ref[rows, lanes] + K2 * beside)


def dense(rhs, sigma):
    n = 8 * ND
    main = pl.BlockSpec((n, C), lambda i: (i, 0))
    prev = pl.BlockSpec((8, C), lambda i: (jnp.maximum(ND * i - 1, 0), 0))
    succ = pl.BlockSpec((8, C), lambda i: (jnp.minimum(ND * i + ND, R // 8 - 1), 0))
    return pl.pallas_call(
        dense_kernel, grid=(R // n,), out_shape=sds((R, C)), in_specs=[main, main, prev, prev, succ, succ], out_specs=main,
        scratch_shapes=[pltpu.VMEM((C // W, n + 16, W), F32), pltpu.VMEM((C // W, n, W), F32)],
        compiler_params=PARAMS, name="dense")(rhs, sigma, rhs, sigma, rhs, sigma)


def cols_kernel(xl, sl, xr, sr, hup, hdn, right_out, left_out, buf):
    buf[0:OFF] = jnp.zeros((OFF, W), F32)
    buf[OFF + R:FC] = jnp.zeros((FC - OFF - R, W), F32)
    for out, x, s, c0, lane in ((right_out, xr, sr, C - W, W - 8), (left_out, xl, sl, 0, 0)):
        cols = slice(c0, c0 + W)
        for k, src in ((0, x), (2, s)):
            buf[OFF - 2:OFF] = hup[k:k + 2, cols]
            buf[OFF:OFF + R] = src[...]
            buf[OFF + R:OFF + R + 2] = hdn[k:k + 2, cols]
            for c in range(FC // W):
                out[4 * k:4 * k + 8, c * W:(c + 1) * W] = buf[c * W:(c + 1) * W].T[lane:lane + 8]


def edge_cols(rhs, sigma, hup, hdn):
    left = pl.BlockSpec((R, W), lambda i: (0, 0))
    right = pl.BlockSpec((R, W), lambda i: (0, C // W - 1))
    rows = pl.BlockSpec((4, C), lambda i: (0, 0))
    out = pl.BlockSpec((16, FC), lambda i: (0, 0))
    return pl.pallas_call(cols_kernel, grid=(1,), out_shape=[sds((16, FC))] * 2, in_specs=[left, left, right, right, rows, rows], out_specs=[out, out],
                          scratch_shapes=[pltpu.VMEM((FC, W), F32)], compiler_params=PARAMS, name="cols")(rhs, sigma, rhs, sigma, hup, hdn)


def rim_kernel(has_ref, run_ref, slot_ref, xl, sl, xr, sr, xt, st, xb, sb, hup, hdn, hcl, hcr, cnt, strips_out, rows_out, tiles_out, slots_ref,
               r_out, strips, rows_buf, tiles, sems, X, D, G, S, H, D2, G2, S2):
    up, down, left, right = (has_ref[k] for k in range(4))
    lane = lax.broadcasted_iota(jnp.int32, (1, W), 1)

    def stencil(x, d, above, under, side):
        return d * (K1 * x + K2 * ((above + under) + side))

    def strip(x, s, c0, hc, m, a, alive, base):
        q = 1 - m
        sel = (lane == a) | (lane == a + 1)
        pad = jnp.zeros((W - 8, W), F32)
        for n in (0, 1):
            for c in range(FC // W):
                got = hc[8 * n:8 * n + 8, c * W:(c + 1) * W]
                H[n, c * W:(c + 1) * W] = jnp.concatenate([got, pad] if a == 0 else [pad, got], axis=0).T
        for c in (0, 1):
            cols = slice(c0 + c * W, c0 + (c + 1) * W)
            for rows, xv, sv in ((slice(OFF - 2, OFF), hup[0:2, cols], hup[2:4, cols]),
                                 (slice(OFF + R, OFF + R + 2), hdn[0:2, cols], hdn[2:4, cols]),
                                 (slice(OFF, OFF + R), x[:, c * W:(c + 1) * W], s[:, c * W:(c + 1) * W])):
                if c == m:
                    xv = jnp.where(sel, H[0, rows], xv)
                    sv = jnp.where(sel, H[1, rows], sv)
                dinv = 1.0 / (4.0 + sv)
                D[c, rows] = dinv
                X[c, rows] = xv
                G[c, rows] = dinv * xv
        live = ~sel | (alive > 0)

        def second(r0, n, ok):
            rows = slice(r0, r0 + n)
            side = sides([G[0, rows], G[1, rows]])
            for c in (0, 1):
                v = stencil(X[c, rows], D[c, rows], G[c, r0 - 1:r0 + n - 1], G[c, r0 + 1:r0 + n + 1], side[c])
                keep = live if c == m else None
                if ok is not None:
                    keep = ok if keep is None else keep & ok
                S[c, rows] = v if keep is None else jnp.where(keep, v, 0.0)

        second(OFF - 1, 1, up > 0)
        second(OFF + R, 1, down > 0)
        for k in range(R // 8):
            second(OFF + 8 * k, 8, None)
        for k in range(R // 8):
            r0 = OFF + 8 * k
            rows = slice(r0, r0 + 8)
            side = sides([S[0, rows], S[1, rows]])[q]
            v = S[q, rows]
            own = slice(8 * k, 8 * k + 8)
            t = 4.0 + s[own, q * W:(q + 1) * W]
            res = X[q, rows] - (t * v - ((S[q, r0 - 1:r0 + 7] + S[q, r0 + 1:r0 + 9]) + side))
            at = slice(base + 8 * k, base + 8 * k + 8)
            r_out[at] = res
            strips[0, at] = v
            strips[1, at] = cnt[at] * res

    strip(xl, sl, 0, hcl, 1, W - 2, left, 0)
    strip(xr, sr, C - 2 * W, hcr, 0, 0, right, R)
    copies = [pltpu.make_async_copy(strips, strips_out, sems.at[0]), pltpu.make_async_copy(rows_buf, rows_out, sems.at[1])]
    copies[0].start()

    def edge(x, s, halo, h, g, o, alive, part, line, base):
        nt = C // W
        tiles = [slice(c * W, (c + 1) * W) for c in range(nt)]
        ok = alive > 0
        for c, cols in enumerate(tiles):
            dinv = 1.0 / (4.0 + s[:, cols])
            D2[c, 8:24] = dinv
            G2[c, 8:24] = dinv * x[:, cols]
            dinv = 1.0 / (4.0 + halo[2:4, cols])
            D2[c, h:h + 2] = dinv
            G2[c, h:h + 2] = dinv * halo[0:2, cols]
        side = sides([G2[c, g:g + 8] for c in range(nt)])
        outer = sides([G2[c, o:o + 1] for c in range(nt)])
        near = halo[1:2, :] if o < g else halo[0:1, :]
        for c, cols in enumerate(tiles):
            S2[c, g:g + 8] = stencil(x[g - 8:g, cols], D2[c, g:g + 8], G2[c, g - 1:g + 7], G2[c, g + 1:g + 9], side[c])
            v = stencil(near[:, cols], D2[c, o:o + 1], G2[c, o - 1:o], G2[c, o + 1:o + 2], outer[c])
            S2[c, o:o + 1] = jnp.where(ok, v, 0.0)
        side = sides([S2[c, g:g + 8] for c in range(nt)])
        for c, cols in enumerate(tiles):
            v = S2[c, g:g + 8]
            rows_buf[part, :, cols] = v
            at = g + line
            one = slice(at, at + 1)
            t = 4.0 + s[at - 8:at - 7, cols]
            res = x[at - 8:at - 7, cols] - (t * S2[c, one] - ((S2[c, at - 1:at] + S2[c, at + 1:at + 2]) + side[c][line:line + 1]))
            r_out[base + c:base + c + 1] = res
            rows_buf[2, part:part + 1, cols] = cnt[base + c:base + c + 1] * res

    edge(xt, st, hup, 6, 8, 7, up, 0, 0, 2 * R)
    edge(xb, sb, hdn, 24, 16, 24, down, 1, 7, 2 * R + 16)
    copies[1].start()

    slots_ref[...] = jnp.zeros_like(slots_ref)

    def body(b, carry):
        for u in range(16):
            t = b * 16 + u
            row = r_out[pl.ds(run_ref[t], 1), :]
            tiles[pl.ds(t, 1), :] = row
            slots_ref[pl.ds(slot_ref[t], 1), :] = row
        return carry

    lax.fori_loop(0, T // 16, body, 0)
    last = pltpu.make_async_copy(tiles, tiles_out, sems.at[2])
    last.start()
    for c in copies:
        c.wait()
    last.wait()


def rim(has, run, slot, rhs, sigma, hup, hdn, hcl, hcr, cnt):
    left = pl.BlockSpec((R, 2 * W), lambda i: (0, 0))
    right = pl.BlockSpec((R, 2 * W), lambda i: (0, C // (2 * W) - 1))
    top = pl.BlockSpec((16, C), lambda i: (0, 0))
    bottom = pl.BlockSpec((16, C), lambda i: (R // 16 - 1, 0))
    strips, rows, tiles = (2, 2 * R, W), (3, 8, C), (T, W)
    return pl.pallas_call(
        rim_kernel, grid=(1,), out_shape=[pltpu.HBM(strips, F32), pltpu.HBM(rows, F32), pltpu.HBM(tiles, F32), keep((2 * NG * CAP, W))],
        in_specs=[SM, SM, SM, left, left, right, right, top, top, bottom, bottom, VM, VM, VM, VM, VM],
        out_specs=[ANY, ANY, ANY, VM],
        scratch_shapes=[pltpu.VMEM((RIM, W), F32), pltpu.VMEM(strips, F32), pltpu.VMEM(rows, F32), pltpu.VMEM(tiles, F32), pltpu.SemaphoreType.DMA((3,))]
        + [pltpu.VMEM((2, FR, W), F32)] * 4 + [pltpu.VMEM((2, FC, W), F32)] + [pltpu.VMEM((C // W, 32, W), F32)] * 3,
        compiler_params=PARAMS, name="rim")(has, run, slot, rhs, sigma, rhs, sigma, rhs, sigma, rhs, sigma, hup, hdn, in_vmem(hcl), in_vmem(hcr), in_vmem(cnt))


def product_kernel(first, slots_ref, blk_ref, *refs):
    if first:
        q_ref, sums_ref, v_ref = refs
    else:
        prev_ref, q_ref, sums_ref = refs
    i = lax.broadcasted_iota(jnp.int32, (64, W), 0)
    j = lax.broadcasted_iota(jnp.int32, (64, W), 1)
    d = j - i
    band = jnp.where((d >= 0) & (d < 64), 1.0, 0.0)
    mask_top = jnp.where(d == 0, 0.5, band).astype(BF16)
    mask_bot = jnp.where(d == 64, 0.5, 1.0 - band).astype(BF16)

    def fold(v):
        return jnp.sum(v.reshape(CAP // 8, 8, W), axis=0)

    scale = 1.0 if first else prev_ref[3, 0:1, :]

    def body(g, carry):
        rr, pq, vv, ra, qa = carry
        rows = pl.ds(pl.multiple_of(g * CAP, CAP), CAP)
        r = slots_ref[rows, :]
        half = r.astype(BF16)
        b = blk_ref[g, 0:64, :]
        u = jnp.concatenate([b * mask_top, b * mask_bot], axis=0)
        cross = blk_ref[g, 64:72, :].astype(F32)
        swapped = pltpu.roll(half.astype(F32), 64, axis=1)
        q = jnp.dot(half, u, preferred_element_type=F32)
        q = q + lax.dot_general(half, u, (((1,), (1,)), ((), ())), preferred_element_type=F32)
        q = q + (swapped.reshape(CAP // 8, 8, W) * cross[None]).reshape(CAP, W)
        q = q.astype(BF16).astype(F32)
        q_ref[rows, :] = q
        rr = rr + fold(r * r)
        pq = pq + fold(r * q)
        if first:
            ra = ra + fold(jnp.abs(r))
            qa = qa + fold(jnp.abs(q))
        else:
            v = q * scale
            vv = vv + fold(v * v)
        return rr, pq, vv, ra, qa

    zero = jnp.zeros((8, W), F32)
    rr, pq, vv, ra, qa = lax.fori_loop(0, NG, body, (zero,) * 5, unroll=8)
    if first:
        ra, qa = jnp.sum(ra), jnp.sum(qa)
        ok = (qa > 0.0) & (ra > 0.0)
        a0 = jnp.full((1, W), jnp.where(ok, ra, 1.0)) / jnp.full((1, W), jnp.where(ok, qa, 1.0))

        def second_pass(k, acc):
            v = q_ref[pl.ds(pl.multiple_of(k * 64, 64), 64), :] * a0
            return acc + jnp.sum((v * v).reshape(8, 8, W), axis=0)

        vv = lax.fori_loop(0, NG * CAP // 64, second_pass, zero, unroll=8)
        sums_ref[0], sums_ref[1], sums_ref[2] = rr, pq, vv
        sums_ref[3] = jnp.broadcast_to(a0, (8, W))
    else:
        rows = [jnp.sum(v + prev_ref[k], axis=0, keepdims=True) for k, v in enumerate((rr, pq, vv))]
        full = jnp.concatenate(rows + [scale], axis=0)
        for k in range(2 * NG):
            sums_ref[k] = full


def product_first(slots, blocks):
    def kernel(s, b, q, sums):
        product_kernel(True, s.at[0:NG * CAP], b, q.at[0:NG * CAP], sums, None)

    return pl.pallas_call(kernel, out_shape=[keep((2 * NG * CAP, W)), keep((4, 8, W))], in_specs=[VM, VM], out_specs=[VM, VM],
                          compiler_params=PARAMS, name="product_a")(slots, in_vmem(blocks))


def product_second(slots, blocks, prev, half):
    def kernel(s, b, p, h, q, sums):
        product_kernel(False, s.at[NG * CAP:2 * NG * CAP], b, p, q.at[NG * CAP:2 * NG * CAP], sums)

    return pl.pallas_call(kernel, out_shape=[keep((2 * NG * CAP, W)), keep((2 * NG, 4, W))], input_output_aliases={3: 0},
                          in_specs=[VM, VM, VM, VM], out_specs=[VM, VM], compiler_params=PARAMS, name="product_b")(slots, in_vmem(blocks), prev, half)


def order_kernel(slot_ref, q_ref, out_ref):
    def body(b, carry):
        for u in range(16):
            t = b * 16 + u
            out_ref[pl.ds(t, 1), :] = q_ref[pl.ds(slot_ref[t], 1), :]
        return carry

    lax.fori_loop(0, T // 16, body, 0)


def order(slot, q):
    return pl.pallas_call(order_kernel, out_shape=keep((T, W)), in_specs=[SM, VM], out_specs=VM, compiler_params=PARAMS, name="order")(slot, q)


CH = 8
TC = T // CH
AT = 2


def final_kernel(red_ref, r_ref, q_ref, strips_ref, rows_ref, field_ref, out_ref, res_ref, dir_ref, coef, strips, rows, sems):
    step = pl.program_id(0)
    inner = slice(W, C - W)
    loads = [pltpu.make_async_copy(strips_ref, strips, sems.at[4]), pltpu.make_async_copy(rows_ref, rows, sems.at[5])]
    copies = [
        pltpu.make_async_copy(strips.at[0, 0:R], out_ref.at[:, 0:W], sems.at[0]),
        pltpu.make_async_copy(strips.at[0, R:2 * R], out_ref.at[:, C - W:C], sems.at[1]),
        pltpu.make_async_copy(rows.at[0, :, inner], out_ref.at[0:8, inner], sems.at[2]),
        pltpu.make_async_copy(rows.at[1, :, inner], out_ref.at[R - 8:R, inner], sems.at[3]),
    ]

    @pl.when(step == 0)
    def _():
        for c in loads:
            c.start()
        rr = jnp.sum(red_ref[:, 0, :])
        pq = jnp.sum(red_ref[:, 1, :])
        alpha = jnp.full((1, W), rr) / jnp.full((1, W), pq)
        t = alpha / red_ref[:, 3, :]
        qq = jnp.sum(t * t * red_ref[:, 2, :])
        rr_new = rr - 2.0 * alpha * pq + qq
        coef[0:1] = alpha
        coef[1:2] = rr_new / rr

    at = pl.ds(pl.multiple_of(step * TC, TC), TC)
    r = r_ref[...]
    res = r - coef[0:1] * q_ref[at, :]
    res_ref[...] = res
    dir_ref[...] = res + coef[1:2] * r

    @pl.when(step == AT)
    def _():
        for c in loads:
            c.wait()
        alpha = coef[0:1]
        strips[0] = strips[0] + alpha * strips[1]
        for k in range(C // W):
            lanes = slice(k * W, (k + 1) * W)
            rows[0, 0:1, lanes] = rows[0, 0:1, lanes] + alpha * rows[2, 0:1, lanes]
            rows[1, 7:8, lanes] = rows[1, 7:8, lanes] + alpha * rows[2, 1:2, lanes]
        for c in copies:
            c.start()

    @pl.when(step == CH - 1)
    def _():
        for c in copies:
            c.wait()


def final(red, r_tiles, q_tiles, strips, rows, field):
    chunk = pl.BlockSpec((TC, W), lambda i: (i, 0))
    return pl.pallas_call(
        final_kernel, grid=(CH,), out_shape=[sds((R, C)), sds((T, W)), sds((T, W))],
        in_specs=[VM, chunk, VM, ANY, ANY, ANY],
        out_specs=[ANY, chunk, chunk],
        scratch_shapes=[pltpu.VMEM((8, W), F32), pltpu.VMEM((2, 2 * R, W), F32), pltpu.VMEM((3, 8, C), F32), pltpu.SemaphoreType.DMA((6,))],
        input_output_aliases={5: 0}, compiler_params=PARAMS, name="final")(in_vmem(red), in_hbm(r_tiles), q_tiles, in_hbm(strips), in_hbm(rows), field)


def per_device(rhs, sigma, tile_list, tile_owner, schur_blocks):
    core = lax.axis_index("c")
    big = (in_hbm(rhs), in_hbm(sigma))
    packed = pack(schur_blocks)
    mine = lax.all_to_all(packed, CHIPS, 0, 0, tiled=True)
    nrow, ncol = 16, 8
    up = [(i, i + 1) for i in range(nrow - 1)]
    down = [(i + 1, i) for i in range(nrow - 1)]
    hup = lax.ppermute(jnp.concatenate([rhs[-2:], sigma[-2:]]), ROWS, up)
    hdn = lax.ppermute(jnp.concatenate([rhs[:2], sigma[:2]]), ROWS, down)

    rightward = [(i, i + 1) for i in range(ncol - 1)]
    leftward = [(i + 1, i) for i in range(ncol - 1)]
    to_right, to_left = edge_cols(*big, hup, hdn)
    hcl = lax.ppermute(to_right, COLS, rightward)
    hcr = lax.ppermute(to_left, COLS, leftward)
    row_at = lax.axis_index(ROWS)
    col_at = lax.axis_index(COLS)
    has = jnp.stack([row_at > 0, row_at < nrow - 1, col_at > 0, col_at < ncol - 1]).astype(jnp.int32)
    runs = C // W
    trow, tcol = tile_list // runs, tile_list % runs
    run = jnp.where(tcol == 0, trow, jnp.where(tcol == runs - 1, R + trow, jnp.where(trow == 0, 2 * R + tcol, 2 * R + 16 + tcol)))
    owner = tile_owner[:, 0]
    onehot = (owner[:, None] == jnp.arange(2 * NG, dtype=jnp.int32)[None, :]).astype(jnp.int32)
    ranks = jnp.cumsum(onehot, axis=0) - onehot
    rank = jnp.sum(ranks * onehot, axis=1)
    slot = (((owner & 1) ^ core) * NG + (owner >> 1)) * CAP + rank
    hits = (jnp.arange(RIM, dtype=jnp.int32)[:, None] == run[None, :]).astype(BF16)
    cnt = jnp.dot(hits, jnp.ones((T, W), BF16), preferred_element_type=F32)
    strips, rows, r_tiles, slots = rim(has, run, slot, *big, hup, hdn, hcl, hcr, cnt)
    mine, slots = lax.optimization_barrier((mine, slots))
    theirs = lax.ppermute(mine, "c", [(0, 1), (1, 0)])
    q, part = product_first(slots, mine)
    q, sums = product_second(slots, theirs, part, q)
    q, sums, late_rhs, late_sigma = lax.optimization_barrier((q, sums, rhs, sigma))
    red = lax.all_to_all(sums, ALL, 0, 0, tiled=True)
    q_tiles = order(slot, q)
    field = dense(in_hbm(late_rhs), in_hbm(late_sigma))
    return tuple(final(red, r_tiles, q_tiles, strips, rows, field))


def solution(mesh):
    grid = Mesh(mesh.devices.reshape(4, 4, 4, 2), ("y", "z", "x", "c"))
    in_specs = (P(ROWS, COLS), P(ROWS, COLS), P(ALL), P(ALL, None), P(ALL, None, None))
    out_specs = (P(ROWS, COLS), P(ALL, None), P(ALL, None))
    return jax.shard_map(per_device, mesh=grid, in_specs=in_specs, out_specs=out_specs, check_vma=False)
```

```python
import jax
import jax.numpy as jnp
from jax import lax
from jax.experimental import pallas as pl
from jax.experimental.pallas import tpu as pltpu
from jax.sharding import Mesh, PartitionSpec as P

F32 = jnp.float32
BF16 = jnp.bfloat16
R, C, W = 768, 2048, 128
T = 2048
CAP = 32
NG = 64
RIM = 2 * R + 32
PR = 72
OFF = 16
FR = R + 2 * OFF
FC = 896
ROWS = ("y", "z")
COLS = ("x", "c")
ALL = ("y", "z", "x", "c")
CHIPS = ("y", "z", "x")
VM = pl.BlockSpec(memory_space=pltpu.VMEM)
SM = pl.BlockSpec(memory_space=pltpu.SMEM)
ANY = pl.BlockSpec(memory_space=pl.ANY)
ND = 16
C1 = 0.6111111
K1 = C1 + 2.75 * (1.0 - C1)
K2 = 2.75 * C1
PARAMS = pltpu.CompilerParams(vmem_limit_bytes=20 << 20)


def sds(shape, dtype=F32):
    return jax.ShapeDtypeStruct(shape, dtype)


def keep(shape, dtype=F32):
    return pltpu.VMEM(shape, dtype)


def in_hbm(x):
    return pltpu.with_memory_space_constraint(x, pltpu.HBM)


def in_vmem(x):
    return pltpu.with_memory_space_constraint(x, pltpu.VMEM)


def pack_kernel(s_ref, out_ref):
    s = s_ref[0].astype(F32)
    top, bot = s[:64], s[64:]
    i = lax.broadcasted_iota(jnp.int32, (64, W), 0)
    j = lax.broadcasted_iota(jnp.int32, (64, W), 1)
    d = j - i
    body = jnp.where((d >= 0) & (d < 64), top, bot)
    cross = jnp.where(d == 64, top, 0.0)
    half = jnp.sum(cross, axis=0, keepdims=True)
    row = half + pltpu.roll(half, 64, axis=1)
    full = jnp.concatenate([body, jnp.broadcast_to(row, (8, W))], axis=0).astype(BF16)
    for k in range(NG):
        out_ref[k] = full


def pack(blocks):
    return pl.pallas_call(pack_kernel, out_shape=sds((NG, PR, W), BF16), in_specs=[VM], out_specs=VM, compiler_params=PARAMS, name="pack")(blocks)


def sides(tiles):
    lane = lax.broadcasted_iota(jnp.int32, (1, W), 1)
    n = len(tiles)
    prev = [pltpu.roll(t, 1, axis=1) for t in tiles]
    succ = [pltpu.roll(t, W - 1, axis=1) for t in tiles]
    return [jnp.where(lane == 0, prev[c - 1], prev[c]) + jnp.where(lane == W - 1, succ[(c + 1) % n], succ[c]) for c in range(n)]


def dense_kernel(x_ref, s_ref, xp_ref, sp_ref, xn_ref, sn_ref, out_ref, g_ref, d_ref):
    tiles = [slice(c * W, (c + 1) * W) for c in range(C // W)]
    n = 8 * ND
    for c, lanes in enumerate(tiles):
        dinv = 1.0 / (4.0 + s_ref[:, lanes])
        d_ref[c] = dinv
        g_ref[c, 8:8 + n] = dinv * x_ref[:, lanes]
        g_ref[c, 7:8] = xp_ref[7:8, lanes] / (4.0 + sp_ref[7:8, lanes])
        g_ref[c, 8 + n:9 + n] = xn_ref[0:1, lanes] / (4.0 + sn_ref[0:1, lanes])
    for k in range(ND):
        rows = slice(8 * k, 8 * k + 8)
        side = sides([g_ref[c, 8 * k + 8:8 * k + 16] for c in range(C // W)])
        for c, lanes in enumerate(tiles):
            beside = (g_ref[c, 8 * k + 7:8 * k + 15] + g_ref[c, 8 * k + 9:8 * k + 17]) + side[c]
            out_ref[rows, lanes] = d_ref[c, rows] * (K1 * x_ref[rows, lanes] + K2 * beside)


def dense(rhs, sigma):
    n = 8 * ND
    main = pl.BlockSpec((n, C), lambda i: (i, 0))
    prev = pl.BlockSpec((8, C), lambda i: (jnp.maximum(ND * i - 1, 0), 0))
    succ = pl.BlockSpec((8, C), lambda i: (jnp.minimum(ND * i + ND, R // 8 - 1), 0))
    return pl.pallas_call(
        dense_kernel, grid=(R // n,), out_shape=sds((R, C)), in_specs=[main, main, prev, prev, succ, succ], out_specs=main,
        scratch_shapes=[pltpu.VMEM((C // W, n + 16, W), F32), pltpu.VMEM((C // W, n, W), F32)],
        compiler_params=PARAMS, name="dense")(rhs, sigma, rhs, sigma, rhs, sigma)


def cols_kernel(xl, sl, xr, sr, hup, hdn, right_out, left_out, buf):
    buf[0:OFF] = jnp.zeros((OFF, W), F32)
    buf[OFF + R:FC] = jnp.zeros((FC - OFF - R, W), F32)
    for out, x, s, c0, lane in ((right_out, xr, sr, C - W, W - 8), (left_out, xl, sl, 0, 0)):
        cols = slice(c0, c0 + W)
        for k, src in ((0, x), (2, s)):
            buf[OFF - 2:OFF] = hup[k:k + 2, cols]
            buf[OFF:OFF + R] = src[...]
            buf[OFF + R:OFF + R + 2] = hdn[k:k + 2, cols]
            for c in range(FC // W):
                out[4 * k:4 * k + 8, c * W:(c + 1) * W] = buf[c * W:(c + 1) * W].T[lane:lane + 8]


def edge_cols(rhs, sigma, hup, hdn):
    left = pl.BlockSpec((R, W), lambda i: (0, 0))
    right = pl.BlockSpec((R, W), lambda i: (0, C // W - 1))
    rows = pl.BlockSpec((4, C), lambda i: (0, 0))
    out = pl.BlockSpec((16, FC), lambda i: (0, 0))
    return pl.pallas_call(cols_kernel, grid=(1,), out_shape=[sds((16, FC))] * 2, in_specs=[left, left, right, right, rows, rows], out_specs=[out, out],
                          scratch_shapes=[pltpu.VMEM((FC, W), F32)], compiler_params=PARAMS, name="cols")(rhs, sigma, rhs, sigma, hup, hdn)


def rim_kernel(has_ref, run_ref, slot_ref, xl, sl, xr, sr, xt, st, xb, sb, hup, hdn, hcl, hcr, cnt, strips_out, rows_out, tiles_out, slots_ref,
               r_out, strips, rows_buf, tiles, sems, X, D, G, S, H, D2, G2, S2):
    up, down, left, right = (has_ref[k] for k in range(4))
    lane = lax.broadcasted_iota(jnp.int32, (1, W), 1)

    def stencil(x, d, above, under, side):
        return d * (K1 * x + K2 * ((above + under) + side))

    def strip(x, s, c0, hc, m, a, alive, base):
        q = 1 - m
        sel = (lane == a) | (lane == a + 1)
        pad = jnp.zeros((W - 8, W), F32)
        for n in (0, 1):
            for c in range(FC // W):
                got = hc[8 * n:8 * n + 8, c * W:(c + 1) * W]
                H[n, c * W:(c + 1) * W] = jnp.concatenate([got, pad] if a == 0 else [pad, got], axis=0).T
        for c in (0, 1):
            cols = slice(c0 + c * W, c0 + (c + 1) * W)
            for rows, xv, sv in ((slice(OFF - 2, OFF), hup[0:2, cols], hup[2:4, cols]),
                                 (slice(OFF + R, OFF + R + 2), hdn[0:2, cols], hdn[2:4, cols]),
                                 (slice(OFF, OFF + R), x[:, c * W:(c + 1) * W], s[:, c * W:(c + 1) * W])):
                if c == m:
                    xv = jnp.where(sel, H[0, rows], xv)
                    sv = jnp.where(sel, H[1, rows], sv)
                dinv = 1.0 / (4.0 + sv)
                D[c, rows] = dinv
                X[c, rows] = xv
                G[c, rows] = dinv * xv
        live = ~sel | (alive > 0)

        def second(r0, n, ok):
            rows = slice(r0, r0 + n)
            side = sides([G[0, rows], G[1, rows]])
            for c in (0, 1):
                v = stencil(X[c, rows], D[c, rows], G[c, r0 - 1:r0 + n - 1], G[c, r0 + 1:r0 + n + 1], side[c])
                keep = live if c == m else None
                if ok is not None:
                    keep = ok if keep is None else keep & ok
                S[c, rows] = v if keep is None else jnp.where(keep, v, 0.0)

        second(OFF - 1, 1, up > 0)
        second(OFF + R, 1, down > 0)
        for k in range(R // 8):
            second(OFF + 8 * k, 8, None)
        for k in range(R // 8):
            r0 = OFF + 8 * k
            rows = slice(r0, r0 + 8)
            side = sides([S[0, rows], S[1, rows]])[q]
            v = S[q, rows]
            own = slice(8 * k, 8 * k + 8)
            t = 4.0 + s[own, q * W:(q + 1) * W]
            res = X[q, rows] - (t * v - ((S[q, r0 - 1:r0 + 7] + S[q, r0 + 1:r0 + 9]) + side))
            at = slice(base + 8 * k, base + 8 * k + 8)
            r_out[at] = res
            strips[0, at] = v
            strips[1, at] = cnt[at] * res

    strip(xl, sl, 0, hcl, 1, W - 2, left, 0)
    strip(xr, sr, C - 2 * W, hcr, 0, 0, right, R)
    copies = [pltpu.make_async_copy(strips, strips_out, sems.at[0]), pltpu.make_async_copy(rows_buf, rows_out, sems.at[1])]
    copies[0].start()

    def edge(x, s, halo, h, g, o, alive, part, line, base):
        nt = C // W
        tiles = [slice(c * W, (c + 1) * W) for c in range(nt)]
        ok = alive > 0
        for c, cols in enumerate(tiles):
            dinv = 1.0 / (4.0 + s[:, cols])
            D2[c, 8:24] = dinv
            G2[c, 8:24] = dinv * x[:, cols]
            dinv = 1.0 / (4.0 + halo[2:4, cols])
            D2[c, h:h + 2] = dinv
            G2[c, h:h + 2] = dinv * halo[0:2, cols]
        side = sides([G2[c, g:g + 8] for c in range(nt)])
        outer = sides([G2[c, o:o + 1] for c in range(nt)])
        near = halo[1:2, :] if o < g else halo[0:1, :]
        for c, cols in enumerate(tiles):
            S2[c, g:g + 8] = stencil(x[g - 8:g, cols], D2[c, g:g + 8], G2[c, g - 1:g + 7], G2[c, g + 1:g + 9], side[c])
            v = stencil(near[:, cols], D2[c, o:o + 1], G2[c, o - 1:o], G2[c, o + 1:o + 2], outer[c])
            S2[c, o:o + 1] = jnp.where(ok, v, 0.0)
        side = sides([S2[c, g:g + 8] for c in range(nt)])
        for c, cols in enumerate(tiles):
            v = S2[c, g:g + 8]
            rows_buf[part, :, cols] = v
            at = g + line
            one = slice(at, at + 1)
            t = 4.0 + s[at - 8:at - 7, cols]
            res = x[at - 8:at - 7, cols] - (t * S2[c, one] - ((S2[c, at - 1:at] + S2[c, at + 1:at + 2]) + side[c][line:line + 1]))
            r_out[base + c:base + c + 1] = res
            rows_buf[2, part:part + 1, cols] = cnt[base + c:base + c + 1] * res

    edge(xt, st, hup, 6, 8, 7, up, 0, 0, 2 * R)
    edge(xb, sb, hdn, 24, 16, 24, down, 1, 7, 2 * R + 16)
    copies[1].start()

    slots_ref[...] = jnp.zeros_like(slots_ref)

    def body(b, carry):
        for u in range(16):
            t = b * 16 + u
            row = r_out[pl.ds(run_ref[t], 1), :]
            tiles[pl.ds(t, 1), :] = row
            slots_ref[pl.ds(slot_ref[t], 1), :] = row
        return carry

    lax.fori_loop(0, T // 16, body, 0)
    last = pltpu.make_async_copy(tiles, tiles_out, sems.at[2])
    last.start()
    for c in copies:
        c.wait()
    last.wait()


def rim(has, run, slot, rhs, sigma, hup, hdn, hcl, hcr, cnt):
    left = pl.BlockSpec((R, 2 * W), lambda i: (0, 0))
    right = pl.BlockSpec((R, 2 * W), lambda i: (0, C // (2 * W) - 1))
    top = pl.BlockSpec((16, C), lambda i: (0, 0))
    bottom = pl.BlockSpec((16, C), lambda i: (R // 16 - 1, 0))
    strips, rows, tiles = (2, 2 * R, W), (3, 8, C), (T, W)
    return pl.pallas_call(
        rim_kernel, grid=(1,), out_shape=[pltpu.HBM(strips, F32), pltpu.HBM(rows, F32), pltpu.HBM(tiles, F32), keep((2 * NG * CAP, W))],
        in_specs=[SM, SM, SM, left, left, right, right, top, top, bottom, bottom, VM, VM, VM, VM, VM],
        out_specs=[ANY, ANY, ANY, VM],
        scratch_shapes=[pltpu.VMEM((RIM, W), F32), pltpu.VMEM(strips, F32), pltpu.VMEM(rows, F32), pltpu.VMEM(tiles, F32), pltpu.SemaphoreType.DMA((3,))]
        + [pltpu.VMEM((2, FR, W), F32)] * 4 + [pltpu.VMEM((2, FC, W), F32)] + [pltpu.VMEM((C // W, 32, W), F32)] * 3,
        compiler_params=PARAMS, name="rim")(has, run, slot, rhs, sigma, rhs, sigma, rhs, sigma, rhs, sigma, hup, hdn, in_vmem(hcl), in_vmem(hcr), in_vmem(cnt))


def product_kernel(first, slots_ref, blk_ref, *refs):
    if first:
        q_ref, sums_ref, v_ref = refs
    else:
        prev_ref, q_ref, sums_ref = refs
    i = lax.broadcasted_iota(jnp.int32, (64, W), 0)
    j = lax.broadcasted_iota(jnp.int32, (64, W), 1)
    d = j - i
    band = jnp.where((d >= 0) & (d < 64), 1.0, 0.0)
    mask_top = jnp.where(d == 0, 0.5, band).astype(BF16)
    mask_bot = jnp.where(d == 64, 0.5, 1.0 - band).astype(BF16)

    def fold(v):
        return jnp.sum(v.reshape(CAP // 8, 8, W), axis=0)

    scale = 1.0 if first else prev_ref[3, 0:1, :]

    def body(g, carry):
        rr, pq, vv, ra, qa = carry
        rows = pl.ds(pl.multiple_of(g * CAP, CAP), CAP)
        r = slots_ref[rows, :]
        half = r.astype(BF16)
        b = blk_ref[g, 0:64, :]
        u = jnp.concatenate([b * mask_top, b * mask_bot], axis=0)
        cross = blk_ref[g, 64:72, :].astype(F32)
        swapped = pltpu.roll(half.astype(F32), 64, axis=1)
        q = jnp.dot(half, u, preferred_element_type=F32)
        q = q + lax.dot_general(half, u, (((1,), (1,)), ((), ())), preferred_element_type=F32)
        q = q + (swapped.reshape(CAP // 8, 8, W) * cross[None]).reshape(CAP, W)
        q = q.astype(BF16).astype(F32)
        q_ref[rows, :] = q
        rr = rr + fold(r * r)
        pq = pq + fold(r * q)
        if first:
            ra = ra + fold(jnp.abs(r))
            qa = qa + fold(jnp.abs(q))
        else:
            v = q * scale
            vv = vv + fold(v * v)
        return rr, pq, vv, ra, qa

    zero = jnp.zeros((8, W), F32)
    rr, pq, vv, ra, qa = lax.fori_loop(0, NG, body, (zero,) * 5, unroll=8)
    if first:
        ra, qa = jnp.sum(ra), jnp.sum(qa)
        ok = (qa > 0.0) & (ra > 0.0)
        a0 = jnp.full((1, W), jnp.where(ok, ra, 1.0)) / jnp.full((1, W), jnp.where(ok, qa, 1.0))

        def second_pass(k, acc):
            v = q_ref[pl.ds(pl.multiple_of(k * 64, 64), 64), :] * a0
            return acc + jnp.sum((v * v).reshape(8, 8, W), axis=0)

        vv = lax.fori_loop(0, NG * CAP // 64, second_pass, zero, unroll=8)
        sums_ref[0], sums_ref[1], sums_ref[2] = rr, pq, vv
        sums_ref[3] = jnp.broadcast_to(a0, (8, W))
    else:
        rows = [jnp.sum(v + prev_ref[k], axis=0, keepdims=True) for k, v in enumerate((rr, pq, vv))]
        full = jnp.concatenate(rows + [scale], axis=0)
        for k in range(2 * NG):
            sums_ref[k] = full


def product_first(slots, blocks):
    def kernel(s, b, q, sums):
        here = q.at[0:NG * CAP]
        product_kernel(True, here, b, here, sums, None)

    return pl.pallas_call(kernel, out_shape=[keep((2 * NG * CAP, W)), keep((4, 8, W))], in_specs=[VM, VM], out_specs=[VM, VM], input_output_aliases={0: 0},
                          compiler_params=PARAMS, name="product_a")(slots, in_vmem(blocks))


def product_second(slots, blocks, prev):
    def kernel(s, b, p, q, sums):
        here = q.at[NG * CAP:2 * NG * CAP]
        product_kernel(False, here, b, p, here, sums)

    return pl.pallas_call(kernel, out_shape=[keep((2 * NG * CAP, W)), keep((2 * NG, 4, W))], input_output_aliases={0: 0},
                          in_specs=[VM, VM, VM], out_specs=[VM, VM], compiler_params=PARAMS, name="product_b")(slots, in_vmem(blocks), prev)


def order_kernel(slot_ref, q_ref, out_ref):
    def body(b, carry):
        for u in range(16):
            t = b * 16 + u
            out_ref[pl.ds(t, 1), :] = q_ref[pl.ds(slot_ref[t], 1), :]
        return carry

    lax.fori_loop(0, T // 16, body, 0)


def order(slot, q):
    return pl.pallas_call(order_kernel, out_shape=keep((T, W)), in_specs=[SM, VM], out_specs=VM, compiler_params=PARAMS, name="order")(slot, q)


CH = 4
TC = T // CH


def final_kernel(red_ref, r_hbm, q_ref, strips_ref, rows_ref, field_ref, out_ref, res_hbm, dir_hbm, r_buf, res_buf, dir_buf, strips, rows, ins, outs):
    inner = slice(W, C - W)
    parts = [slice(k * TC, (k + 1) * TC) for k in range(CH)]
    tiles_in = [pltpu.make_async_copy(r_hbm.at[p], r_buf.at[p], ins.at[k]) for k, p in enumerate(parts)]
    rim_in = [pltpu.make_async_copy(strips_ref, strips, ins.at[CH]), pltpu.make_async_copy(rows_ref, rows, ins.at[CH + 1])]
    for c in tiles_in + rim_in:
        c.start()
    rr = jnp.sum(red_ref[:, 0, :])
    pq = jnp.sum(red_ref[:, 1, :])
    alpha = jnp.full((1, W), rr) / jnp.full((1, W), pq)
    t = alpha / red_ref[:, 3, :]
    qq = jnp.sum(t * t * red_ref[:, 2, :])
    beta = (rr - 2.0 * alpha * pq + qq) / rr
    sent = []

    def send(src, dst):
        c = pltpu.make_async_copy(src, dst, outs.at[len(sent)])
        c.start()
        sent.append(c)

    def rim_out():
        for c in rim_in:
            c.wait()
        strips[0] = strips[0] + alpha * strips[1]
        send(strips.at[0, 0:R], out_ref.at[:, 0:W])
        send(strips.at[0, R:2 * R], out_ref.at[:, C - W:C])
        for k in range(C // W):
            lanes = slice(k * W, (k + 1) * W)
            rows[0, 0:1, lanes] = rows[0, 0:1, lanes] + alpha * rows[2, 0:1, lanes]
            rows[1, 7:8, lanes] = rows[1, 7:8, lanes] + alpha * rows[2, 1:2, lanes]
        send(rows.at[0, :, inner], out_ref.at[0:8, inner])
        send(rows.at[1, :, inner], out_ref.at[R - 8:R, inner])

    for k, p in enumerate(parts):
        tiles_in[k].wait()
        r = r_buf[p]
        res = r - alpha * q_ref[p]
        res_buf[p] = res
        dir_buf[p] = res + beta * r
        send(res_buf.at[p], res_hbm.at[p])
        send(dir_buf.at[p], dir_hbm.at[p])
        if k == 1:
            rim_out()
    for c in sent:
        c.wait()


def final(red, r_tiles, q_tiles, strips, rows, field):
    return pl.pallas_call(
        final_kernel, out_shape=[sds((R, C)), sds((T, W)), sds((T, W))],
        in_specs=[VM, ANY, VM, ANY, ANY, ANY], out_specs=[ANY, ANY, ANY],
        scratch_shapes=[pltpu.VMEM((T, W), F32)] * 3 + [pltpu.VMEM((2, 2 * R, W), F32), pltpu.VMEM((3, 8, C), F32),
                        pltpu.SemaphoreType.DMA((CH + 2,)), pltpu.SemaphoreType.DMA((2 * CH + 4,))],
        input_output_aliases={5: 0}, compiler_params=PARAMS, name="final")(in_vmem(red), in_hbm(r_tiles), q_tiles, in_hbm(strips), in_hbm(rows), field)


def per_device(rhs, sigma, tile_list, tile_owner, schur_blocks):
    core = lax.axis_index("c")
    big = (in_hbm(rhs), in_hbm(sigma))
    packed, *ready = lax.optimization_barrier((pack(schur_blocks), rhs, sigma))
    mine = lax.all_to_all(packed, CHIPS, 0, 0, tiled=True)
    nrow, ncol = 16, 8
    up = [(i, i + 1) for i in range(nrow - 1)]
    down = [(i + 1, i) for i in range(nrow - 1)]
    tail, head = jnp.concatenate([ready[0][-2:], ready[1][-2:]]), jnp.concatenate([ready[0][:2], ready[1][:2]])
    hup = lax.ppermute(tail, ROWS, up)
    hdn = lax.ppermute(head, ROWS, down)

    rightward = [(i, i + 1) for i in range(ncol - 1)]
    leftward = [(i + 1, i) for i in range(ncol - 1)]
    to_right, to_left, tile_list = lax.optimization_barrier((*edge_cols(*big, hup, hdn), tile_list))
    hcl = lax.ppermute(to_right, COLS, rightward)
    hcr = lax.ppermute(to_left, COLS, leftward)
    row_at = lax.axis_index(ROWS)
    col_at = lax.axis_index(COLS)
    has = jnp.stack([row_at > 0, row_at < nrow - 1, col_at > 0, col_at < ncol - 1]).astype(jnp.int32)
    runs = C // W
    trow, tcol = tile_list // runs, tile_list % runs
    run = jnp.where(tcol == 0, trow, jnp.where(tcol == runs - 1, R + trow, jnp.where(trow == 0, 2 * R + tcol, 2 * R + 16 + tcol)))
    owner = tile_owner[:, 0]
    onehot = (owner[:, None] == jnp.arange(2 * NG, dtype=jnp.int32)[None, :]).astype(jnp.int32)
    ranks = jnp.cumsum(onehot, axis=0) - onehot
    rank = jnp.sum(ranks * onehot, axis=1)
    slot = (((owner & 1) ^ core) * NG + (owner >> 1)) * CAP + rank
    hits = (jnp.arange(RIM, dtype=jnp.int32)[:, None] == run[None, :]).astype(BF16)
    cnt = jnp.dot(hits, jnp.ones((T, W), BF16), preferred_element_type=F32)
    strips, rows, r_tiles, slots = rim(has, run, slot, *big, hup, hdn, hcl, hcr, cnt)
    mine, slots = lax.optimization_barrier((mine, slots))
    theirs = lax.ppermute(mine, "c", [(0, 1), (1, 0)])
    q, part = product_first(slots, mine)
    q, sums = product_second(q, theirs, part)
    q, sums, late_rhs, late_sigma = lax.optimization_barrier((q, sums, rhs, sigma))
    red = lax.all_to_all(sums, ALL, 0, 0, tiled=True)
    q_tiles = order(slot, q)
    field = dense(in_hbm(late_rhs), in_hbm(late_sigma))
    return tuple(final(red, r_tiles, q_tiles, strips, rows, field))


def solution(mesh):
    grid = Mesh(mesh.devices.reshape(4, 4, 4, 2), ("y", "z", "x", "c"))
    in_specs = (P(ROWS, COLS), P(ROWS, COLS), P(ALL), P(ALL, None), P(ALL, None, None))
    out_specs = (P(ROWS, COLS), P(ALL, None), P(ALL, None))
    return jax.shard_map(per_device, mesh=grid, in_specs=in_specs, out_specs=out_specs, check_vma=False)
```

```python
import jax
import jax.numpy as jnp
from jax import lax
from jax.experimental import pallas as pl
from jax.experimental.pallas import tpu as pltpu
from jax.sharding import Mesh, PartitionSpec as P

F32 = jnp.float32
BF16 = jnp.bfloat16
R, C, W = 768, 2048, 128
T = 2048
CAP = 32
NG = 64
RIM = 2 * R + 32
PR = 72
OFF = 16
FR = R + 2 * OFF
FC = 896
ROWS = ("y", "z")
COLS = ("x", "c")
ALL = ("y", "z", "x", "c")
CHIPS = ("y", "z", "x")
VM = pl.BlockSpec(memory_space=pltpu.VMEM)
SM = pl.BlockSpec(memory_space=pltpu.SMEM)
ANY = pl.BlockSpec(memory_space=pl.ANY)
ND = 12
C1 = 0.6111111
K1 = C1 + 2.75 * (1.0 - C1)
K2 = 2.75 * C1
PARAMS = pltpu.CompilerParams(vmem_limit_bytes=20 << 20)


def sds(shape, dtype=F32):
    return jax.ShapeDtypeStruct(shape, dtype)


def keep(shape, dtype=F32):
    return pltpu.VMEM(shape, dtype)


def in_hbm(x):
    return pltpu.with_memory_space_constraint(x, pltpu.HBM)


def in_vmem(x):
    return pltpu.with_memory_space_constraint(x, pltpu.VMEM)


def pack_kernel(s_ref, out_ref):
    s = s_ref[0].astype(F32)
    top, bot = s[:64], s[64:]
    i = lax.broadcasted_iota(jnp.int32, (64, W), 0)
    j = lax.broadcasted_iota(jnp.int32, (64, W), 1)
    d = j - i
    body = jnp.where((d >= 0) & (d < 64), top, bot)
    cross = jnp.where(d == 64, top, 0.0)
    half = jnp.sum(cross, axis=0, keepdims=True)
    row = half + pltpu.roll(half, 64, axis=1)
    full = jnp.concatenate([body, jnp.broadcast_to(row, (8, W))], axis=0).astype(BF16)
    for k in range(NG):
        out_ref[k] = full


def pack(blocks):
    return pl.pallas_call(pack_kernel, out_shape=sds((NG, PR, W), BF16), in_specs=[VM], out_specs=VM, compiler_params=PARAMS, name="pack")(blocks)


def sides(tiles):
    lane = lax.broadcasted_iota(jnp.int32, (1, W), 1)
    n = len(tiles)
    prev = [pltpu.roll(t, 1, axis=1) for t in tiles]
    succ = [pltpu.roll(t, W - 1, axis=1) for t in tiles]
    return [jnp.where(lane == 0, prev[c - 1], prev[c]) + jnp.where(lane == W - 1, succ[(c + 1) % n], succ[c]) for c in range(n)]


def dense_kernel(slot_ref, q_ref, x_ref, s_ref, xp_ref, sp_ref, xn_ref, sn_ref, out_ref, tiles_ref, g_ref, d_ref):
    share = T // (R // (8 * ND))
    first = pl.program_id(0) * share

    def body(b, carry):
        for u in range(16):
            t = first + b * 16 + u
            tiles_ref[pl.ds(t, 1), :] = q_ref[pl.ds(slot_ref[t], 1), :]
        return carry

    lax.fori_loop(0, share // 16, body, 0)
    tiles = [slice(c * W, (c + 1) * W) for c in range(C // W)]
    n = 8 * ND
    for c, lanes in enumerate(tiles):
        dinv = 1.0 / (4.0 + s_ref[:, lanes])
        d_ref[c] = dinv
        g_ref[c, 8:8 + n] = dinv * x_ref[:, lanes]
        g_ref[c, 7:8] = xp_ref[7:8, lanes] / (4.0 + sp_ref[7:8, lanes])
        g_ref[c, 8 + n:9 + n] = xn_ref[0:1, lanes] / (4.0 + sn_ref[0:1, lanes])
    for k in range(ND):
        rows = slice(8 * k, 8 * k + 8)
        side = sides([g_ref[c, 8 * k + 8:8 * k + 16] for c in range(C // W)])
        for c, lanes in enumerate(tiles):
            beside = (g_ref[c, 8 * k + 7:8 * k + 15] + g_ref[c, 8 * k + 9:8 * k + 17]) + side[c]
            out_ref[rows, lanes] = d_ref[c, rows] * (K1 * x_ref[rows, lanes] + K2 * beside)


def dense(slot, q, rhs, sigma):
    n = 8 * ND
    main = pl.BlockSpec((n, C), lambda i: (i, 0))
    prev = pl.BlockSpec((8, C), lambda i: (jnp.maximum(ND * i - 1, 0), 0))
    succ = pl.BlockSpec((8, C), lambda i: (jnp.minimum(ND * i + ND, R // 8 - 1), 0))
    return pl.pallas_call(
        dense_kernel, grid=(R // n,), out_shape=[sds((R, C)), keep((T, W))], in_specs=[SM, VM, main, main, prev, prev, succ, succ], out_specs=[main, VM],
        scratch_shapes=[pltpu.VMEM((C // W, n + 16, W), F32), pltpu.VMEM((C // W, n, W), F32)],
        compiler_params=PARAMS, name="dense")(slot, q, rhs, sigma, rhs, sigma, rhs, sigma)


def cols_kernel(xl, sl, xr, sr, hup, hdn, right_out, left_out, buf):
    buf[0:OFF] = jnp.zeros((OFF, W), F32)
    buf[OFF + R:FC] = jnp.zeros((FC - OFF - R, W), F32)
    for out, x, s, c0, lane in ((right_out, xr, sr, C - W, W - 8), (left_out, xl, sl, 0, 0)):
        cols = slice(c0, c0 + W)
        for k, src in ((0, x), (2, s)):
            buf[OFF - 2:OFF] = hup[k:k + 2, cols]
            buf[OFF:OFF + R] = src[...]
            buf[OFF + R:OFF + R + 2] = hdn[k:k + 2, cols]
            for c in range(FC // W):
                out[4 * k:4 * k + 8, c * W:(c + 1) * W] = buf[c * W:(c + 1) * W].T[lane:lane + 8]


def edge_cols(rhs, sigma, hup, hdn):
    left = pl.BlockSpec((R, W), lambda i: (0, 0))
    right = pl.BlockSpec((R, W), lambda i: (0, C // W - 1))
    rows = pl.BlockSpec((4, C), lambda i: (0, 0))
    out = pl.BlockSpec((16, FC), lambda i: (0, 0))
    return pl.pallas_call(cols_kernel, grid=(1,), out_shape=[sds((16, FC))] * 2, in_specs=[left, left, right, right, rows, rows], out_specs=[out, out],
                          scratch_shapes=[pltpu.VMEM((FC, W), F32)], compiler_params=PARAMS, name="cols")(rhs, sigma, rhs, sigma, hup, hdn)


def rim_kernel(has_ref, run_ref, slot_ref, rhs, sigma, hup, hdn, hcl, hcr, cnt, strips_out, rows_out, tiles_out, slots_ref,
               r_out, strips, rows_buf, tiles, sems, ins, xl, sl, xr, sr, xt, st, xb, sb, X, D, G, S, H, D2, G2, S2):
    wide, low, high = slice(C - 2 * W, C), slice(0, 16), slice(R - 16, R)
    loads = [
        pltpu.make_async_copy(src.at[where], dst, ins.at[k])
        for k, (src, where, dst) in enumerate((
            (rhs, (slice(None), slice(0, 2 * W)), xl), (sigma, (slice(None), slice(0, 2 * W)), sl),
            (rhs, (slice(None), wide), xr), (sigma, (slice(None), wide), sr),
            (rhs, (low, slice(None)), xt), (sigma, (low, slice(None)), st), (rhs, (high, slice(None)), xb), (sigma, (high, slice(None)), sb)))
    ]
    for c in loads:
        c.start()
    slots_ref[...] = jnp.zeros_like(slots_ref)
    up, down, left, right = (has_ref[k] for k in range(4))
    lane = lax.broadcasted_iota(jnp.int32, (1, W), 1)

    def stencil(x, d, above, under, side):
        return d * (K1 * x + K2 * ((above + under) + side))

    def strip(x, s, c0, hc, m, a, alive, base):
        q = 1 - m
        sel = (lane == a) | (lane == a + 1)
        pad = jnp.zeros((W - 8, W), F32)
        for n in (0, 1):
            for c in range(FC // W):
                got = hc[8 * n:8 * n + 8, c * W:(c + 1) * W]
                H[n, c * W:(c + 1) * W] = jnp.concatenate([got, pad] if a == 0 else [pad, got], axis=0).T
        for c in (0, 1):
            cols = slice(c0 + c * W, c0 + (c + 1) * W)
            for rows, xv, sv in ((slice(OFF - 2, OFF), hup[0:2, cols], hup[2:4, cols]),
                                 (slice(OFF + R, OFF + R + 2), hdn[0:2, cols], hdn[2:4, cols]),
                                 (slice(OFF, OFF + R), x[:, c * W:(c + 1) * W], s[:, c * W:(c + 1) * W])):
                if c == m:
                    xv = jnp.where(sel, H[0, rows], xv)
                    sv = jnp.where(sel, H[1, rows], sv)
                dinv = 1.0 / (4.0 + sv)
                D[c, rows] = dinv
                X[c, rows] = xv
                G[c, rows] = dinv * xv
        live = ~sel | (alive > 0)

        def second(r0, n, ok):
            rows = slice(r0, r0 + n)
            side = sides([G[0, rows], G[1, rows]])
            for c in (0, 1):
                v = stencil(X[c, rows], D[c, rows], G[c, r0 - 1:r0 + n - 1], G[c, r0 + 1:r0 + n + 1], side[c])
                keep = live if c == m else None
                if ok is not None:
                    keep = ok if keep is None else keep & ok
                S[c, rows] = v if keep is None else jnp.where(keep, v, 0.0)

        second(OFF - 1, 1, up > 0)
        second(OFF + R, 1, down > 0)
        for k in range(R // 8):
            second(OFF + 8 * k, 8, None)
        for k in range(R // 8):
            r0 = OFF + 8 * k
            rows = slice(r0, r0 + 8)
            side = sides([S[0, rows], S[1, rows]])[q]
            v = S[q, rows]
            own = slice(8 * k, 8 * k + 8)
            t = 4.0 + s[own, q * W:(q + 1) * W]
            res = X[q, rows] - (t * v - ((S[q, r0 - 1:r0 + 7] + S[q, r0 + 1:r0 + 9]) + side))
            at = slice(base + 8 * k, base + 8 * k + 8)
            r_out[at] = res
            strips[0, at] = v
            strips[1, at] = cnt[at] * res

    loads[0].wait()
    loads[1].wait()
    strip(xl, sl, 0, hcl, 1, W - 2, left, 0)
    loads[2].wait()
    loads[3].wait()
    strip(xr, sr, C - 2 * W, hcr, 0, 0, right, R)
    for c in loads[4:]:
        c.wait()
    copies = [pltpu.make_async_copy(strips, strips_out, sems.at[0]), pltpu.make_async_copy(rows_buf, rows_out, sems.at[1])]
    copies[0].start()

    def edge(x, s, halo, h, g, o, alive, part, line, base):
        nt = C // W
        tiles = [slice(c * W, (c + 1) * W) for c in range(nt)]
        ok = alive > 0
        for c, cols in enumerate(tiles):
            dinv = 1.0 / (4.0 + s[:, cols])
            D2[c, 8:24] = dinv
            G2[c, 8:24] = dinv * x[:, cols]
            dinv = 1.0 / (4.0 + halo[2:4, cols])
            D2[c, h:h + 2] = dinv
            G2[c, h:h + 2] = dinv * halo[0:2, cols]
        side = sides([G2[c, g:g + 8] for c in range(nt)])
        outer = sides([G2[c, o:o + 1] for c in range(nt)])
        near = halo[1:2, :] if o < g else halo[0:1, :]
        for c, cols in enumerate(tiles):
            S2[c, g:g + 8] = stencil(x[g - 8:g, cols], D2[c, g:g + 8], G2[c, g - 1:g + 7], G2[c, g + 1:g + 9], side[c])
            v = stencil(near[:, cols], D2[c, o:o + 1], G2[c, o - 1:o], G2[c, o + 1:o + 2], outer[c])
            S2[c, o:o + 1] = jnp.where(ok, v, 0.0)
        side = sides([S2[c, g:g + 8] for c in range(nt)])
        for c, cols in enumerate(tiles):
            v = S2[c, g:g + 8]
            rows_buf[part, :, cols] = v
            at = g + line
            one = slice(at, at + 1)
            t = 4.0 + s[at - 8:at - 7, cols]
            res = x[at - 8:at - 7, cols] - (t * S2[c, one] - ((S2[c, at - 1:at] + S2[c, at + 1:at + 2]) + side[c][line:line + 1]))
            r_out[base + c:base + c + 1] = res
            rows_buf[2, part:part + 1, cols] = cnt[base + c:base + c + 1] * res

    edge(xt, st, hup, 6, 8, 7, up, 0, 0, 2 * R)
    edge(xb, sb, hdn, 24, 16, 24, down, 1, 7, 2 * R + 16)
    copies[1].start()

    def body(b, carry):
        for u in range(16):
            t = b * 16 + u
            row = r_out[pl.ds(run_ref[t], 1), :]
            tiles[pl.ds(t, 1), :] = row
            slots_ref[pl.ds(slot_ref[t], 1), :] = row
        return carry

    for k in range(4):
        lax.fori_loop(k * T // 64, (k + 1) * T // 64, body, 0)
        part = pl.ds(k * T // 4, T // 4)
        copies.append(pltpu.make_async_copy(tiles.at[part], tiles_out.at[part], sems.at[2 + k]))
        copies[-1].start()
    for c in copies:
        c.wait()


def rim(has, run, slot, rhs, sigma, hup, hdn, hcl, hcr, cnt):
    strips, rows, tiles = (2, 2 * R, W), (3, 8, C), (T, W)
    return pl.pallas_call(
        rim_kernel, out_shape=[pltpu.HBM(strips, F32), pltpu.HBM(rows, F32), pltpu.HBM(tiles, F32), keep((2 * NG * CAP, W))],
        in_specs=[SM, SM, SM, ANY, ANY, VM, VM, VM, VM, VM],
        out_specs=[ANY, ANY, ANY, VM],
        scratch_shapes=[pltpu.VMEM((RIM, W), F32), pltpu.VMEM(strips, F32), pltpu.VMEM(rows, F32), pltpu.VMEM(tiles, F32), pltpu.SemaphoreType.DMA((6,)),
                        pltpu.SemaphoreType.DMA((8,))]
        + [pltpu.VMEM((R, 2 * W), F32)] * 4 + [pltpu.VMEM((16, C), F32)] * 4 + [pltpu.VMEM((2, FR, W), F32)] * 4 + [pltpu.VMEM((2, FC, W), F32)] + [pltpu.VMEM((C // W, 32, W), F32)] * 3,
        compiler_params=PARAMS, name="rim")(has, run, slot, rhs, sigma, hup, hdn, in_vmem(hcl), in_vmem(hcr), in_vmem(cnt))


def product_kernel(first, slots_ref, blk_ref, *refs):
    if first:
        q_ref, sums_ref, _ = refs
    else:
        prev_ref, q_ref, sums_ref = refs
    i = lax.broadcasted_iota(jnp.int32, (64, W), 0)
    j = lax.broadcasted_iota(jnp.int32, (64, W), 1)
    d = j - i
    band = jnp.where((d >= 0) & (d < 64), 1.0, 0.0)
    mask_top = jnp.where(d == 0, 0.5, band).astype(BF16)
    mask_bot = jnp.where(d == 64, 0.5, 1.0 - band).astype(BF16)

    def fold(v):
        return jnp.sum(v.reshape(CAP // 8, 8, W), axis=0)

    scale = 1.0 if first else prev_ref[3, 0:1, :]

    def body(g, carry):
        rr, pq, vv, ra, qa = carry
        rows = pl.ds(pl.multiple_of(g * CAP, CAP), CAP)
        r = slots_ref[rows, :]
        half = r.astype(BF16)
        b = blk_ref[g, 0:64, :]
        u = jnp.concatenate([b * mask_top, b * mask_bot], axis=0)
        cross = blk_ref[g, 64:72, :].astype(F32)
        swapped = pltpu.roll(half.astype(F32), 64, axis=1)
        q = jnp.dot(half, u, preferred_element_type=F32)
        q = q + lax.dot_general(half, u, (((1,), (1,)), ((), ())), preferred_element_type=F32)
        q = q + (swapped.reshape(CAP // 8, 8, W) * cross[None]).reshape(CAP, W)
        q = q.astype(BF16).astype(F32)
        q_ref[rows, :] = q
        rr = rr + fold(r * r)
        pq = pq + fold(r * q)
        if first:
            ra = ra + fold(jnp.abs(r))
            qa = qa + fold(jnp.abs(q))
        else:
            v = q * scale
            vv = vv + fold(v * v)
        return rr, pq, vv, ra, qa

    zero = jnp.zeros((8, W), F32)
    rr, pq, vv, ra, qa = lax.fori_loop(0, NG, body, (zero,) * 5, unroll=8)
    if first:
        ra, qa = jnp.sum(ra), jnp.sum(qa)
        ok = (qa > 0.0) & (ra > 0.0)
        a0 = jnp.full((1, W), jnp.where(ok, ra, 1.0)) / jnp.full((1, W), jnp.where(ok, qa, 1.0))

        def second_pass(k, acc):
            v = q_ref[pl.ds(pl.multiple_of(k * 64, 64), 64), :] * a0
            return acc + jnp.sum((v * v).reshape(8, 8, W), axis=0)

        vv = lax.fori_loop(0, NG * CAP // 64, second_pass, zero, unroll=8)
        sums_ref[0], sums_ref[1], sums_ref[2] = rr, pq, vv
        sums_ref[3] = jnp.broadcast_to(a0, (8, W))
    else:
        rows = [jnp.sum(v + prev_ref[k], axis=0, keepdims=True) for k, v in enumerate((rr, pq, vv))]
        full = jnp.concatenate(rows + [scale], axis=0)
        for k in range(2 * NG):
            sums_ref[k] = full


def product_first(slots, blocks):
    def kernel(s, b, q, sums):
        here = q.at[0:NG * CAP]
        product_kernel(True, here, b, here, sums, None)

    return pl.pallas_call(kernel, out_shape=[keep((2 * NG * CAP, W)), keep((4, 8, W))], in_specs=[VM, VM], out_specs=[VM, VM], input_output_aliases={0: 0},
                          compiler_params=PARAMS, name="product_a")(slots, in_vmem(blocks))


def product_second(slots, blocks, prev):
    def kernel(s, b, p, q, sums):
        here = q.at[NG * CAP:2 * NG * CAP]
        product_kernel(False, here, b, p, here, sums)

    return pl.pallas_call(kernel, out_shape=[keep((2 * NG * CAP, W)), keep((2 * NG, 4, W))], input_output_aliases={0: 0},
                          in_specs=[VM, VM, VM], out_specs=[VM, VM], compiler_params=PARAMS, name="product_b")(slots, in_vmem(blocks), prev)


CH = 4
TC = T // CH


def final_kernel(red_ref, r_hbm, q_ref, strips_ref, rows_ref, field_ref, out_ref, res_hbm, dir_hbm, r_buf, res_buf, dir_buf, strips, rows, ins, outs):
    inner = slice(W, C - W)
    parts = [slice(k * TC, (k + 1) * TC) for k in range(CH)]
    tiles_in = [pltpu.make_async_copy(r_hbm.at[p], r_buf.at[p], ins.at[k]) for k, p in enumerate(parts)]
    rim_in = [pltpu.make_async_copy(strips_ref, strips, ins.at[CH]), pltpu.make_async_copy(rows_ref, rows, ins.at[CH + 1])]
    for c in tiles_in + rim_in:
        c.start()
    rr = jnp.sum(red_ref[:, 0, :])
    pq = jnp.sum(red_ref[:, 1, :])
    alpha = jnp.full((1, W), rr) / jnp.full((1, W), pq)
    t = alpha / red_ref[:, 3, :]
    qq = jnp.sum(t * t * red_ref[:, 2, :])
    beta = (rr - 2.0 * alpha * pq + qq) / rr
    sent = []

    def send(src, dst):
        c = pltpu.make_async_copy(src, dst, outs.at[len(sent)])
        c.start()
        sent.append(c)

    def rim_out():
        for c in rim_in:
            c.wait()
        strips[0] = strips[0] + alpha * strips[1]
        send(strips.at[0, 0:R], out_ref.at[:, 0:W])
        send(strips.at[0, R:2 * R], out_ref.at[:, C - W:C])
        for k in range(C // W):
            lanes = slice(k * W, (k + 1) * W)
            rows[0, 0:1, lanes] = rows[0, 0:1, lanes] + alpha * rows[2, 0:1, lanes]
            rows[1, 7:8, lanes] = rows[1, 7:8, lanes] + alpha * rows[2, 1:2, lanes]
        send(rows.at[0, :, inner], out_ref.at[0:8, inner])
        send(rows.at[1, :, inner], out_ref.at[R - 8:R, inner])

    for k, p in enumerate(parts):
        tiles_in[k].wait()
        r = r_buf[p]
        res = r - alpha * q_ref[p]
        res_buf[p] = res
        dir_buf[p] = res + beta * r
        send(res_buf.at[p], res_hbm.at[p])
        send(dir_buf.at[p], dir_hbm.at[p])
        if k == 1:
            rim_out()
    for c in sent:
        c.wait()


def final(red, r_tiles, q_tiles, strips, rows, field):
    return pl.pallas_call(
        final_kernel, out_shape=[sds((R, C)), sds((T, W)), sds((T, W))],
        in_specs=[VM, ANY, VM, ANY, ANY, ANY], out_specs=[ANY, ANY, ANY],
        scratch_shapes=[pltpu.VMEM((T, W), F32)] * 3 + [pltpu.VMEM((2, 2 * R, W), F32), pltpu.VMEM((3, 8, C), F32),
                        pltpu.SemaphoreType.DMA((CH + 2,)), pltpu.SemaphoreType.DMA((2 * CH + 4,))],
        input_output_aliases={5: 0}, compiler_params=PARAMS, name="final")(in_vmem(red), in_hbm(r_tiles), q_tiles, in_hbm(strips), in_hbm(rows), field)


def step(rhs, sigma, tile_list, tile_owner, schur_blocks):
    core = lax.axis_index("c")
    big = (in_hbm(rhs), in_hbm(sigma))
    packed, *ready = lax.optimization_barrier((pack(schur_blocks), rhs, sigma))
    mine = lax.all_to_all(packed, CHIPS, 0, 0, tiled=True)
    nrow, ncol = 16, 8
    up = [(i, i + 1) for i in range(nrow - 1)]
    down = [(i + 1, i) for i in range(nrow - 1)]
    tail, head = jnp.concatenate([ready[0][-2:], ready[1][-2:]]), jnp.concatenate([ready[0][:2], ready[1][:2]])
    hup = lax.ppermute(tail, ROWS, up)
    hdn = lax.ppermute(head, ROWS, down)

    rightward = [(i, i + 1) for i in range(ncol - 1)]
    leftward = [(i + 1, i) for i in range(ncol - 1)]
    to_right, to_left, tile_list, tile_owner = lax.optimization_barrier((*edge_cols(*big, hup, hdn), tile_list, tile_owner))
    hcl = lax.ppermute(to_right, COLS, rightward)
    hcr = lax.ppermute(to_left, COLS, leftward)
    row_at = lax.axis_index(ROWS)
    col_at = lax.axis_index(COLS)
    has = jnp.stack([row_at > 0, row_at < nrow - 1, col_at > 0, col_at < ncol - 1]).astype(jnp.int32)
    runs = C // W
    trow, tcol = tile_list // runs, tile_list % runs
    run = jnp.where(tcol == 0, trow, jnp.where(tcol == runs - 1, R + trow, jnp.where(trow == 0, 2 * R + tcol, 2 * R + 16 + tcol)))
    owner = tile_owner[:, 0]
    onehot = (owner[:, None] == jnp.arange(2 * NG, dtype=jnp.int32)[None, :]).astype(jnp.int32)
    ranks = jnp.cumsum(onehot, axis=0) - onehot
    rank = jnp.sum(ranks * onehot, axis=1)
    slot = (((owner & 1) ^ core) * NG + (owner >> 1)) * CAP + rank
    hits = (jnp.arange(RIM, dtype=jnp.int32)[:, None] == run[None, :]).astype(BF16)
    cnt = jnp.dot(hits, jnp.ones((T, W), BF16), preferred_element_type=F32)
    strips, rows, r_tiles, slots = rim(has, run, slot, *big, hup, hdn, hcl, hcr, cnt)
    mine, slots = lax.optimization_barrier((mine, slots))
    theirs = lax.ppermute(mine, "c", [(0, 1), (1, 0)])
    q, part = product_first(slots, mine)
    q, sums = product_second(q, theirs, part)
    q, sums, late_rhs, late_sigma = lax.optimization_barrier((q, sums, rhs, sigma))
    red = lax.all_to_all(sums, ALL, 0, 0, tiled=True)
    field, q_tiles = dense(slot, q, in_hbm(late_rhs), in_hbm(late_sigma))
    return tuple(final(red, r_tiles, q_tiles, strips, rows, field))


def solution(mesh):
    grid = Mesh(mesh.devices.reshape(4, 4, 4, 2), ("y", "z", "x", "c"))
    in_specs = (P(ROWS, COLS), P(ROWS, COLS), P(ALL), P(ALL, None), P(ALL, None, None))
    out_specs = (P(ROWS, COLS), P(ALL, None), P(ALL, None))
    return jax.shard_map(step, mesh=grid, in_specs=in_specs, out_specs=out_specs, check_vma=False)
```

```python
import jax
import jax.numpy as jnp
from jax import lax
from jax.experimental import pallas as pl
from jax.experimental.pallas import tpu as pltpu
from jax.sharding import Mesh, PartitionSpec as P

F32 = jnp.float32
BF16 = jnp.bfloat16
R, C, W = 768, 2048, 128
T = 2048
CAP = 32
NG = 64
RIM = 2 * R + 32
PR = 72
OFF = 16
FR = R + 2 * OFF
FC = 896
ROWS = ("y", "z")
COLS = ("x", "c")
ALL = ("y", "z", "x", "c")
CHIPS = ("y", "z", "x")
VM = pl.BlockSpec(memory_space=pltpu.VMEM)
SM = pl.BlockSpec(memory_space=pltpu.SMEM)
ANY = pl.BlockSpec(memory_space=pl.ANY)
C1 = 0.6111111
K1 = C1 + 2.75 * (1.0 - C1)
K2 = 2.75 * C1
PARAMS = pltpu.CompilerParams(vmem_limit_bytes=20 << 20)


def sds(shape, dtype=F32):
    return jax.ShapeDtypeStruct(shape, dtype)


def keep(shape, dtype=F32):
    return pltpu.VMEM(shape, dtype)


def in_hbm(x):
    return pltpu.with_memory_space_constraint(x, pltpu.HBM)


def in_vmem(x):
    return pltpu.with_memory_space_constraint(x, pltpu.VMEM)


def pack_kernel(s_ref, out_ref):
    s = s_ref[0].astype(F32)
    top, bot = s[:64], s[64:]
    i = lax.broadcasted_iota(jnp.int32, (64, W), 0)
    j = lax.broadcasted_iota(jnp.int32, (64, W), 1)
    d = j - i
    body = jnp.where((d >= 0) & (d < 64), top, bot)
    cross = jnp.where(d == 64, top, 0.0)
    half = jnp.sum(cross, axis=0, keepdims=True)
    row = half + pltpu.roll(half, 64, axis=1)
    full = jnp.concatenate([body, jnp.broadcast_to(row, (8, W))], axis=0).astype(BF16)
    for k in range(NG):
        out_ref[k] = full


def pack(blocks):
    return pl.pallas_call(pack_kernel, out_shape=sds((NG, PR, W), BF16), in_specs=[VM], out_specs=VM, compiler_params=PARAMS, name="pack")(blocks)


def sides(tiles):
    lane = lax.broadcasted_iota(jnp.int32, (1, W), 1)
    n = len(tiles)
    prev = [pltpu.roll(t, 1, axis=1) for t in tiles]
    succ = [pltpu.roll(t, W - 1, axis=1) for t in tiles]
    return [jnp.where(lane == 0, prev[c - 1], prev[c]) + jnp.where(lane == W - 1, succ[(c + 1) % n], succ[c]) for c in range(n)]


NC = 8
NR = R // NC


def dense_kernel(slot_ref, q_ref, x_hbm, s_hbm, out_hbm, tiles_ref, x, s, g, ins, outs):
    nt = C // W
    tiles = [slice(c * W, (c + 1) * W) for c in range(nt)]
    chunks = [slice(k * NR, (k + 1) * NR) for k in range(NC)]
    loads = [[pltpu.make_async_copy(src.at[p], dst.at[p], ins.at[n, k]) for n, (src, dst) in enumerate(((x_hbm, x), (s_hbm, s)))]
             for k, p in enumerate(chunks)]
    for pair in loads:
        for c in pair:
            c.start()

    def body(b, carry):
        for u in range(16):
            t = b * 16 + u
            tiles_ref[pl.ds(t, 1), :] = q_ref[pl.ds(slot_ref[t], 1), :]
        return carry

    lax.fori_loop(0, T // 16, body, 0)
    for c in range(nt):
        g[c, 0:8] = jnp.zeros((8, W), F32)
        g[c, R + 8:R + 16] = jnp.zeros((8, W), F32)

    def first(k):
        for c in loads[k]:
            c.wait()
        p = chunks[k]
        for c, lanes in enumerate(tiles):
            dinv = 1.0 / (4.0 + s[p, lanes])
            s[p, lanes] = dinv
            g[c, 8 + k * NR:8 + (k + 1) * NR] = dinv * x[p, lanes]

    def second(k):
        for j in range(k * NR // 8, (k + 1) * NR // 8):
            rows = slice(8 * j, 8 * j + 8)
            side = sides([g[c, 8 * j + 8:8 * j + 16] for c in range(nt)])
            for c, lanes in enumerate(tiles):
                beside = (g[c, 8 * j + 7:8 * j + 15] + g[c, 8 * j + 9:8 * j + 17]) + side[c]
                x[rows, lanes] = s[rows, lanes] * (K1 * x[rows, lanes] + K2 * beside)
        c = pltpu.make_async_copy(x.at[chunks[k]], out_hbm.at[chunks[k]], outs.at[k])
        c.start()
        return c

    sent = []
    for k in range(NC):
        first(k)
        if k:
            sent.append(second(k - 1))
    sent.append(second(NC - 1))
    for c in sent:
        c.wait()


def dense(slot, q, rhs, sigma):
    return pl.pallas_call(
        dense_kernel, out_shape=[sds((R, C)), keep((T, W))], in_specs=[SM, VM, ANY, ANY], out_specs=[ANY, VM],
        scratch_shapes=[pltpu.VMEM((R, C), F32), pltpu.VMEM((R, C), F32), pltpu.VMEM((C // W, R + 16, W), F32),
                        pltpu.SemaphoreType.DMA((2, NC)), pltpu.SemaphoreType.DMA((NC,))],
        compiler_params=pltpu.CompilerParams(vmem_limit_bytes=32 << 20), name="dense")(slot, q, rhs, sigma)


def cols_kernel(xl, sl, xr, sr, hup, hdn, right_out, left_out, buf):
    buf[0:OFF] = jnp.zeros((OFF, W), F32)
    buf[OFF + R:FC] = jnp.zeros((FC - OFF - R, W), F32)
    for out, x, s, c0, lane in ((right_out, xr, sr, C - W, W - 8), (left_out, xl, sl, 0, 0)):
        cols = slice(c0, c0 + W)
        for k, src in ((0, x), (2, s)):
            buf[OFF - 2:OFF] = hup[k:k + 2, cols]
            buf[OFF:OFF + R] = src[...]
            buf[OFF + R:OFF + R + 2] = hdn[k:k + 2, cols]
            for c in range(FC // W):
                out[4 * k:4 * k + 8, c * W:(c + 1) * W] = buf[c * W:(c + 1) * W].T[lane:lane + 8]


def edge_cols(rhs, sigma, hup, hdn):
    left = pl.BlockSpec((R, W), lambda i: (0, 0))
    right = pl.BlockSpec((R, W), lambda i: (0, C // W - 1))
    rows = pl.BlockSpec((4, C), lambda i: (0, 0))
    out = pl.BlockSpec((16, FC), lambda i: (0, 0))
    return pl.pallas_call(cols_kernel, grid=(1,), out_shape=[sds((16, FC))] * 2, in_specs=[left, left, right, right, rows, rows], out_specs=[out, out],
                          scratch_shapes=[pltpu.VMEM((FC, W), F32)], compiler_params=PARAMS, name="cols")(rhs, sigma, rhs, sigma, hup, hdn)


def rim_kernel(has_ref, run_ref, slot_ref, rhs, sigma, hup, hdn, hcl, hcr, cnt, strips_out, rows_out, tiles_out, slots_ref,
               r_out, strips, rows_buf, tiles, sems, ins, xl, sl, xr, sr, xt, st, xb, sb, X, D, G, S, H, D2, G2, S2):
    wide, low, high = slice(C - 2 * W, C), slice(0, 16), slice(R - 16, R)
    loads = [
        pltpu.make_async_copy(src.at[where], dst, ins.at[k])
        for k, (src, where, dst) in enumerate((
            (rhs, (slice(None), slice(0, 2 * W)), xl), (sigma, (slice(None), slice(0, 2 * W)), sl),
            (rhs, (slice(None), wide), xr), (sigma, (slice(None), wide), sr),
            (rhs, (low, slice(None)), xt), (sigma, (low, slice(None)), st), (rhs, (high, slice(None)), xb), (sigma, (high, slice(None)), sb)))
    ]
    for c in loads:
        c.start()
    slots_ref[...] = jnp.zeros_like(slots_ref)
    up, down, left, right = (has_ref[k] for k in range(4))
    lane = lax.broadcasted_iota(jnp.int32, (1, W), 1)

    def stencil(x, d, above, under, side):
        return d * (K1 * x + K2 * ((above + under) + side))

    def strip(x, s, c0, hc, m, a, alive, base):
        q = 1 - m
        sel = (lane == a) | (lane == a + 1)
        pad = jnp.zeros((W - 8, W), F32)
        for n in (0, 1):
            for c in range(FC // W):
                got = hc[8 * n:8 * n + 8, c * W:(c + 1) * W]
                H[n, c * W:(c + 1) * W] = jnp.concatenate([got, pad] if a == 0 else [pad, got], axis=0).T
        for c in (0, 1):
            cols = slice(c0 + c * W, c0 + (c + 1) * W)
            for rows, xv, sv in ((slice(OFF - 2, OFF), hup[0:2, cols], hup[2:4, cols]),
                                 (slice(OFF + R, OFF + R + 2), hdn[0:2, cols], hdn[2:4, cols]),
                                 (slice(OFF, OFF + R), x[:, c * W:(c + 1) * W], s[:, c * W:(c + 1) * W])):
                if c == m:
                    xv = jnp.where(sel, H[0, rows], xv)
                    sv = jnp.where(sel, H[1, rows], sv)
                dinv = 1.0 / (4.0 + sv)
                D[c, rows] = dinv
                X[c, rows] = xv
                G[c, rows] = dinv * xv
        live = ~sel | (alive > 0)

        def second(r0, n, ok):
            rows = slice(r0, r0 + n)
            side = sides([G[0, rows], G[1, rows]])
            for c in (0, 1):
                v = stencil(X[c, rows], D[c, rows], G[c, r0 - 1:r0 + n - 1], G[c, r0 + 1:r0 + n + 1], side[c])
                keep = live if c == m else None
                if ok is not None:
                    keep = ok if keep is None else keep & ok
                S[c, rows] = v if keep is None else jnp.where(keep, v, 0.0)

        second(OFF - 1, 1, up > 0)
        second(OFF + R, 1, down > 0)
        for k in range(R // 8):
            second(OFF + 8 * k, 8, None)
        for k in range(R // 8):
            r0 = OFF + 8 * k
            rows = slice(r0, r0 + 8)
            side = sides([S[0, rows], S[1, rows]])[q]
            v = S[q, rows]
            own = slice(8 * k, 8 * k + 8)
            t = 4.0 + s[own, q * W:(q + 1) * W]
            res = X[q, rows] - (t * v - ((S[q, r0 - 1:r0 + 7] + S[q, r0 + 1:r0 + 9]) + side))
            at = slice(base + 8 * k, base + 8 * k + 8)
            r_out[at] = res
            strips[0, at] = v
            strips[1, at] = cnt[at] * res

    loads[0].wait()
    loads[1].wait()
    strip(xl, sl, 0, hcl, 1, W - 2, left, 0)
    loads[2].wait()
    loads[3].wait()
    strip(xr, sr, C - 2 * W, hcr, 0, 0, right, R)
    for c in loads[4:]:
        c.wait()
    copies = [pltpu.make_async_copy(strips, strips_out, sems.at[0]), pltpu.make_async_copy(rows_buf, rows_out, sems.at[1])]
    copies[0].start()

    def edge(x, s, halo, h, g, o, alive, part, line, base):
        nt = C // W
        tiles = [slice(c * W, (c + 1) * W) for c in range(nt)]
        ok = alive > 0
        for c, cols in enumerate(tiles):
            dinv = 1.0 / (4.0 + s[:, cols])
            D2[c, 8:24] = dinv
            G2[c, 8:24] = dinv * x[:, cols]
            dinv = 1.0 / (4.0 + halo[2:4, cols])
            D2[c, h:h + 2] = dinv
            G2[c, h:h + 2] = dinv * halo[0:2, cols]
        side = sides([G2[c, g:g + 8] for c in range(nt)])
        outer = sides([G2[c, o:o + 1] for c in range(nt)])
        near = halo[1:2, :] if o < g else halo[0:1, :]
        for c, cols in enumerate(tiles):
            S2[c, g:g + 8] = stencil(x[g - 8:g, cols], D2[c, g:g + 8], G2[c, g - 1:g + 7], G2[c, g + 1:g + 9], side[c])
            v = stencil(near[:, cols], D2[c, o:o + 1], G2[c, o - 1:o], G2[c, o + 1:o + 2], outer[c])
            S2[c, o:o + 1] = jnp.where(ok, v, 0.0)
        side = sides([S2[c, g:g + 8] for c in range(nt)])
        for c, cols in enumerate(tiles):
            v = S2[c, g:g + 8]
            rows_buf[part, :, cols] = v
            at = g + line
            one = slice(at, at + 1)
            t = 4.0 + s[at - 8:at - 7, cols]
            res = x[at - 8:at - 7, cols] - (t * S2[c, one] - ((S2[c, at - 1:at] + S2[c, at + 1:at + 2]) + side[c][line:line + 1]))
            r_out[base + c:base + c + 1] = res
            rows_buf[2, part:part + 1, cols] = cnt[base + c:base + c + 1] * res

    edge(xt, st, hup, 6, 8, 7, up, 0, 0, 2 * R)
    edge(xb, sb, hdn, 24, 16, 24, down, 1, 7, 2 * R + 16)
    copies[1].start()

    def body(b, carry):
        for u in range(16):
            t = b * 16 + u
            row = r_out[pl.ds(run_ref[t], 1), :]
            tiles[pl.ds(t, 1), :] = row
            slots_ref[pl.ds(slot_ref[t], 1), :] = row
        return carry

    for k in range(4):
        lax.fori_loop(k * T // 64, (k + 1) * T // 64, body, 0)
        part = pl.ds(k * T // 4, T // 4)
        copies.append(pltpu.make_async_copy(tiles.at[part], tiles_out.at[part], sems.at[2 + k]))
        copies[-1].start()
    for c in copies:
        c.wait()


def rim(has, run, slot, rhs, sigma, hup, hdn, hcl, hcr, cnt):
    strips, rows, tiles = (2, 2 * R, W), (3, 8, C), (T, W)
    return pl.pallas_call(
        rim_kernel, out_shape=[pltpu.HBM(strips, F32), pltpu.HBM(rows, F32), pltpu.HBM(tiles, F32), keep((2 * NG * CAP, W))],
        in_specs=[SM, SM, SM, ANY, ANY, VM, VM, VM, VM, VM],
        out_specs=[ANY, ANY, ANY, VM],
        scratch_shapes=[pltpu.VMEM((RIM, W), F32), pltpu.VMEM(strips, F32), pltpu.VMEM(rows, F32), pltpu.VMEM(tiles, F32), pltpu.SemaphoreType.DMA((6,)),
                        pltpu.SemaphoreType.DMA((8,))]
        + [pltpu.VMEM((R, 2 * W), F32)] * 4 + [pltpu.VMEM((16, C), F32)] * 4 + [pltpu.VMEM((2, FR, W), F32)] * 4 + [pltpu.VMEM((2, FC, W), F32)] + [pltpu.VMEM((C // W, 32, W), F32)] * 3,
        compiler_params=PARAMS, name="rim")(has, run, slot, rhs, sigma, hup, hdn, in_vmem(hcl), in_vmem(hcr), in_vmem(cnt))


def product_kernel(first, slots_ref, blk_ref, *refs):
    if first:
        q_ref, sums_ref, _ = refs
    else:
        prev_ref, q_ref, sums_ref = refs
    i = lax.broadcasted_iota(jnp.int32, (64, W), 0)
    j = lax.broadcasted_iota(jnp.int32, (64, W), 1)
    d = j - i
    band = jnp.where((d >= 0) & (d < 64), 1.0, 0.0)
    mask_top = jnp.where(d == 0, 0.5, band).astype(BF16)
    mask_bot = jnp.where(d == 64, 0.5, 1.0 - band).astype(BF16)

    def fold(v):
        return jnp.sum(v.reshape(CAP // 8, 8, W), axis=0)

    scale = 1.0 if first else prev_ref[3, 0:1, :]

    def body(g, carry):
        rr, pq, vv, ra, qa = carry
        rows = pl.ds(pl.multiple_of(g * CAP, CAP), CAP)
        r = slots_ref[rows, :]
        half = r.astype(BF16)
        b = blk_ref[g, 0:64, :]
        u = jnp.concatenate([b * mask_top, b * mask_bot], axis=0)
        cross = blk_ref[g, 64:72, :].astype(F32)
        swapped = pltpu.roll(half.astype(F32), 64, axis=1)
        q = jnp.dot(half, u, preferred_element_type=F32)
        q = q + lax.dot_general(half, u, (((1,), (1,)), ((), ())), preferred_element_type=F32)
        q = q + (swapped.reshape(CAP // 8, 8, W) * cross[None]).reshape(CAP, W)
        q = q.astype(BF16).astype(F32)
        q_ref[rows, :] = q
        rr = rr + fold(r * r)
        pq = pq + fold(r * q)
        if first:
            ra = ra + fold(jnp.abs(r))
            qa = qa + fold(jnp.abs(q))
        else:
            v = q * scale
            vv = vv + fold(v * v)
        return rr, pq, vv, ra, qa

    zero = jnp.zeros((8, W), F32)
    rr, pq, vv, ra, qa = lax.fori_loop(0, NG, body, (zero,) * 5, unroll=8)
    if first:
        ra, qa = jnp.sum(ra), jnp.sum(qa)
        ok = (qa > 0.0) & (ra > 0.0)
        a0 = jnp.full((1, W), jnp.where(ok, ra, 1.0)) / jnp.full((1, W), jnp.where(ok, qa, 1.0))

        def second_pass(k, acc):
            v = q_ref[pl.ds(pl.multiple_of(k * 64, 64), 64), :] * a0
            return acc + jnp.sum((v * v).reshape(8, 8, W), axis=0)

        vv = lax.fori_loop(0, NG * CAP // 64, second_pass, zero, unroll=8)
        sums_ref[0], sums_ref[1], sums_ref[2] = rr, pq, vv
        sums_ref[3] = jnp.broadcast_to(a0, (8, W))
    else:
        rows = [jnp.sum(v + prev_ref[k], axis=0, keepdims=True) for k, v in enumerate((rr, pq, vv))]
        full = jnp.concatenate(rows + [scale], axis=0)
        for k in range(2 * NG):
            sums_ref[k] = full


def product_first(slots, blocks):
    def kernel(s, b, q, sums):
        here = q.at[0:NG * CAP]
        product_kernel(True, here, b, here, sums, None)

    return pl.pallas_call(kernel, out_shape=[keep((2 * NG * CAP, W)), keep((4, 8, W))], in_specs=[VM, VM], out_specs=[VM, VM], input_output_aliases={0: 0},
                          compiler_params=PARAMS, name="product_a")(slots, in_vmem(blocks))


def product_second(slots, blocks, prev):
    def kernel(s, b, p, q, sums):
        here = q.at[NG * CAP:2 * NG * CAP]
        product_kernel(False, here, b, p, here, sums)

    return pl.pallas_call(kernel, out_shape=[keep((2 * NG * CAP, W)), keep((2 * NG, 4, W))], input_output_aliases={0: 0},
                          in_specs=[VM, VM, VM], out_specs=[VM, VM], compiler_params=PARAMS, name="product_b")(slots, in_vmem(blocks), prev)


CH = 4
TC = T // CH


def final_kernel(red_ref, r_hbm, q_ref, strips_ref, rows_ref, field_ref, out_ref, res_hbm, dir_hbm, r_buf, res_buf, dir_buf, strips, rows, ins, outs):
    inner = slice(W, C - W)
    parts = [slice(k * TC, (k + 1) * TC) for k in range(CH)]
    tiles_in = [pltpu.make_async_copy(r_hbm.at[p], r_buf.at[p], ins.at[k]) for k, p in enumerate(parts)]
    rim_in = [pltpu.make_async_copy(strips_ref, strips, ins.at[CH]), pltpu.make_async_copy(rows_ref, rows, ins.at[CH + 1])]
    for c in tiles_in + rim_in:
        c.start()
    rr = jnp.sum(red_ref[:, 0, :])
    pq = jnp.sum(red_ref[:, 1, :])
    alpha = jnp.full((1, W), rr) / jnp.full((1, W), pq)
    t = alpha / red_ref[:, 3, :]
    qq = jnp.sum(t * t * red_ref[:, 2, :])
    beta = (rr - 2.0 * alpha * pq + qq) / rr
    sent = []

    def send(src, dst):
        c = pltpu.make_async_copy(src, dst, outs.at[len(sent)])
        c.start()
        sent.append(c)

    def rim_out():
        for c in rim_in:
            c.wait()
        strips[0] = strips[0] + alpha * strips[1]
        send(strips.at[0, 0:R], out_ref.at[:, 0:W])
        send(strips.at[0, R:2 * R], out_ref.at[:, C - W:C])
        for k in range(C // W):
            lanes = slice(k * W, (k + 1) * W)
            rows[0, 0:1, lanes] = rows[0, 0:1, lanes] + alpha * rows[2, 0:1, lanes]
            rows[1, 7:8, lanes] = rows[1, 7:8, lanes] + alpha * rows[2, 1:2, lanes]
        send(rows.at[0, :, inner], out_ref.at[0:8, inner])
        send(rows.at[1, :, inner], out_ref.at[R - 8:R, inner])

    for k, p in enumerate(parts):
        tiles_in[k].wait()
        r = r_buf[p]
        res = r - alpha * q_ref[p]
        res_buf[p] = res
        dir_buf[p] = res + beta * r
        send(res_buf.at[p], res_hbm.at[p])
        send(dir_buf.at[p], dir_hbm.at[p])
        if k == 1:
            rim_out()
    for c in sent:
        c.wait()


def final(red, r_tiles, q_tiles, strips, rows, field):
    return pl.pallas_call(
        final_kernel, out_shape=[sds((R, C)), sds((T, W)), sds((T, W))],
        in_specs=[VM, ANY, VM, ANY, ANY, ANY], out_specs=[ANY, ANY, ANY],
        scratch_shapes=[pltpu.VMEM((T, W), F32)] * 3 + [pltpu.VMEM((2, 2 * R, W), F32), pltpu.VMEM((3, 8, C), F32),
                        pltpu.SemaphoreType.DMA((CH + 2,)), pltpu.SemaphoreType.DMA((2 * CH + 4,))],
        input_output_aliases={5: 0}, compiler_params=PARAMS, name="final")(in_vmem(red), in_hbm(r_tiles), q_tiles, in_hbm(strips), in_hbm(rows), field)


def step(rhs, sigma, tile_list, tile_owner, schur_blocks):
    core = lax.axis_index("c")
    big = (in_hbm(rhs), in_hbm(sigma))
    packed, *ready = lax.optimization_barrier((pack(schur_blocks), rhs, sigma))
    mine = lax.all_to_all(packed, CHIPS, 0, 0, tiled=True)
    nrow, ncol = 16, 8
    up = [(i, i + 1) for i in range(nrow - 1)]
    down = [(i + 1, i) for i in range(nrow - 1)]
    tail, head = jnp.concatenate([ready[0][-2:], ready[1][-2:]]), jnp.concatenate([ready[0][:2], ready[1][:2]])
    hup = lax.ppermute(tail, ROWS, up)
    hdn = lax.ppermute(head, ROWS, down)

    rightward = [(i, i + 1) for i in range(ncol - 1)]
    leftward = [(i + 1, i) for i in range(ncol - 1)]
    to_right, to_left, tile_list, tile_owner = lax.optimization_barrier((*edge_cols(*big, hup, hdn), tile_list, tile_owner))
    hcl = lax.ppermute(to_right, COLS, rightward)
    hcr = lax.ppermute(to_left, COLS, leftward)
    row_at = lax.axis_index(ROWS)
    col_at = lax.axis_index(COLS)
    has = jnp.stack([row_at > 0, row_at < nrow - 1, col_at > 0, col_at < ncol - 1]).astype(jnp.int32)
    runs = C // W
    trow, tcol = tile_list // runs, tile_list % runs
    run = jnp.where(tcol == 0, trow, jnp.where(tcol == runs - 1, R + trow, jnp.where(trow == 0, 2 * R + tcol, 2 * R + 16 + tcol)))
    owner = tile_owner[:, 0]
    onehot = (owner[:, None] == jnp.arange(2 * NG, dtype=jnp.int32)[None, :]).astype(jnp.int32)
    ranks = jnp.cumsum(onehot, axis=0) - onehot
    rank = jnp.sum(ranks * onehot, axis=1)
    slot = (((owner & 1) ^ core) * NG + (owner >> 1)) * CAP + rank
    hits = (jnp.arange(RIM, dtype=jnp.int32)[:, None] == run[None, :]).astype(BF16)
    cnt = jnp.dot(hits, jnp.ones((T, W), BF16), preferred_element_type=F32)
    strips, rows, r_tiles, slots = rim(has, run, slot, *big, hup, hdn, hcl, hcr, cnt)
    mine, slots = lax.optimization_barrier((mine, slots))
    theirs = lax.ppermute(mine, "c", [(0, 1), (1, 0)])
    q, part = product_first(slots, mine)
    q, sums = product_second(q, theirs, part)
    q, sums, late_rhs, late_sigma = lax.optimization_barrier((q, sums, rhs, sigma))
    red = lax.all_to_all(sums, ALL, 0, 0, tiled=True)
    field, q_tiles = dense(slot, q, in_hbm(late_rhs), in_hbm(late_sigma))
    return tuple(final(red, r_tiles, q_tiles, strips, rows, field))


def solution(mesh):
    grid = Mesh(mesh.devices.reshape(4, 4, 4, 2), ("y", "z", "x", "c"))
    in_specs = (P(ROWS, COLS), P(ROWS, COLS), P(ALL), P(ALL, None), P(ALL, None, None))
    out_specs = (P(ROWS, COLS), P(ALL, None), P(ALL, None))
    return jax.shard_map(step, mesh=grid, in_specs=in_specs, out_specs=out_specs, check_vma=False)
```

```python
import jax
import jax.numpy as jnp
from jax import lax
from jax.experimental import pallas as pl
from jax.experimental.pallas import tpu as pltpu
from jax.sharding import Mesh, PartitionSpec as P

F32 = jnp.float32
BF16 = jnp.bfloat16
R, C, W = 768, 2048, 128
T = 2048
CAP = 32
NG = 64
RIM = 2 * R + 32
PR = 72
OFF = 16
FR = R + 2 * OFF
FC = 896
ROWS = ("y", "z")
COLS = ("x", "c")
ALL = ("y", "z", "x", "c")
CHIPS = ("y", "z", "x")
VM = pl.BlockSpec(memory_space=pltpu.VMEM)
SM = pl.BlockSpec(memory_space=pltpu.SMEM)
ANY = pl.BlockSpec(memory_space=pl.ANY)
C1 = 0.6111111
K1 = C1 + 2.75 * (1.0 - C1)
K2 = 2.75 * C1
PARAMS = pltpu.CompilerParams(vmem_limit_bytes=20 << 20)


def sds(shape, dtype=F32):
    return jax.ShapeDtypeStruct(shape, dtype)


def keep(shape, dtype=F32):
    return pltpu.VMEM(shape, dtype)


def in_hbm(x):
    return pltpu.with_memory_space_constraint(x, pltpu.HBM)


def in_vmem(x):
    return pltpu.with_memory_space_constraint(x, pltpu.VMEM)


def head_kernel(s_ref, rhs, sigma, out_ref, tail_ref, head_ref, rows, sems):
    ends = (slice(R - 8, R), slice(0, 8))
    loads = [pltpu.make_async_copy(src.at[p], rows.at[2 * k + n], sems.at[2 * k + n]) for k, p in enumerate(ends) for n, src in enumerate((rhs, sigma))]
    for c in loads:
        c.start()
    s = s_ref[0].astype(F32)
    top, bot = s[:64], s[64:]
    i = lax.broadcasted_iota(jnp.int32, (64, W), 0)
    j = lax.broadcasted_iota(jnp.int32, (64, W), 1)
    d = j - i
    body = jnp.where((d >= 0) & (d < 64), top, bot)
    half = jnp.sum(jnp.where(d == 64, top, 0.0), axis=0, keepdims=True)
    row = half + pltpu.roll(half, 64, axis=1)
    full = jnp.concatenate([body, jnp.broadcast_to(row, (8, W))], axis=0).astype(BF16)
    for k in range(NG):
        out_ref[k] = full
    for c in loads:
        c.wait()
    tail_ref[0:2] = rows[0, 6:8]
    tail_ref[2:4] = rows[1, 6:8]
    head_ref[0:2] = rows[2, 0:2]
    head_ref[2:4] = rows[3, 0:2]


def start(blocks, rhs, sigma):
    return pl.pallas_call(
        head_kernel, out_shape=[keep((NG, PR, W), BF16), keep((4, C)), keep((4, C))], in_specs=[VM, ANY, ANY], out_specs=[VM, VM, VM],
        scratch_shapes=[pltpu.VMEM((4, 8, C), F32), pltpu.SemaphoreType.DMA((4,))], compiler_params=PARAMS, name="head")(in_hbm(blocks), rhs, sigma)


def sides(tiles):
    lane = lax.broadcasted_iota(jnp.int32, (1, W), 1)
    n = len(tiles)
    prev = [pltpu.roll(t, 1, axis=1) for t in tiles]
    succ = [pltpu.roll(t, W - 1, axis=1) for t in tiles]
    return [jnp.where(lane == 0, prev[c - 1], prev[c]) + jnp.where(lane == W - 1, succ[(c + 1) % n], succ[c]) for c in range(n)]


NC = 8
NR = R // NC


def dense_kernel(slot_ref, q_ref, x_hbm, s_hbm, out_hbm, tiles_ref, x, s, g, ins, outs):
    nt = C // W
    tiles = [slice(c * W, (c + 1) * W) for c in range(nt)]
    chunks = [slice(k * NR, (k + 1) * NR) for k in range(NC)]
    loads = [[pltpu.make_async_copy(src.at[p], dst.at[p], ins.at[n, k]) for n, (src, dst) in enumerate(((x_hbm, x), (s_hbm, s)))]
             for k, p in enumerate(chunks)]
    for pair in loads:
        for c in pair:
            c.start()

    def body(b, carry):
        for u in range(16):
            t = b * 16 + u
            tiles_ref[pl.ds(t, 1), :] = q_ref[pl.ds(slot_ref[t], 1), :]
        return carry

    lax.fori_loop(0, T // 16, body, 0)
    for c in range(nt):
        g[c, 0:8] = jnp.zeros((8, W), F32)
        g[c, R + 8:R + 16] = jnp.zeros((8, W), F32)

    def first(k):
        for c in loads[k]:
            c.wait()
        p = chunks[k]
        for c, lanes in enumerate(tiles):
            dinv = 1.0 / (4.0 + s[p, lanes])
            s[p, lanes] = dinv
            g[c, 8 + k * NR:8 + (k + 1) * NR] = dinv * x[p, lanes]

    def second(k):
        for j in range(k * NR // 8, (k + 1) * NR // 8):
            rows = slice(8 * j, 8 * j + 8)
            side = sides([g[c, 8 * j + 8:8 * j + 16] for c in range(nt)])
            for c, lanes in enumerate(tiles):
                beside = (g[c, 8 * j + 7:8 * j + 15] + g[c, 8 * j + 9:8 * j + 17]) + side[c]
                x[rows, lanes] = s[rows, lanes] * (K1 * x[rows, lanes] + K2 * beside)
        c = pltpu.make_async_copy(x.at[chunks[k]], out_hbm.at[chunks[k]], outs.at[k])
        c.start()
        return c

    sent = []
    for k in range(NC):
        first(k)
        if k:
            sent.append(second(k - 1))
    sent.append(second(NC - 1))
    for c in sent:
        c.wait()


def dense(slot, q, rhs, sigma):
    return pl.pallas_call(
        dense_kernel, out_shape=[sds((R, C)), keep((T, W))], in_specs=[SM, VM, ANY, ANY], out_specs=[ANY, VM],
        scratch_shapes=[pltpu.VMEM((R, C), F32), pltpu.VMEM((R, C), F32), pltpu.VMEM((C // W, R + 16, W), F32),
                        pltpu.SemaphoreType.DMA((2, NC)), pltpu.SemaphoreType.DMA((NC,))],
        compiler_params=pltpu.CompilerParams(vmem_limit_bytes=32 << 20), name="dense")(slot, q, rhs, sigma)


def cols_kernel(xl, sl, xr, sr, hup, hdn, right_out, left_out, buf):
    buf[0:OFF] = jnp.zeros((OFF, W), F32)
    buf[OFF + R:FC] = jnp.zeros((FC - OFF - R, W), F32)
    for out, x, s, c0, lane in ((right_out, xr, sr, C - W, W - 8), (left_out, xl, sl, 0, 0)):
        cols = slice(c0, c0 + W)
        for k, src in ((0, x), (2, s)):
            buf[OFF - 2:OFF] = hup[k:k + 2, cols]
            buf[OFF:OFF + R] = src[...]
            buf[OFF + R:OFF + R + 2] = hdn[k:k + 2, cols]
            for c in range(FC // W):
                out[4 * k:4 * k + 8, c * W:(c + 1) * W] = buf[c * W:(c + 1) * W].T[lane:lane + 8]


def edge_cols(rhs, sigma, hup, hdn):
    left = pl.BlockSpec((R, W), lambda i: (0, 0))
    right = pl.BlockSpec((R, W), lambda i: (0, C // W - 1))
    rows = pl.BlockSpec((4, C), lambda i: (0, 0))
    out = pl.BlockSpec((16, FC), lambda i: (0, 0))
    return pl.pallas_call(cols_kernel, grid=(1,), out_shape=[sds((16, FC))] * 2, in_specs=[left, left, right, right, rows, rows], out_specs=[out, out],
                          scratch_shapes=[pltpu.VMEM((FC, W), F32)], compiler_params=PARAMS, name="cols")(rhs, sigma, rhs, sigma, hup, hdn)


def rim_kernel(has_ref, run_ref, slot_ref, xl, sl, xr, sr, xt, st, xb, sb, hup, hdn, hcl, hcr, cnt, strips_out, rows_out, tiles_out, slots_ref,
               r_out, strips, rows_buf, tiles, sems, X, D, G, S, H, D2, G2, S2):
    slots_ref[...] = jnp.zeros_like(slots_ref)
    up, down, left, right = (has_ref[k] for k in range(4))
    lane = lax.broadcasted_iota(jnp.int32, (1, W), 1)

    def stencil(x, d, above, under, side):
        return d * (K1 * x + K2 * ((above + under) + side))

    def strip(x, s, c0, hc, m, a, alive, base):
        q = 1 - m
        sel = (lane == a) | (lane == a + 1)
        pad = jnp.zeros((W - 8, W), F32)
        for n in (0, 1):
            for c in range(FC // W):
                got = hc[8 * n:8 * n + 8, c * W:(c + 1) * W]
                H[n, c * W:(c + 1) * W] = jnp.concatenate([got, pad] if a == 0 else [pad, got], axis=0).T
        for c in (0, 1):
            cols = slice(c0 + c * W, c0 + (c + 1) * W)
            for rows, xv, sv in ((slice(OFF - 2, OFF), hup[0:2, cols], hup[2:4, cols]),
                                 (slice(OFF + R, OFF + R + 2), hdn[0:2, cols], hdn[2:4, cols]),
                                 (slice(OFF, OFF + R), x[:, c * W:(c + 1) * W], s[:, c * W:(c + 1) * W])):
                if c == m:
                    xv = jnp.where(sel, H[0, rows], xv)
                    sv = jnp.where(sel, H[1, rows], sv)
                dinv = 1.0 / (4.0 + sv)
                D[c, rows] = dinv
                X[c, rows] = xv
                G[c, rows] = dinv * xv
        live = ~sel | (alive > 0)

        def second(r0, n, ok):
            rows = slice(r0, r0 + n)
            side = sides([G[0, rows], G[1, rows]])
            for c in (0, 1):
                v = stencil(X[c, rows], D[c, rows], G[c, r0 - 1:r0 + n - 1], G[c, r0 + 1:r0 + n + 1], side[c])
                keep = live if c == m else None
                if ok is not None:
                    keep = ok if keep is None else keep & ok
                S[c, rows] = v if keep is None else jnp.where(keep, v, 0.0)

        second(OFF - 1, 1, up > 0)
        second(OFF + R, 1, down > 0)
        for k in range(R // 8):
            second(OFF + 8 * k, 8, None)
        for k in range(R // 8):
            r0 = OFF + 8 * k
            rows = slice(r0, r0 + 8)
            side = sides([S[0, rows], S[1, rows]])[q]
            v = S[q, rows]
            own = slice(8 * k, 8 * k + 8)
            t = 4.0 + s[own, q * W:(q + 1) * W]
            res = X[q, rows] - (t * v - ((S[q, r0 - 1:r0 + 7] + S[q, r0 + 1:r0 + 9]) + side))
            at = slice(base + 8 * k, base + 8 * k + 8)
            r_out[at] = res
            strips[0, at] = v
            strips[1, at] = cnt[at] * res

    strip(xl, sl, 0, hcl, 1, W - 2, left, 0)
    strip(xr, sr, C - 2 * W, hcr, 0, 0, right, R)
    copies = [pltpu.make_async_copy(strips, strips_out, sems.at[0]), pltpu.make_async_copy(rows_buf, rows_out, sems.at[1])]
    copies[0].start()

    def edge(x, s, halo, h, g, o, alive, part, line, base):
        nt = C // W
        tiles = [slice(c * W, (c + 1) * W) for c in range(nt)]
        ok = alive > 0
        for c, cols in enumerate(tiles):
            dinv = 1.0 / (4.0 + s[:, cols])
            D2[c, 8:24] = dinv
            G2[c, 8:24] = dinv * x[:, cols]
            dinv = 1.0 / (4.0 + halo[2:4, cols])
            D2[c, h:h + 2] = dinv
            G2[c, h:h + 2] = dinv * halo[0:2, cols]
        side = sides([G2[c, g:g + 8] for c in range(nt)])
        outer = sides([G2[c, o:o + 1] for c in range(nt)])
        near = halo[1:2, :] if o < g else halo[0:1, :]
        for c, cols in enumerate(tiles):
            S2[c, g:g + 8] = stencil(x[g - 8:g, cols], D2[c, g:g + 8], G2[c, g - 1:g + 7], G2[c, g + 1:g + 9], side[c])
            v = stencil(near[:, cols], D2[c, o:o + 1], G2[c, o - 1:o], G2[c, o + 1:o + 2], outer[c])
            S2[c, o:o + 1] = jnp.where(ok, v, 0.0)
        side = sides([S2[c, g:g + 8] for c in range(nt)])
        for c, cols in enumerate(tiles):
            v = S2[c, g:g + 8]
            rows_buf[part, :, cols] = v
            at = g + line
            one = slice(at, at + 1)
            t = 4.0 + s[at - 8:at - 7, cols]
            res = x[at - 8:at - 7, cols] - (t * S2[c, one] - ((S2[c, at - 1:at] + S2[c, at + 1:at + 2]) + side[c][line:line + 1]))
            r_out[base + c:base + c + 1] = res
            rows_buf[2, part:part + 1, cols] = cnt[base + c:base + c + 1] * res

    edge(xt, st, hup, 6, 8, 7, up, 0, 0, 2 * R)
    edge(xb, sb, hdn, 24, 16, 24, down, 1, 7, 2 * R + 16)
    copies[1].start()

    def body(b, carry):
        for u in range(16):
            t = b * 16 + u
            row = r_out[pl.ds(run_ref[t], 1), :]
            tiles[pl.ds(t, 1), :] = row
            slots_ref[pl.ds(slot_ref[t], 1), :] = row
        return carry

    for k in range(4):
        lax.fori_loop(k * T // 64, (k + 1) * T // 64, body, 0)
        part = pl.ds(k * T // 4, T // 4)
        copies.append(pltpu.make_async_copy(tiles.at[part], tiles_out.at[part], sems.at[2 + k]))
        copies[-1].start()
    for c in copies:
        c.wait()


def near_kernel(rhs, sigma, *refs):
    outs, sems = refs[:8], refs[8]
    places = ((slice(None), slice(0, 2 * W)), (slice(None), slice(C - 2 * W, C)), (slice(0, 16), slice(None)), (slice(R - 16, R), slice(None)))
    copies = [pltpu.make_async_copy(src.at[p], outs[2 * k + n], sems.at[2 * k + n]) for k, p in enumerate(places) for n, src in enumerate((rhs, sigma))]
    for c in copies:
        c.start()
    for c in copies:
        c.wait()


def near(rhs, sigma):
    return pl.pallas_call(near_kernel, out_shape=[keep((R, 2 * W))] * 4 + [keep((16, C))] * 4, in_specs=[ANY, ANY], out_specs=[VM] * 8,
                          scratch_shapes=[pltpu.SemaphoreType.DMA((8,))], compiler_params=PARAMS, name="near")(rhs, sigma)


def rim(has, run, slot, parts, hup, hdn, hcl, hcr, cnt):
    strips, rows, tiles = (2, 2 * R, W), (3, 8, C), (T, W)
    return pl.pallas_call(
        rim_kernel, out_shape=[pltpu.HBM(strips, F32), pltpu.HBM(rows, F32), pltpu.HBM(tiles, F32), keep((2 * NG * CAP, W))],
        in_specs=[SM, SM, SM] + [VM] * 13,
        out_specs=[ANY, ANY, ANY, VM],
        scratch_shapes=[pltpu.VMEM((RIM, W), F32), pltpu.VMEM(strips, F32), pltpu.VMEM(rows, F32), pltpu.VMEM(tiles, F32), pltpu.SemaphoreType.DMA((6,))]
        + [pltpu.VMEM((2, FR, W), F32)] * 4 + [pltpu.VMEM((2, FC, W), F32)] + [pltpu.VMEM((C // W, 32, W), F32)] * 3,
        compiler_params=PARAMS, name="rim")(has, run, slot, *parts, hup, hdn, in_vmem(hcl), in_vmem(hcr), in_vmem(cnt))


def product_kernel(first, slots_ref, blk_ref, *refs):
    if first:
        q_ref, sums_ref, _ = refs
    else:
        prev_ref, q_ref, sums_ref = refs
    i = lax.broadcasted_iota(jnp.int32, (64, W), 0)
    j = lax.broadcasted_iota(jnp.int32, (64, W), 1)
    d = j - i
    band = jnp.where((d >= 0) & (d < 64), 1.0, 0.0)
    mask_top = jnp.where(d == 0, 0.5, band).astype(BF16)
    mask_bot = jnp.where(d == 64, 0.5, 1.0 - band).astype(BF16)

    def fold(v):
        return jnp.sum(v.reshape(CAP // 8, 8, W), axis=0)

    scale = 1.0 if first else prev_ref[3, 0:1, :]

    def body(g, carry):
        rr, pq, vv, ra, qa = carry
        rows = pl.ds(pl.multiple_of(g * CAP, CAP), CAP)
        r = slots_ref[rows, :]
        half = r.astype(BF16)
        b = blk_ref[g, 0:64, :]
        u = jnp.concatenate([b * mask_top, b * mask_bot], axis=0)
        cross = blk_ref[g, 64:72, :].astype(F32)
        swapped = pltpu.roll(half.astype(F32), 64, axis=1)
        q = jnp.dot(half, u + u.T, preferred_element_type=F32)
        q = q + (swapped.reshape(CAP // 8, 8, W) * cross[None]).reshape(CAP, W)
        q = q.astype(BF16).astype(F32)
        q_ref[rows, :] = q
        rr = rr + fold(r * r)
        pq = pq + fold(r * q)
        if first:
            ra = ra + fold(jnp.abs(r))
            qa = qa + fold(jnp.abs(q))
        else:
            v = q * scale
            vv = vv + fold(v * v)
        return rr, pq, vv, ra, qa

    zero = jnp.zeros((8, W), F32)
    rr, pq, vv, ra, qa = lax.fori_loop(0, NG, body, (zero,) * 5, unroll=8)
    if first:
        ra, qa = jnp.sum(ra), jnp.sum(qa)
        ok = (qa > 0.0) & (ra > 0.0)
        a0 = jnp.full((1, W), jnp.where(ok, ra, 1.0)) / jnp.full((1, W), jnp.where(ok, qa, 1.0))

        def second_pass(k, acc):
            v = q_ref[pl.ds(pl.multiple_of(k * 64, 64), 64), :] * a0
            return acc + jnp.sum((v * v).reshape(8, 8, W), axis=0)

        vv = lax.fori_loop(0, NG * CAP // 64, second_pass, zero, unroll=8)
        sums_ref[0], sums_ref[1], sums_ref[2] = rr, pq, vv
        sums_ref[3] = jnp.broadcast_to(a0, (8, W))
    else:
        rows = [jnp.sum(v + prev_ref[k], axis=0, keepdims=True) for k, v in enumerate((rr, pq, vv))]
        full = jnp.concatenate(rows + [scale], axis=0)
        for k in range(2 * NG):
            sums_ref[k] = full


def product_first(slots, blocks):
    def kernel(s, b, q, sums):
        here = q.at[0:NG * CAP]
        product_kernel(True, here, b, here, sums, None)

    return pl.pallas_call(kernel, out_shape=[keep((2 * NG * CAP, W)), keep((4, 8, W))], in_specs=[VM, VM], out_specs=[VM, VM], input_output_aliases={0: 0},
                          compiler_params=PARAMS, name="product_a")(slots, in_vmem(blocks))


def product_second(slots, blocks, prev):
    def kernel(s, b, p, q, sums):
        here = q.at[NG * CAP:2 * NG * CAP]
        product_kernel(False, here, b, p, here, sums)

    return pl.pallas_call(kernel, out_shape=[keep((2 * NG * CAP, W)), keep((2 * NG, 4, W))], input_output_aliases={0: 0},
                          in_specs=[VM, VM, VM], out_specs=[VM, VM], compiler_params=PARAMS, name="product_b")(slots, in_vmem(blocks), prev)


CH = 4
TC = T // CH


def final_kernel(red_ref, r_hbm, q_ref, strips_ref, rows_ref, field_ref, out_ref, res_hbm, dir_hbm, r_buf, res_buf, dir_buf, strips, rows, ins, outs):
    inner = slice(W, C - W)
    parts = [slice(k * TC, (k + 1) * TC) for k in range(CH)]
    tiles_in = [pltpu.make_async_copy(r_hbm.at[p], r_buf.at[p], ins.at[k]) for k, p in enumerate(parts)]
    rim_in = [pltpu.make_async_copy(strips_ref, strips, ins.at[CH]), pltpu.make_async_copy(rows_ref, rows, ins.at[CH + 1])]
    for c in tiles_in + rim_in:
        c.start()
    rr = jnp.sum(red_ref[:, 0, :])
    pq = jnp.sum(red_ref[:, 1, :])
    alpha = jnp.full((1, W), rr) / jnp.full((1, W), pq)
    t = alpha / red_ref[:, 3, :]
    qq = jnp.sum(t * t * red_ref[:, 2, :])
    beta = (rr - 2.0 * alpha * pq + qq) / rr
    sent = []

    def send(src, dst):
        c = pltpu.make_async_copy(src, dst, outs.at[len(sent)])
        c.start()
        sent.append(c)

    def rim_out():
        for c in rim_in:
            c.wait()
        strips[0] = strips[0] + alpha * strips[1]
        send(strips.at[0, 0:R], out_ref.at[:, 0:W])
        send(strips.at[0, R:2 * R], out_ref.at[:, C - W:C])
        for k in range(C // W):
            lanes = slice(k * W, (k + 1) * W)
            rows[0, 0:1, lanes] = rows[0, 0:1, lanes] + alpha * rows[2, 0:1, lanes]
            rows[1, 7:8, lanes] = rows[1, 7:8, lanes] + alpha * rows[2, 1:2, lanes]
        send(rows.at[0, :, inner], out_ref.at[0:8, inner])
        send(rows.at[1, :, inner], out_ref.at[R - 8:R, inner])

    for k, p in enumerate(parts):
        tiles_in[k].wait()
        r = r_buf[p]
        res = r - alpha * q_ref[p]
        res_buf[p] = res
        dir_buf[p] = res + beta * r
        send(res_buf.at[p], res_hbm.at[p])
        send(dir_buf.at[p], dir_hbm.at[p])
        if k == 1:
            rim_out()
    for c in sent:
        c.wait()


def final(red, r_tiles, q_tiles, strips, rows, field):
    return pl.pallas_call(
        final_kernel, out_shape=[sds((R, C)), sds((T, W)), sds((T, W))],
        in_specs=[VM, ANY, VM, ANY, ANY, ANY], out_specs=[ANY, ANY, ANY],
        scratch_shapes=[pltpu.VMEM((T, W), F32)] * 3 + [pltpu.VMEM((2, 2 * R, W), F32), pltpu.VMEM((3, 8, C), F32),
                        pltpu.SemaphoreType.DMA((CH + 2,)), pltpu.SemaphoreType.DMA((2 * CH + 4,))],
        input_output_aliases={5: 0}, compiler_params=PARAMS, name="final")(in_vmem(red), in_hbm(r_tiles), q_tiles, in_hbm(strips), in_hbm(rows), field)


def step(rhs, sigma, tile_list, tile_owner, schur_blocks):
    core = lax.axis_index("c")
    big = (in_hbm(rhs), in_hbm(sigma))
    packed, tail, head = start(schur_blocks, *big)
    mine = lax.all_to_all(packed, CHIPS, 0, 0, tiled=True)
    nrow, ncol = 16, 8
    up = [(i, i + 1) for i in range(nrow - 1)]
    down = [(i + 1, i) for i in range(nrow - 1)]
    hup = lax.ppermute(tail, ROWS, up)
    hdn = lax.ppermute(head, ROWS, down)

    rightward = [(i, i + 1) for i in range(ncol - 1)]
    leftward = [(i + 1, i) for i in range(ncol - 1)]
    to_right, to_left, tile_list, tile_owner = lax.optimization_barrier((*edge_cols(*big, hup, hdn), tile_list, tile_owner))
    hcl = lax.ppermute(to_right, COLS, rightward)
    hcr = lax.ppermute(to_left, COLS, leftward)
    row_at = lax.axis_index(ROWS)
    col_at = lax.axis_index(COLS)
    has = jnp.stack([row_at > 0, row_at < nrow - 1, col_at > 0, col_at < ncol - 1]).astype(jnp.int32)
    runs = C // W
    trow, tcol = tile_list // runs, tile_list % runs
    run = jnp.where(tcol == 0, trow, jnp.where(tcol == runs - 1, R + trow, jnp.where(trow == 0, 2 * R + tcol, 2 * R + 16 + tcol)))
    owner = tile_owner[:, 0]
    onehot = (owner[:, None] == jnp.arange(2 * NG, dtype=jnp.int32)[None, :]).astype(jnp.int32)
    ranks = jnp.cumsum(onehot, axis=0) - onehot
    rank = jnp.sum(ranks * onehot, axis=1)
    slot = (((owner & 1) ^ core) * NG + (owner >> 1)) * CAP + rank
    hits = (jnp.arange(RIM, dtype=jnp.int32)[:, None] == run[None, :]).astype(BF16)
    cnt = jnp.dot(hits, jnp.ones((T, W), BF16), preferred_element_type=F32)
    cnt, slot, *here = lax.optimization_barrier((cnt, slot, rhs, sigma))
    parts = near(*(in_hbm(v) for v in here))
    strips, rows, r_tiles, slots = rim(has, run, slot, parts, hup, hdn, hcl, hcr, cnt)
    mine, slots = lax.optimization_barrier((mine, slots))
    theirs = lax.ppermute(mine, "c", [(0, 1), (1, 0)])
    q, part = product_first(slots, mine)
    q, sums = product_second(q, theirs, part)
    q, sums, late_rhs, late_sigma = lax.optimization_barrier((q, sums, rhs, sigma))
    red = lax.all_to_all(sums, ALL, 0, 0, tiled=True)
    field, q_tiles = dense(slot, q, in_hbm(late_rhs), in_hbm(late_sigma))
    return tuple(final(red, r_tiles, q_tiles, strips, rows, field))


def solution(mesh):
    grid = Mesh(mesh.devices.reshape(4, 4, 4, 2), ("y", "z", "x", "c"))
    in_specs = (P(ROWS, COLS), P(ROWS, COLS), P(ALL), P(ALL, None), P(ALL, None, None))
    out_specs = (P(ROWS, COLS), P(ALL, None), P(ALL, None))
    return jax.shard_map(step, mesh=grid, in_specs=in_specs, out_specs=out_specs, check_vma=False)
```

```python
import jax
import jax.numpy as jnp
from jax import lax
from jax.experimental import pallas as pl
from jax.experimental.pallas import tpu as pltpu
from jax.sharding import Mesh, PartitionSpec as P

F32 = jnp.float32
BF16 = jnp.bfloat16
R, C, W = 768, 2048, 128
T = 2048
CAP = 32
NG = 64
RIM = 2 * R + 32
PR = 72
OFF = 16
FR = R + 2 * OFF
FC = 896
ROWS = ("y", "z")
COLS = ("x", "c")
ALL = ("y", "z", "x", "c")
CHIPS = ("y", "z", "x")
VM = pl.BlockSpec(memory_space=pltpu.VMEM)
SM = pl.BlockSpec(memory_space=pltpu.SMEM)
ANY = pl.BlockSpec(memory_space=pl.ANY)
C1 = 0.6111111
K1 = C1 + 2.75 * (1.0 - C1)
K2 = 2.75 * C1
PARAMS = pltpu.CompilerParams(vmem_limit_bytes=20 << 20)


def sds(shape, dtype=F32):
    return jax.ShapeDtypeStruct(shape, dtype)


def keep(shape, dtype=F32):
    return pltpu.VMEM(shape, dtype)


def in_hbm(x):
    return pltpu.with_memory_space_constraint(x, pltpu.HBM)


def in_vmem(x):
    return pltpu.with_memory_space_constraint(x, pltpu.VMEM)


def head_kernel(s_ref, rhs, sigma, out_ref, tail_ref, head_ref, rows, sems):
    ends = (slice(R - 8, R), slice(0, 8))
    loads = [pltpu.make_async_copy(src.at[p], rows.at[2 * k + n], sems.at[2 * k + n]) for k, p in enumerate(ends) for n, src in enumerate((rhs, sigma))]
    for c in loads:
        c.start()
    s = s_ref[0].astype(F32)
    top, bot = s[:64], s[64:]
    i = lax.broadcasted_iota(jnp.int32, (64, W), 0)
    j = lax.broadcasted_iota(jnp.int32, (64, W), 1)
    d = j - i
    body = jnp.where((d >= 0) & (d < 64), top, bot)
    half = jnp.sum(jnp.where(d == 64, top, 0.0), axis=0, keepdims=True)
    row = half + pltpu.roll(half, 64, axis=1)
    full = jnp.concatenate([body, jnp.broadcast_to(row, (8, W))], axis=0).astype(BF16)
    for k in range(NG):
        out_ref[k] = full
    for c in loads:
        c.wait()
    tail_ref[0:2] = rows[0, 6:8]
    tail_ref[2:4] = rows[1, 6:8]
    head_ref[0:2] = rows[2, 0:2]
    head_ref[2:4] = rows[3, 0:2]


def start(blocks, rhs, sigma):
    return pl.pallas_call(
        head_kernel, out_shape=[keep((NG, PR, W), BF16), keep((4, C)), keep((4, C))], in_specs=[VM, ANY, ANY], out_specs=[VM, VM, VM],
        scratch_shapes=[pltpu.VMEM((4, 8, C), F32), pltpu.SemaphoreType.DMA((4,))], compiler_params=PARAMS, name="head")(in_hbm(blocks), rhs, sigma)


def sides(tiles):
    lane = lax.broadcasted_iota(jnp.int32, (1, W), 1)
    n = len(tiles)
    prev = [pltpu.roll(t, 1, axis=1) for t in tiles]
    succ = [pltpu.roll(t, W - 1, axis=1) for t in tiles]
    return [jnp.where(lane == 0, prev[c - 1], prev[c]) + jnp.where(lane == W - 1, succ[(c + 1) % n], succ[c]) for c in range(n)]


NC = 8
NR = R // NC


def dense_kernel(slot_ref, q_ref, x_hbm, s_hbm, out_hbm, tiles_ref, x, s, g, ins, outs):
    nt = C // W
    tiles = [slice(c * W, (c + 1) * W) for c in range(nt)]
    chunks = [slice(k * NR, (k + 1) * NR) for k in range(NC)]
    loads = [[pltpu.make_async_copy(src.at[p], dst.at[p], ins.at[n, k]) for n, (src, dst) in enumerate(((x_hbm, x), (s_hbm, s)))]
             for k, p in enumerate(chunks)]
    for pair in loads:
        for c in pair:
            c.start()

    def body(b, carry):
        for u in range(16):
            t = b * 16 + u
            tiles_ref[pl.ds(t, 1), :] = q_ref[pl.ds(slot_ref[t], 1), :]
        return carry

    lax.fori_loop(0, T // 16, body, 0)
    for c in range(nt):
        g[c, 0:8] = jnp.zeros((8, W), F32)
        g[c, R + 8:R + 16] = jnp.zeros((8, W), F32)

    def first(k):
        for c in loads[k]:
            c.wait()
        p = chunks[k]
        for c, lanes in enumerate(tiles):
            dinv = 1.0 / (4.0 + s[p, lanes])
            s[p, lanes] = dinv
            g[c, 8 + k * NR:8 + (k + 1) * NR] = dinv * x[p, lanes]

    def second(k):
        for j in range(k * NR // 8, (k + 1) * NR // 8):
            rows = slice(8 * j, 8 * j + 8)
            side = sides([g[c, 8 * j + 8:8 * j + 16] for c in range(nt)])
            for c, lanes in enumerate(tiles):
                beside = (g[c, 8 * j + 7:8 * j + 15] + g[c, 8 * j + 9:8 * j + 17]) + side[c]
                x[rows, lanes] = s[rows, lanes] * (K1 * x[rows, lanes] + K2 * beside)
        c = pltpu.make_async_copy(x.at[chunks[k]], out_hbm.at[chunks[k]], outs.at[k])
        c.start()
        return c

    sent = []
    for k in range(NC):
        first(k)
        if k:
            sent.append(second(k - 1))
    sent.append(second(NC - 1))
    for c in sent:
        c.wait()


def dense(slot, q, rhs, sigma):
    return pl.pallas_call(
        dense_kernel, out_shape=[sds((R, C)), keep((T, W))], in_specs=[SM, VM, ANY, ANY], out_specs=[ANY, VM],
        scratch_shapes=[pltpu.VMEM((R, C), F32), pltpu.VMEM((R, C), F32), pltpu.VMEM((C // W, R + 16, W), F32),
                        pltpu.SemaphoreType.DMA((2, NC)), pltpu.SemaphoreType.DMA((NC,))],
        compiler_params=pltpu.CompilerParams(vmem_limit_bytes=32 << 20), name="dense")(slot, q, rhs, sigma)


def cols_kernel(xl, sl, xr, sr, hup, hdn, right_out, left_out, buf):
    buf[0:OFF] = jnp.zeros((OFF, W), F32)
    buf[OFF + R:FC] = jnp.zeros((FC - OFF - R, W), F32)
    for out, x, s, c0, lane in ((right_out, xr, sr, C - W, W - 8), (left_out, xl, sl, 0, 0)):
        cols = slice(c0, c0 + W)
        for k, src in ((0, x), (2, s)):
            buf[OFF - 2:OFF] = hup[k:k + 2, cols]
            buf[OFF:OFF + R] = src[...]
            buf[OFF + R:OFF + R + 2] = hdn[k:k + 2, cols]
            for c in range(FC // W):
                out[4 * k:4 * k + 8, c * W:(c + 1) * W] = buf[c * W:(c + 1) * W].T[lane:lane + 8]


def edge_cols(rhs, sigma, hup, hdn):
    left = pl.BlockSpec((R, W), lambda i: (0, 0))
    right = pl.BlockSpec((R, W), lambda i: (0, C // W - 1))
    rows = pl.BlockSpec((4, C), lambda i: (0, 0))
    out = pl.BlockSpec((16, FC), lambda i: (0, 0))
    return pl.pallas_call(cols_kernel, grid=(1,), out_shape=[sds((16, FC))] * 2, in_specs=[left, left, right, right, rows, rows], out_specs=[out, out],
                          scratch_shapes=[pltpu.VMEM((FC, W), F32)], compiler_params=PARAMS, name="cols")(rhs, sigma, rhs, sigma, hup, hdn)


def rim_kernel(has_ref, run_ref, slot_ref, xl, sl, xr, sr, xt, st, xb, sb, hup, hdn, hcl, hcr, strips_out, rows_out, tiles_out, slots_ref,
               r_out, strips, rows_buf, tiles, sems, X, D, G, S, H, D2, G2, S2):
    slots_ref[...] = jnp.zeros_like(slots_ref)
    up, down, left, right = (has_ref[k] for k in range(4))
    lane = lax.broadcasted_iota(jnp.int32, (1, W), 1)

    def stencil(x, d, above, under, side):
        return d * (K1 * x + K2 * ((above + under) + side))

    def strip(x, s, c0, hc, m, a, alive, base):
        q = 1 - m
        sel = (lane == a) | (lane == a + 1)
        pad = jnp.zeros((W - 8, W), F32)
        for n in (0, 1):
            for c in range(FC // W):
                got = hc[8 * n:8 * n + 8, c * W:(c + 1) * W]
                H[n, c * W:(c + 1) * W] = jnp.concatenate([got, pad] if a == 0 else [pad, got], axis=0).T
        for c in (0, 1):
            cols = slice(c0 + c * W, c0 + (c + 1) * W)
            for rows, xv, sv in ((slice(OFF - 2, OFF), hup[0:2, cols], hup[2:4, cols]),
                                 (slice(OFF + R, OFF + R + 2), hdn[0:2, cols], hdn[2:4, cols]),
                                 (slice(OFF, OFF + R), x[:, c * W:(c + 1) * W], s[:, c * W:(c + 1) * W])):
                if c == m:
                    xv = jnp.where(sel, H[0, rows], xv)
                    sv = jnp.where(sel, H[1, rows], sv)
                dinv = 1.0 / (4.0 + sv)
                D[c, rows] = dinv
                X[c, rows] = xv
                G[c, rows] = dinv * xv
        live = ~sel | (alive > 0)

        def second(r0, n, ok):
            rows = slice(r0, r0 + n)
            side = sides([G[0, rows], G[1, rows]])
            for c in (0, 1):
                v = stencil(X[c, rows], D[c, rows], G[c, r0 - 1:r0 + n - 1], G[c, r0 + 1:r0 + n + 1], side[c])
                keep = live if c == m else None
                if ok is not None:
                    keep = ok if keep is None else keep & ok
                S[c, rows] = v if keep is None else jnp.where(keep, v, 0.0)

        second(OFF - 1, 1, up > 0)
        second(OFF + R, 1, down > 0)
        for k in range(R // 8):
            second(OFF + 8 * k, 8, None)
        for k in range(R // 8):
            r0 = OFF + 8 * k
            rows = slice(r0, r0 + 8)
            side = sides([S[0, rows], S[1, rows]])[q]
            v = S[q, rows]
            own = slice(8 * k, 8 * k + 8)
            t = 4.0 + s[own, q * W:(q + 1) * W]
            res = X[q, rows] - (t * v - ((S[q, r0 - 1:r0 + 7] + S[q, r0 + 1:r0 + 9]) + side))
            at = slice(base + 8 * k, base + 8 * k + 8)
            r_out[at] = res
            strips[0, at] = v
            strips[1, at] = res

    strip(xl, sl, 0, hcl, 1, W - 2, left, 0)
    strip(xr, sr, C - 2 * W, hcr, 0, 0, right, R)
    copies = [pltpu.make_async_copy(strips, strips_out, sems.at[0]), pltpu.make_async_copy(rows_buf, rows_out, sems.at[1])]
    copies[0].start()

    def edge(x, s, halo, h, g, o, alive, part, line, base):
        nt = C // W
        tiles = [slice(c * W, (c + 1) * W) for c in range(nt)]
        ok = alive > 0
        for c, cols in enumerate(tiles):
            dinv = 1.0 / (4.0 + s[:, cols])
            D2[c, 8:24] = dinv
            G2[c, 8:24] = dinv * x[:, cols]
            dinv = 1.0 / (4.0 + halo[2:4, cols])
            D2[c, h:h + 2] = dinv
            G2[c, h:h + 2] = dinv * halo[0:2, cols]
        side = sides([G2[c, g:g + 8] for c in range(nt)])
        outer = sides([G2[c, o:o + 1] for c in range(nt)])
        near = halo[1:2, :] if o < g else halo[0:1, :]
        for c, cols in enumerate(tiles):
            S2[c, g:g + 8] = stencil(x[g - 8:g, cols], D2[c, g:g + 8], G2[c, g - 1:g + 7], G2[c, g + 1:g + 9], side[c])
            v = stencil(near[:, cols], D2[c, o:o + 1], G2[c, o - 1:o], G2[c, o + 1:o + 2], outer[c])
            S2[c, o:o + 1] = jnp.where(ok, v, 0.0)
        side = sides([S2[c, g:g + 8] for c in range(nt)])
        for c, cols in enumerate(tiles):
            v = S2[c, g:g + 8]
            rows_buf[part, :, cols] = v
            at = g + line
            one = slice(at, at + 1)
            t = 4.0 + s[at - 8:at - 7, cols]
            res = x[at - 8:at - 7, cols] - (t * S2[c, one] - ((S2[c, at - 1:at] + S2[c, at + 1:at + 2]) + side[c][line:line + 1]))
            r_out[base + c:base + c + 1] = res
            rows_buf[2, part:part + 1, cols] = res

    edge(xt, st, hup, 6, 8, 7, up, 0, 0, 2 * R)
    edge(xb, sb, hdn, 24, 16, 24, down, 1, 7, 2 * R + 16)
    copies[1].start()

    def body(b, carry):
        for u in range(16):
            t = b * 16 + u
            row = r_out[pl.ds(run_ref[t], 1), :]
            tiles[pl.ds(t, 1), :] = row
            slots_ref[pl.ds(slot_ref[t], 1), :] = row
        return carry

    for k in range(4):
        lax.fori_loop(k * T // 64, (k + 1) * T // 64, body, 0)
        part = pl.ds(k * T // 4, T // 4)
        copies.append(pltpu.make_async_copy(tiles.at[part], tiles_out.at[part], sems.at[2 + k]))
        copies[-1].start()
    for c in copies:
        c.wait()


def near_kernel(rhs, sigma, *refs):
    outs, sems = refs[:8], refs[8]
    places = ((slice(None), slice(0, 2 * W)), (slice(None), slice(C - 2 * W, C)), (slice(0, 16), slice(None)), (slice(R - 16, R), slice(None)))
    copies = [pltpu.make_async_copy(src.at[p], outs[2 * k + n], sems.at[2 * k + n]) for k, p in enumerate(places) for n, src in enumerate((rhs, sigma))]
    for c in copies:
        c.start()
    for c in copies:
        c.wait()


def near(rhs, sigma):
    return pl.pallas_call(near_kernel, out_shape=[keep((R, 2 * W))] * 4 + [keep((16, C))] * 4, in_specs=[ANY, ANY], out_specs=[VM] * 8,
                          scratch_shapes=[pltpu.SemaphoreType.DMA((8,))], compiler_params=PARAMS, name="near")(rhs, sigma)


def rim(has, run, slot, parts, hup, hdn, hcl, hcr):
    strips, rows, tiles = (2, 2 * R, W), (3, 8, C), (T, W)
    return pl.pallas_call(
        rim_kernel, out_shape=[pltpu.HBM(strips, F32), pltpu.HBM(rows, F32), pltpu.HBM(tiles, F32), keep((2 * NG * CAP, W))],
        in_specs=[SM, SM, SM] + [VM] * 12,
        out_specs=[ANY, ANY, ANY, VM],
        scratch_shapes=[pltpu.VMEM((RIM, W), F32), pltpu.VMEM(strips, F32), pltpu.VMEM(rows, F32), pltpu.VMEM(tiles, F32), pltpu.SemaphoreType.DMA((6,))]
        + [pltpu.VMEM((2, FR, W), F32)] * 4 + [pltpu.VMEM((2, FC, W), F32)] + [pltpu.VMEM((C // W, 32, W), F32)] * 3,
        compiler_params=PARAMS, name="rim")(has, run, slot, *parts, hup, hdn, in_vmem(hcl), in_vmem(hcr))


def product_kernel(first, slots_ref, blk_ref, *refs):
    if first:
        q_ref, sums_ref, _ = refs
    else:
        prev_ref, q_ref, sums_ref = refs
    i = lax.broadcasted_iota(jnp.int32, (64, W), 0)
    j = lax.broadcasted_iota(jnp.int32, (64, W), 1)
    d = j - i
    band = jnp.where((d >= 0) & (d < 64), 1.0, 0.0)
    mask_top = jnp.where(d == 0, 0.5, band).astype(BF16)
    mask_bot = jnp.where(d == 64, 0.5, 1.0 - band).astype(BF16)

    def fold(v):
        return jnp.sum(v.reshape(CAP // 8, 8, W), axis=0)

    scale = 1.0 if first else prev_ref[3, 0:1, :]

    def body(g, carry):
        rr, pq, vv, ra, qa = carry
        rows = pl.ds(pl.multiple_of(g * CAP, CAP), CAP)
        r = slots_ref[rows, :]
        half = r.astype(BF16)
        b = blk_ref[g, 0:64, :]
        u = jnp.concatenate([b * mask_top, b * mask_bot], axis=0)
        cross = blk_ref[g, 64:72, :].astype(F32)
        swapped = pltpu.roll(half.astype(F32), 64, axis=1)
        q = jnp.dot(half, u + u.T, preferred_element_type=F32)
        q = q + (swapped.reshape(CAP // 8, 8, W) * cross[None]).reshape(CAP, W)
        q = q.astype(BF16).astype(F32)
        q_ref[rows, :] = q
        rr = rr + fold(r * r)
        pq = pq + fold(r * q)
        if first:
            ra = ra + fold(jnp.abs(r))
            qa = qa + fold(jnp.abs(q))
        else:
            v = q * scale
            vv = vv + fold(v * v)
        return rr, pq, vv, ra, qa

    zero = jnp.zeros((8, W), F32)
    rr, pq, vv, ra, qa = lax.fori_loop(0, NG, body, (zero,) * 5, unroll=8)
    if first:
        ra, qa = jnp.sum(ra), jnp.sum(qa)
        ok = (qa > 0.0) & (ra > 0.0)
        a0 = jnp.full((1, W), jnp.where(ok, ra, 1.0)) / jnp.full((1, W), jnp.where(ok, qa, 1.0))

        def second_pass(k, acc):
            v = q_ref[pl.ds(pl.multiple_of(k * 64, 64), 64), :] * a0
            return acc + jnp.sum((v * v).reshape(8, 8, W), axis=0)

        vv = lax.fori_loop(0, NG * CAP // 64, second_pass, zero, unroll=8)
        sums_ref[0], sums_ref[1], sums_ref[2] = rr, pq, vv
        sums_ref[3] = jnp.broadcast_to(a0, (8, W))
    else:
        rows = [jnp.sum(v + prev_ref[k], axis=0, keepdims=True) for k, v in enumerate((rr, pq, vv))]
        full = jnp.concatenate(rows + [scale], axis=0)
        for k in range(2 * NG):
            sums_ref[k] = full


def product_first(slots, blocks):
    def kernel(s, b, q, sums):
        here = q.at[0:NG * CAP]
        product_kernel(True, here, b, here, sums, None)

    return pl.pallas_call(kernel, out_shape=[keep((2 * NG * CAP, W)), keep((4, 8, W))], in_specs=[VM, VM], out_specs=[VM, VM], input_output_aliases={0: 0},
                          compiler_params=PARAMS, name="product_a")(slots, in_vmem(blocks))


def product_second(slots, blocks, prev):
    def kernel(s, b, p, q, sums):
        here = q.at[NG * CAP:2 * NG * CAP]
        product_kernel(False, here, b, p, here, sums)

    return pl.pallas_call(kernel, out_shape=[keep((2 * NG * CAP, W)), keep((2 * NG, 4, W))], input_output_aliases={0: 0},
                          in_specs=[VM, VM, VM], out_specs=[VM, VM], compiler_params=PARAMS, name="product_b")(slots, in_vmem(blocks), prev)


CH = 4
TC = T // CH


def final_kernel(red_ref, r_hbm, q_ref, cnt, strips_ref, rows_ref, field_ref, out_ref, res_hbm, dir_hbm, r_buf, res_buf, dir_buf, strips, rows, ins, outs):
    inner = slice(W, C - W)
    parts = [slice(k * TC, (k + 1) * TC) for k in range(CH)]
    tiles_in = [pltpu.make_async_copy(r_hbm.at[p], r_buf.at[p], ins.at[k]) for k, p in enumerate(parts)]
    rim_in = [pltpu.make_async_copy(strips_ref, strips, ins.at[CH]), pltpu.make_async_copy(rows_ref, rows, ins.at[CH + 1])]
    for c in tiles_in + rim_in:
        c.start()
    rr = jnp.sum(red_ref[:, 0, :])
    pq = jnp.sum(red_ref[:, 1, :])
    alpha = jnp.full((1, W), rr) / jnp.full((1, W), pq)
    t = alpha / red_ref[:, 3, :]
    qq = jnp.sum(t * t * red_ref[:, 2, :])
    beta = (rr - 2.0 * alpha * pq + qq) / rr
    sent = []

    def send(src, dst):
        c = pltpu.make_async_copy(src, dst, outs.at[len(sent)])
        c.start()
        sent.append(c)

    def rim_out():
        for c in rim_in:
            c.wait()
        strips[0] = strips[0] + (alpha * cnt[0:2 * R]) * strips[1]
        send(strips.at[0, 0:R], out_ref.at[:, 0:W])
        send(strips.at[0, R:2 * R], out_ref.at[:, C - W:C])
        for k in range(C // W):
            lanes = slice(k * W, (k + 1) * W)
            a, b = slice(2 * R + k, 2 * R + k + 1), slice(2 * R + 16 + k, 2 * R + 17 + k)
            rows[0, 0:1, lanes] = rows[0, 0:1, lanes] + (alpha * cnt[a]) * rows[2, 0:1, lanes]
            rows[1, 7:8, lanes] = rows[1, 7:8, lanes] + (alpha * cnt[b]) * rows[2, 1:2, lanes]
        send(rows.at[0, :, inner], out_ref.at[0:8, inner])
        send(rows.at[1, :, inner], out_ref.at[R - 8:R, inner])

    for k, p in enumerate(parts):
        tiles_in[k].wait()
        r = r_buf[p]
        res = r - alpha * q_ref[p]
        res_buf[p] = res
        dir_buf[p] = res + beta * r
        send(res_buf.at[p], res_hbm.at[p])
        send(dir_buf.at[p], dir_hbm.at[p])
        if k == 1:
            rim_out()
    for c in sent:
        c.wait()


def final(red, r_tiles, q_tiles, cnt, strips, rows, field):
    return pl.pallas_call(
        final_kernel, out_shape=[sds((R, C)), sds((T, W)), sds((T, W))],
        in_specs=[VM, ANY, VM, VM, ANY, ANY, ANY], out_specs=[ANY, ANY, ANY],
        scratch_shapes=[pltpu.VMEM((T, W), F32)] * 3 + [pltpu.VMEM((2, 2 * R, W), F32), pltpu.VMEM((3, 8, C), F32),
                        pltpu.SemaphoreType.DMA((CH + 2,)), pltpu.SemaphoreType.DMA((2 * CH + 4,))],
        input_output_aliases={6: 0}, compiler_params=PARAMS, name="final")(in_vmem(red), in_hbm(r_tiles), q_tiles, in_vmem(cnt), in_hbm(strips), in_hbm(rows), field)


def step(rhs, sigma, tile_list, tile_owner, schur_blocks):
    core = lax.axis_index("c")
    big = (in_hbm(rhs), in_hbm(sigma))
    packed, tail, head = start(schur_blocks, *big)
    mine = lax.all_to_all(packed, CHIPS, 0, 0, tiled=True)
    nrow, ncol = 16, 8
    up = [(i, i + 1) for i in range(nrow - 1)]
    down = [(i + 1, i) for i in range(nrow - 1)]
    hup = lax.ppermute(tail, ROWS, up)
    hdn = lax.ppermute(head, ROWS, down)

    rightward = [(i, i + 1) for i in range(ncol - 1)]
    leftward = [(i + 1, i) for i in range(ncol - 1)]
    to_right, to_left, tile_list, tile_owner = lax.optimization_barrier((*edge_cols(*big, hup, hdn), tile_list, tile_owner))
    hcr = lax.ppermute(to_left, COLS, leftward)
    hcl = lax.ppermute(to_right, COLS, rightward)
    row_at = lax.axis_index(ROWS)
    col_at = lax.axis_index(COLS)
    has = jnp.stack([row_at > 0, row_at < nrow - 1, col_at > 0, col_at < ncol - 1]).astype(jnp.int32)
    runs = C // W
    trow, tcol = tile_list // runs, tile_list % runs
    run = jnp.where(tcol == 0, trow, jnp.where(tcol == runs - 1, R + trow, jnp.where(trow == 0, 2 * R + tcol, 2 * R + 16 + tcol)))
    owner = tile_owner[:, 0]
    onehot = (owner[:, None] == jnp.arange(2 * NG, dtype=jnp.int32)[None, :]).astype(jnp.int32)
    ranks = jnp.cumsum(onehot, axis=0) - onehot
    rank = jnp.sum(ranks * onehot, axis=1)
    slot = (((owner & 1) ^ core) * NG + (owner >> 1)) * CAP + rank
    slot, *here = lax.optimization_barrier((slot, rhs, sigma))
    parts = near(*(in_hbm(v) for v in here))
    strips, rows, r_tiles, slots = rim(has, run, slot, parts, hup, hdn, hcl, hcr)
    mine, slots = lax.optimization_barrier((mine, slots))
    theirs = lax.ppermute(mine, "c", [(0, 1), (1, 0)])
    q, part = product_first(slots, mine)
    q, sums = product_second(q, theirs, part)
    q, sums, run, late_rhs, late_sigma = lax.optimization_barrier((q, sums, run, rhs, sigma))
    red = lax.all_to_all(sums, ALL, 0, 0, tiled=True)
    hits = (jnp.arange(RIM, dtype=jnp.int32)[:, None] == run[None, :]).astype(BF16)
    cnt = jnp.dot(hits, jnp.ones((T, W), BF16), preferred_element_type=F32)
    field, q_tiles = dense(slot, q, in_hbm(late_rhs), in_hbm(late_sigma))
    return tuple(final(red, r_tiles, q_tiles, cnt, strips, rows, field))


def solution(mesh):
    grid = Mesh(mesh.devices.reshape(4, 4, 4, 2), ("y", "z", "x", "c"))
    in_specs = (P(ROWS, COLS), P(ROWS, COLS), P(ALL), P(ALL, None), P(ALL, None, None))
    out_specs = (P(ROWS, COLS), P(ALL, None), P(ALL, None))
    return jax.shard_map(step, mesh=grid, in_specs=in_specs, out_specs=out_specs, check_vma=False)
```
